32 devices in a mesh: lat: 8 (over y, x, core), lon: 4 (over z).
Axes of the slice: x: 2, y: 2, z: 4, core: 2. Of those that a mesh axis runs over, the one named last changes fastest.
Arguments:
- fine_grid: bfloat16 [32, 1440, 256], P('lat', 'lon'), may hold values from -6 to 6
- coarse_grid: bfloat16 [16, 720, 256], P('lat', 'lon'), may hold values from -6 to 6
- fine_cotangent: bfloat16 [32, 1440, 256], P('lat', 'lon'), may hold values from -6 to 6
- coarse_cotangent: bfloat16 [16, 720, 256], P('lat', 'lon'), may hold values from -6 to 6
- spectral_weight: float32 [48, 2, 256, 256], P('lat', None, 'lon'), may hold values from -0.25 to 0.25
- spectral_momentum: float32 [48, 2, 256, 256], P('lat', None, 'lon'), may hold values from -63.63961 to 63.63961
- hidden_weight: float32 [2, 256, 512], replicated, may hold values from -0.375 to 0.375
- hidden_momentum: float32 [2, 256, 512], replicated, may hold values from -768 to 768
- norm_gains: float32 [2, 256], replicated, may hold values from 0.5 to 1.5
- gain_momentum: float32 [2, 256], replicated, may hold values from -768 to 768
Outputs:
- fine_output: bfloat16 [32, 1440, 256], P('lat', 'lon')
- coarse_output: bfloat16 [16, 720, 256], P('lat', 'lon')
- fine_gradient: bfloat16 [32, 1440, 256], P('lat', 'lon')
- coarse_gradient: bfloat16 [16, 720, 256], P('lat', 'lon')
- spectral_gradient: float32 [48, 2, 256, 256], P('lat', None, 'lon')
- spectral_moment: float32 [48, 2, 256, 256], P('lat', None, 'lon')
- spectral_updated: float32 [48, 2, 256, 256], P('lat', None, 'lon')
- spectral_copy: bfloat16 [48, 2, 256, 256], P('lat', None, 'lon')
- hidden_gradient: float32 [2, 256, 512], replicated
- hidden_moment: float32 [2, 256, 512], replicated
- hidden_updated: float32 [2, 256, 512], replicated
- hidden_copy: bfloat16 [2, 256, 512], replicated
- gain_gradient: float32 [2, 256], replicated
- gain_moment: float32 [2, 256], replicated
- gain_updated: float32 [2, 256], replicated
The draws below stay inside these ranges and needn't reach their ends.
All inputs are finite; a program needn't handle non-finite values.
Results may differ from the reference program's by a relative error of at most 0.015.
Values may be sent and summed in bfloat16 or wider, within the bound.
No kernel may reach another device: no remote copies, remote signals or barrier semaphores. Data moves between devices by JAX's collectives and lax.ppermute only.
A program may use at most 192 MiB of HBM per device.

```python
import math
import jax
import jax.numpy as jnp
from jax import lax

C = 256
FF = 512
DEG_DEV = 6
DEGREES = 48
DEG2 = 24
NLAT1 = 32
NLON1 = 1440
NLAT2 = 16
NLON2 = 720
CELLS = 57600
N_LAT = 8


def draw_spectral_momentum(key, part):
    degree = jnp.arange(DEGREES).astype(jnp.float32)
    orders_seen = jnp.minimum(degree + 1.0, 1.0 * DEGREES) + jnp.minimum(degree + 1.0, 1.0 * DEG2)
    spread = (2.5 * jnp.sqrt(orders_seen))[:, None, None, None]
    noise = jax.random.normal(key, (DEGREES, 2, C, C), jnp.float32)
    return jnp.clip(noise, -3.0, 3.0) * spread


def block_levels(rng, shape, pieces, least, top_value):
    def one(position, blocks):
        draws = jax.random.uniform(jax.random.fold_in(jax.random.fold_in(rng, 6), position), (blocks,), jnp.float32, least / len(pieces), top_value / len(pieces))
        return jnp.repeat(jnp.exp(draws), shape[position] // blocks).reshape((-1,) + (1,) * (len(shape) - position - 1))

    gain = one(*pieces[0])
    for cut in pieces[1:]:
        gain = gain * one(*cut)
    return gain


def scatter_about(key, extent, scale, reach, cuts=(), held_as=jnp.bfloat16):
    drawn = jax.random.normal(key, extent, jnp.float32) * scale
    if len(cuts) > 0:
        drawn = block_levels(key, extent, cuts, -0.22, 0.18) * drawn
    return jnp.clip(drawn, min=-reach, max=reach).astype(held_as)


def setup_inputs(seed: int = 0) -> dict:
    seeds = jax.random.split(jax.random.key(seed), 11)
    return {
        "fine_grid": scatter_about(seeds[0], (NLAT1, NLON1, C), 1.0, 6.0, ((0, 8), (1, 4))),
        "coarse_grid": scatter_about(seeds[1], (NLAT2, NLON2, C), 1.0, 6.0, ((0, 8), (1, 4))),
        "fine_cotangent": scatter_about(seeds[2], (NLAT1, NLON1, C), 1.0, 6.0, ((0, 8), (1, 4))),
        "coarse_cotangent": scatter_about(seeds[3], (NLAT2, NLON2, C), 1.0, 6.0, ((0, 8), (1, 4))),
        "spectral_weight": scatter_about(seeds[4], (DEGREES, 2, C, C), (2 * C) ** -0.5, 0.25, ((0, 8), (2, 4)), jnp.float32),
        "spectral_momentum": draw_spectral_momentum(jax.random.fold_in(seeds[10], 71), 0),
        "hidden_weight": scatter_about(seeds[6], (2, C, FF), C ** -0.5, 0.375, (), jnp.float32),
        "hidden_momentum": scatter_about(seeds[7], (2, C, FF), (0.5 * CELLS ** 0.5), 768.0, (), jnp.float32),
        "norm_gains": jnp.clip(1.0 + 0.1 * jax.random.normal(seeds[8], (2, C), jnp.float32), 0.5, 1.5),
        "gain_momentum": scatter_about(seeds[9], (2, C), (0.5 * CELLS ** 0.5), 768.0, (), jnp.float32),
    }


NORM_EPSILON = 1e-05
MOMENTUM_DECAY = 0.5
STEP_RATE = 0.6
GAIN_RATE = 0.2
POLY_FIRST = 3.4445
POLY_SECOND = -4.775
POLY_THIRD = 2.0315
PRECISE = lax.Precision.HIGHEST

@jax.custom_vjp
def low(v):
    return lax.optimization_barrier(v.astype(jnp.bfloat16)).astype(jnp.float32)

@jax.custom_vjp
def low_back(v):
    return v

def low_keep(v):
    return (low(v), None)

def low_pass(kept, grad):
    return (grad,)

def back_keep(v):
    return (v, None)

def back_low(kept, grad):
    return (low(grad),)
low.defvjp(low_keep, low_pass)
low_back.defvjp(back_keep, back_low)

def legendre(orders, colatitude, degree_count, used_count):
    cosine = jnp.cos(colatitude)[:, None]
    order_row = orders[None, :]
    log_start = 0.5 * (jnp.log((2.0 * order_row + 1.0) / (4.0 * math.pi)) + lax.lgamma(order_row + 0.5) - lax.lgamma(order_row + 1.0) - 0.5 * math.log(math.pi)) + order_row * jnp.log(jnp.sin(colatitude))[:, None]
    diagonal = jnp.exp(log_start)

    def advance(carried, degree):
        latest, earlier = carried
        square = degree * degree
        factor_now = jnp.sqrt(jnp.maximum(4.0 * square - 1.0, 1.0) / jnp.maximum(square - order_row * order_row, 1.0))
        prior_square = (degree - 1.0) * (degree - 1.0)
        factor_prior = jnp.sqrt(jnp.maximum(4.0 * prior_square - 1.0, 1.0) / jnp.maximum(prior_square - order_row * order_row, 1.0))
        general = factor_now * (cosine * latest - earlier / factor_prior)
        result = jnp.where(degree == order_row + 1.0, cosine * jnp.sqrt(2.0 * order_row + 3.0) * latest, general)
        result = jnp.where(degree == order_row, diagonal, result)
        result = jnp.where((degree < order_row) | (degree >= used_count), 0.0, result)
        return ((result, latest), result)
    zeros_start = jnp.zeros_like(diagonal)
    degrees = jnp.arange(degree_count).astype(diagonal.dtype)
    final_state, stacked = lax.scan(advance, (zeros_start, zeros_start), degrees, unroll=8)
    return stacked

def fourier_table(count_lon, orders):
    longitude = jnp.arange(count_lon, dtype=jnp.int32)
    phase_index = longitude[:, None] * orders[None, :] % count_lon
    angles = 2.0 * math.pi / count_lon * phase_index.astype(jnp.float32)
    return jnp.stack([jnp.cos(angles), -jnp.sin(angles)], axis=1)

def layer_norm(values, scaling):
    center = lax.optimization_barrier(jnp.mean(values, axis=-1, keepdims=True))
    shifted = values - center
    spread = lax.optimization_barrier(jnp.mean(shifted * shifted, axis=-1, keepdims=True))
    return shifted * lax.rsqrt(spread + NORM_EPSILON) * scaling

def complex_blocks(weights):
    real_part = weights[:, 0]
    imag_part = weights[:, 1]
    upper_row = jnp.stack([real_part, imag_part], axis=1)
    lower_row = jnp.stack([-imag_part, real_part], axis=1)
    return jnp.stack([upper_row, lower_row], axis=1)

def spectral(signal_in, weights_low, count_lon, orders_count):
    count_lat = signal_in.shape[0]
    slot_count = orders_count // N_LAT
    colatitude = math.pi * (jnp.arange(count_lat).astype(jnp.float32) + 0.5) / count_lat
    quadrature = math.pi / count_lat * jnp.sin(colatitude)
    fourier = low(fourier_table(count_lon, jnp.arange(orders_count, dtype=jnp.int32)))
    forward_scale = math.sqrt(count_lat * count_lon / (4.0 * math.pi))
    inverse_scale = 1.0 / forward_scale
    spectrum = low_back(low(2.0 * math.pi / count_lon * jnp.einsum('tnc,nrm->tmrc', signal_in, fourier, precision=PRECISE)))
    order_blocks = jnp.arange(orders_count).astype(jnp.float32).reshape(N_LAT, slot_count)
    spec_blocks = jnp.moveaxis(spectrum.reshape(count_lat, N_LAT, slot_count, 2, C), 1, 0)

    def down_block(paired):
        piece_in, order_row = paired
        legendre_rows = low(quadrature[None, :, None] * legendre(order_row, colatitude, DEGREES, orders_count))
        return forward_scale * jnp.einsum('lts,tsrc->lsrc', legendre_rows, piece_in, precision=PRECISE)
    coef_blocks = lax.map(jax.checkpoint(down_block), (spec_blocks, order_blocks))
    coeffs = low_back(low(jnp.moveaxis(coef_blocks, 0, 1).reshape(DEGREES, orders_count, 2, C)))
    degree_blocks = coeffs.reshape(N_LAT, DEG_DEV, orders_count, 2, C)
    weight_blocks = weights_low.reshape(N_LAT, DEG_DEV, 2, C, C)

    def mix_block(paired):
        piece_in, weight_piece = paired
        return jnp.einsum('lmrc,lrqdc->lmqd', piece_in, complex_blocks(weight_piece), precision=PRECISE)
    mixed_coef = lax.map(jax.checkpoint(mix_block), (degree_blocks, weight_blocks)).reshape(DEGREES, orders_count, 2, C)
    mixed_coef = low_back(low(mixed_coef))
    mixed_blocks = jnp.moveaxis(mixed_coef.reshape(DEGREES, N_LAT, slot_count, 2, C), 1, 0)

    def up_block(paired):
        piece_in, order_row = paired
        legendre_rows = low(legendre(order_row, colatitude, DEGREES, orders_count))
        factor = inverse_scale * jnp.where(order_row == 0.0, 1.0, 2.0)
        return jnp.einsum('lts,lsrc->tsrc', legendre_rows, piece_in, precision=PRECISE) * factor[None, :, None, None]
    grid_blocks = lax.map(jax.checkpoint(up_block), (mixed_blocks, order_blocks))
    grid_vals = low_back(low(jnp.moveaxis(grid_blocks, 0, 1).reshape(count_lat, orders_count, 2, C)))
    return low_back(low(jnp.einsum('tmrc,nrm->tnc', grid_vals, fourier, precision=PRECISE)))

def feed_forward(rows_in, first_low, second_low, scaling):
    normed = low(layer_norm(rows_in, scaling))
    hidden_pre = low_back(jnp.einsum('nc,cf->nf', normed, first_low, precision=PRECISE))
    activated = low(jax.nn.gelu(hidden_pre))
    return rows_in + jnp.einsum('nf,cf->nc', activated, second_low, precision=PRECISE)

def forward(fine_in, coarse_in, spectral_weight, hidden_weight, norm_gains):
    weights_low = low(spectral_weight)
    first_low = low(hidden_weight[0])
    second_low = low(hidden_weight[1])
    results = []
    for signal_in, count_lon, orders_count in ((fine_in, NLON1, DEGREES), (coarse_in, NLON2, DEG2)):
        normed = low_back(low(layer_norm(signal_in, norm_gains[0])))
        branch = spectral(normed, weights_low, count_lon, orders_count)
        residual = signal_in + branch

        def row_block(rows_in):
            return feed_forward(rows_in, first_low, second_low, norm_gains[1])
        results.append(lax.map(jax.checkpoint(row_block), residual))
    return (results[0], results[1])

def complex_product(left_real, left_imag, right_real, right_imag):
    return (jnp.dot(left_real, right_real, precision=PRECISE) - jnp.dot(left_imag, right_imag, precision=PRECISE), jnp.dot(left_real, right_imag, precision=PRECISE) + jnp.dot(left_imag, right_real, precision=PRECISE))

def orthogonal_complex(moment):
    norm_value = jnp.sqrt(jnp.sum(moment * moment)) + 1e-07
    real_part = moment[0] / norm_value
    imag_part = moment[1] / norm_value
    for iteration in range(5):
        gram_real, gram_imag = complex_product(real_part.T, -imag_part.T, real_part, imag_part)
        square_real, square_imag = complex_product(gram_real, gram_imag, gram_real, gram_imag)
        poly_real = POLY_SECOND * gram_real + POLY_THIRD * square_real
        poly_imag = POLY_SECOND * gram_imag + POLY_THIRD * square_imag
        prod_real, prod_imag = complex_product(real_part, imag_part, poly_real, poly_imag)
        real_part = POLY_FIRST * real_part + prod_real
        imag_part = POLY_FIRST * imag_part + prod_imag
    return jnp.stack([real_part, imag_part])

def orthogonal_real(matrix):
    norm_value = jnp.sqrt(jnp.sum(matrix * matrix)) + 1e-07
    current = matrix / norm_value
    for iteration in range(5):
        gram_rows = jnp.dot(current, current.T, precision=PRECISE)
        square = jnp.dot(gram_rows, gram_rows, precision=PRECISE)
        polynomial = POLY_SECOND * gram_rows + POLY_THIRD * square
        current = POLY_FIRST * current + jnp.dot(polynomial, current, precision=PRECISE)
    return current

def reference(fine_grid, coarse_grid, fine_cotangent, coarse_cotangent, spectral_weight, spectral_momentum, hidden_weight, hidden_momentum, norm_gains, gain_momentum):
    outputs, pullback = jax.vjp(forward, fine_grid.astype(jnp.float32), coarse_grid.astype(jnp.float32), spectral_weight, hidden_weight, norm_gains)
    fine_back, coarse_back, spectral_grad, hidden_grad, gain_grad = pullback((fine_cotangent.astype(jnp.float32), coarse_cotangent.astype(jnp.float32)))
    spectral_moment = MOMENTUM_DECAY * spectral_momentum + spectral_grad
    spectral_updated = spectral_weight - STEP_RATE * lax.map(orthogonal_complex, spectral_moment)
    hidden_moment = MOMENTUM_DECAY * hidden_momentum + hidden_grad
    hidden_updated = hidden_weight - STEP_RATE * jnp.stack([orthogonal_real(hidden_moment[0]), orthogonal_real(hidden_moment[1])])
    gain_moment = MOMENTUM_DECAY * gain_momentum + gain_grad
    gain_scale = jnp.sqrt(lax.optimization_barrier(jnp.mean(gain_moment * gain_moment, axis=-1, keepdims=True)))
    gain_updated = norm_gains - GAIN_RATE * gain_moment / (gain_scale + 1e-06)
    return (outputs[0].astype(jnp.bfloat16), outputs[1].astype(jnp.bfloat16), fine_back.astype(jnp.bfloat16), coarse_back.astype(jnp.bfloat16), spectral_grad, spectral_moment, spectral_updated, spectral_updated.astype(jnp.bfloat16), hidden_grad, hidden_moment, hidden_updated, hidden_updated.astype(jnp.bfloat16), gain_grad, gain_moment, gain_updated)
```

```python
import functools
import math

import jax
import jax.numpy as jnp
import ml_dtypes
import numpy as np
from jax import lax
from jax.experimental import pallas as pl
from jax.experimental.pallas import tpu as pltpu
from jax.sharding import PartitionSpec as P

OWNED = 2
RIDER = 3
NORM_EPSILON = 1e-05
MOMENTUM_DECAY = 0.5
STEP_RATE = 0.6
GAIN_RATE = 0.2
POLY_FIRST = 3.4445
POLY_SECOND = -4.775
POLY_THIRD = 2.0315
PRECISE = lax.Precision.HIGHEST
BOTH = ("lat", "lon")
LOW = jnp.bfloat16
WIDE = jnp.float32


class Plan:
    def __init__(self, lat_count, lon_count, fine, coarse, weight):
        self.lat, self.lon = lat_count, lon_count
        self.devices = lat_count * lon_count
        self.tf, self.nf, self.channels = fine.shape
        self.tc, self.nc = coarse.shape[:2]
        self.deg_dev = weight.shape[0]
        self.degrees = self.deg_dev * lat_count
        self.half = self.degrees // 2
        self.fine_lat, self.coarse_lat = self.tf * lat_count, self.tc * lat_count
        self.fine_lon, self.coarse_lon = self.nf * lon_count, self.nc * lon_count
        self.rows = 3 * self.tf + 2 * self.tc
        self.fine_ka = math.sqrt(self.fine_lat * self.fine_lon / (4.0 * math.pi))
        self.coarse_ka = math.sqrt(self.coarse_lat * self.coarse_lon / (4.0 * math.pi))
        self.parts_lat = lat_count // 2

    def orders(self, lat_index, lon_index):
        part = lat_index // self.parts_lat
        trio = (lat_index % self.parts_lat) * self.lon + lon_index
        even = 1 - trio % 2
        pair = trio // 2
        low, high = 3 * pair, self.half + 3 * pair
        first = high + 2 * (1 - even)
        second = even * (high + 1) + (1 - even) * (low + 1)
        third = even * low + (1 - even) * (low + 2)
        return (first, second, third), part, even

    def fourier(self):
        fine = np.zeros((self.lon, self.devices, 3, self.nf))
        coarse = np.zeros((self.lon, self.devices, 2, self.nc))

        def fill(out, order, part, total):
            position = np.arange(total)
            angle = 2.0 * np.pi / total * (position * order % total)
            line = -np.sin(angle) if part else np.cos(angle)
            out[...] = line.reshape(self.lon, -1)

        for lat_index in range(self.lat):
            for lon_index in range(self.lon):
                device = lat_index * self.lon + lon_index
                orders, part, even = self.orders(lat_index, lon_index)
                for row in range(3):
                    fill(fine[:, device, row], orders[row], part, self.fine_lon)
                for row in range(1 + even):
                    fill(coarse[:, device, row], orders[row] - self.half, part, self.coarse_lon)
        return fine.astype(ml_dtypes.bfloat16), coarse.astype(ml_dtypes.bfloat16)


def legendre_kernel(columns, weighted_out, doubled_out, slope, back, start, *, degrees, half):
    order, cosine, quadrature, doubling = (columns[row : row + 1, :] for row in range(4))
    used, diagonal = columns[4:5, :], columns[5:6, :]
    degree = lax.broadcasted_iota(jnp.int32, slope.shape, 0).astype(WIDE)

    def factor(at):
        square = at * at
        return jnp.sqrt(
            jnp.maximum(4.0 * square - 1.0, 1.0) / jnp.maximum(square - order * order, 1.0)
        )

    now = factor(degree)
    running = (degree > order) & (degree < used)
    slope[...] = jnp.where(running, now * cosine, 0.0)
    back[...] = jnp.where(running, now / factor(degree - 1.0), 0.0)
    start[...] = jnp.where((degree == order) & (degree < used), diagonal, 0.0)

    def step(block, carried):
        latest, earlier = carried
        base = pl.multiple_of(block * 8, 8)
        slopes, backs, starts = (ref[pl.ds(base, 8), :] for ref in (slope, back, start))
        found = []
        for row in range(8):
            at = slice(row, row + 1)
            latest, earlier = slopes[at] * latest - backs[at] * earlier + starts[at], latest
            found.append(latest)
        start[pl.ds(base, 8), :] = jnp.concatenate(found, axis=0)
        return latest, earlier

    zero = jnp.zeros_like(order)
    lax.fori_loop(0, degrees // 8, step, (zero, zero))
    plain = start[...]
    weighted_out[...] = (quadrature * plain).astype(LOW)
    doubled_out[...] = (doubling * plain.astype(LOW).astype(WIDE)).astype(LOW)


def legendre_tables(plan, lat_index, lon_index):
    orders, part, even = plan.orders(lat_index, lon_index)
    fine_kind = np.repeat(np.arange(3), plan.tf)
    coarse_kind = np.repeat(np.arange(2), plan.tc)
    kind = np.tile(np.concatenate([fine_kind, coarse_kind]), plan.devices)
    is_fine = np.tile(np.arange(plan.rows) < 3 * plan.tf, plan.devices)
    lat_of = np.repeat(np.arange(plan.devices) // plan.lon, plan.rows)
    fine_lat = lat_of * plan.tf + np.tile(np.arange(plan.rows) % plan.tf, plan.devices)
    coarse_lat = lat_of * plan.tc + np.tile(np.arange(plan.rows) % plan.tc, plan.devices)
    position = np.where(is_fine, fine_lat, coarse_lat)
    count = np.where(is_fine, plan.fine_lat, plan.coarse_lat)
    colatitude = np.pi * (position + 0.5) / count
    own = jnp.where(kind == 0, orders[0], jnp.where(kind == 1, orders[1], orders[2]))
    own = jnp.where(is_fine, own, own - plan.half)
    held = own >= 0
    own = jnp.maximum(own, 0)
    span = np.arange(plan.degrees)
    norms = np.array(
        [
            0.5
            * (
                math.log((2.0 * m + 1.0) / (4.0 * math.pi))
                + math.lgamma(m + 0.5)
                - math.lgamma(m + 1.0)
                - 0.5 * math.log(math.pi)
            )
            for m in span
        ],
        np.float32,
    )
    norm = jnp.sum(jnp.where(own[None, :] == span[:, None], norms[:, None], 0.0), axis=0)
    log_sine = np.log(np.sin(colatitude)).astype(np.float32)
    diagonal = jnp.where(held, jnp.exp(norm + own.astype(WIDE) * log_sine), 0.0)
    columns = jnp.stack(
        [
            own.astype(WIDE),
            jnp.asarray(np.cos(colatitude).astype(np.float32)),
            jnp.asarray((np.pi / count * np.sin(colatitude)).astype(np.float32)),
            jnp.where(own == 0, 1.0, 2.0),
            jnp.asarray(np.where(is_fine, plan.degrees, plan.half).astype(np.float32)),
            diagonal,
        ]
    )
    shape = (plan.degrees, plan.devices * plan.rows)
    compact = pl.pallas_call(
        functools.partial(legendre_kernel, degrees=plan.degrees, half=plan.half),
        out_shape=(jax.ShapeDtypeStruct(shape, LOW),) * 2,
        scratch_shapes=[pltpu.VMEM(shape, WIDE)] * 3,
        compiler_params=pltpu.CompilerParams(vmem_limit_bytes=56 << 20),
        name="legendre",
    )(columns)
    chosen = kind[None, :] == np.arange(4)[:, None]
    pairs = plan.deg_dev // OWNED
    results = []
    for table in compact:
        spread = table.reshape(plan.lat, pairs, OWNED, 1, shape[1])
        spread = jnp.where(chosen, spread, jnp.zeros_like(spread))
        spread = jnp.pad(spread, ((0, 0), (0, plan.lon - pairs), (0, 0), (0, 0), (0, 0)))
        results.append(spread.reshape(plan.devices * 8, shape[1]))
    return results


def layer_norm(values, scaling):
    center = jnp.mean(values, axis=-1, keepdims=True)
    shifted = values - center
    spread = jnp.mean(shifted * shifted, axis=-1, keepdims=True)
    return shifted * lax.rsqrt(spread + NORM_EPSILON) * scaling


def exchange(rows, axes, count):
    block = rows.reshape((count, -1) + rows.shape[1:])
    return lax.all_to_all(block, axes, 0, 0, tiled=True).reshape(rows.shape)


def wide_dot(left, right, contract=((1,), (0,))):
    return lax.dot_general(left, right, (contract, ((), ())), preferred_element_type=WIDE)


def analysis(plan, fine, coarse, tables, scales, legendre_table):
    fine_part = scales[0] * jnp.einsum("dkn,tnc->dktc", tables[0], fine, preferred_element_type=WIDE)
    coarse_part = scales[1] * jnp.einsum("dkn,tnc->dktc", tables[1], coarse, preferred_element_type=WIDE)
    sent = jnp.concatenate(
        [
            fine_part.reshape(plan.devices, -1, plan.channels),
            coarse_part.reshape(plan.devices, -1, plan.channels),
        ],
        axis=1,
    ).astype(LOW)
    spectrum = exchange(sent.reshape(-1, plan.channels), BOTH, plan.devices)
    coeffs = wide_dot(legendre_table, spectrum).astype(LOW)
    return coeffs


def synthesis(plan, mixed, tables, scales, legendre_table):
    values = wide_dot(legendre_table, mixed, ((0,), (0,))).astype(LOW)
    values = exchange(values, BOTH, plan.devices).reshape(plan.devices, plan.rows, plan.channels)
    fine = values[:, : 3 * plan.tf].reshape(plan.devices, 3, plan.tf, plan.channels)
    coarse = values[:, 3 * plan.tf :].reshape(plan.devices, 2, plan.tc, plan.channels)
    fine_out = scales[0] * jnp.einsum("dktc,dkn->tnc", fine, tables[0], preferred_element_type=WIDE)
    coarse_out = scales[1] * jnp.einsum("dktc,dkn->tnc", coarse, tables[1], preferred_element_type=WIDE)
    return fine_out.astype(LOW), coarse_out.astype(LOW)


def orthogonal_real(matrix):
    norm_value = jnp.sqrt(jnp.sum(matrix * matrix)) + 1e-07
    current = matrix / norm_value
    for iteration in range(5):
        gram_rows = jnp.dot(current, current.T, precision=PRECISE)
        square = jnp.dot(gram_rows, gram_rows, precision=PRECISE)
        polynomial = POLY_SECOND * gram_rows + POLY_THIRD * square
        current = POLY_FIRST * current + jnp.dot(polynomial, current, precision=PRECISE)
    return current


def batch(left, right, spec="lab,lbc->lac"):
    return jnp.einsum(spec, left, right, precision=PRECISE)


def orthogonal_complex(moment):
    norm_value = jnp.sqrt(jnp.sum(moment * moment, axis=(1, 2, 3))) + 1e-07
    current = moment / norm_value[:, None, None, None]
    real, imag = current[:, 0], current[:, 1]
    for iteration in range(5):
        gram_real = batch(real, real, "lda,ldb->lab") + batch(imag, imag, "lda,ldb->lab")
        cross = batch(real, imag, "lda,ldb->lab")
        gram_imag = cross - jnp.swapaxes(cross, 1, 2)
        square_real = batch(gram_real, gram_real) - batch(gram_imag, gram_imag)
        cross = batch(gram_real, gram_imag)
        square_imag = cross - jnp.swapaxes(cross, 1, 2)
        poly_real = POLY_SECOND * gram_real + POLY_THIRD * square_real
        poly_imag = POLY_SECOND * gram_imag + POLY_THIRD * square_imag
        real, imag = (
            POLY_FIRST * real + batch(real, poly_real) - batch(imag, poly_imag),
            POLY_FIRST * imag + batch(real, poly_imag) + batch(imag, poly_real),
        )
    return jnp.stack([real, imag], axis=1)


def to_owners(plan, rows):
    held, block = rows.shape[0], rows.shape[2]
    padded = jnp.pad(rows, ((0, plan.lon * OWNED - held), (0, 0), (0, 0), (0, 0)))
    padded = padded.reshape(plan.lon, OWNED, 2, block, plan.channels)
    got = lax.all_to_all(padded, "lon", 0, 0, tiled=True)
    return jnp.transpose(got, (1, 2, 0, 3, 4)).reshape(OWNED, 2, plan.lon * block, plan.channels)


def from_owners(plan, whole):
    block = plan.channels // plan.lon
    sent = jnp.transpose(
        whole.reshape(OWNED, 2, plan.lon, block, plan.channels), (2, 0, 1, 3, 4)
    )
    got = lax.all_to_all(sent, "lon", 0, 0, tiled=True)
    return got.reshape(plan.lon * OWNED, 2, block, plan.channels)[: plan.deg_dev]


def body(
    fine_grid,
    coarse_grid,
    fine_cotangent,
    coarse_cotangent,
    spectral_weight,
    spectral_momentum,
    hidden_weight,
    hidden_momentum,
    norm_gains,
    gain_momentum,
):
    plan = Plan(lax.axis_size("lat"), lax.axis_size("lon"), fine_grid, coarse_grid, spectral_weight)
    lat_index, lon_index = lax.axis_index("lat"), lax.axis_index("lon")
    channels = plan.channels
    tables = [
        lax.dynamic_index_in_dim(jnp.asarray(table), lon_index, 0, keepdims=False)
        for table in plan.fourier()
    ]
    weighted, doubled = legendre_tables(plan, lat_index, lon_index)
    weights = to_owners(plan, spectral_weight.astype(LOW))
    momentum = to_owners(plan, spectral_momentum)
    first_low = hidden_weight[0].astype(LOW)
    second_low = hidden_weight[1].astype(LOW)

    fine32, coarse32 = fine_grid.astype(WIDE), coarse_grid.astype(WIDE)
    normed_fine, pull_fine = jax.vjp(lambda v: layer_norm(v, norm_gains[0]), fine32)
    normed_coarse, pull_coarse = jax.vjp(lambda v: layer_norm(v, norm_gains[0]), coarse32)
    forward_scales = (
        2.0 * math.pi / plan.fine_lon * plan.fine_ka,
        2.0 * math.pi / plan.coarse_lon * plan.coarse_ka,
    )
    inverse_scales = (1.0 / plan.fine_ka, 1.0 / plan.coarse_ka)
    coeffs = analysis(
        plan, normed_fine.astype(LOW), normed_coarse.astype(LOW), tables, forward_scales, weighted
    )
    held = exchange(coeffs, BOTH, plan.devices)
    slot = jnp.arange(plan.devices * 8, dtype=jnp.int32) % 8
    masks = [((slot // 4 == owned) & (slot % 4 < 3))[:, None] for owned in range(OWNED)]
    split = plan.devices * 4

    def mixing(rows, matrices, sign, contract):
        total = 0.0
        for owned in range(OWNED):
            chosen = jnp.where(masks[owned], rows, jnp.zeros_like(rows))
            by_real = wide_dot(chosen, matrices[owned, 0], contract)
            by_imag = sign * wide_dot(chosen, matrices[owned, 1], contract)
            total = total + jnp.concatenate(
                [by_real[:split] - by_imag[split:], by_real[split:] + by_imag[:split]]
            )
        return total

    mixed = mixing(held, weights, 1.0, ((1,), (1,))).astype(LOW)
    mixed = exchange(mixed, BOTH, plan.devices)
    branch = synthesis(plan, mixed, tables, inverse_scales, doubled)

    outputs, residual_grads = [], []
    first_grad = second_grad = gain_second = 0.0
    for signal, part, cotangent in (
        (fine32, branch[0], fine_cotangent),
        (coarse32, branch[1], coarse_cotangent),
    ):
        residual = signal + part.astype(WIDE)
        rows_in = residual.reshape(-1, channels)
        second_normed, second_pull = jax.vjp(layer_norm, rows_in, norm_gains[1])
        normed_low = second_normed.astype(LOW)
        hidden_pre = wide_dot(normed_low, first_low)
        activated, gelu_pull = jax.vjp(jax.nn.gelu, hidden_pre)
        activated_low = activated.astype(LOW)
        output_rows = rows_in + wide_dot(activated_low, second_low, ((1,), (1,)))
        outputs.append(output_rows.reshape(signal.shape).astype(LOW))
        upstream = cotangent.reshape(-1, channels)
        act_grad = wide_dot(upstream, second_low)
        second_grad = second_grad + wide_dot(upstream, activated_low, ((0,), (0,)))
        pre_grad = gelu_pull(act_grad)[0].astype(LOW)
        first_grad = first_grad + wide_dot(normed_low, pre_grad, ((0,), (0,)))
        normed_grad = wide_dot(pre_grad, first_low, ((1,), (1,)))
        rows_grad, gain_piece = second_pull(normed_grad)
        gain_second = gain_second + gain_piece
        residual_grads.append((rows_grad + upstream.astype(WIDE)).reshape(residual.shape))

    partial_hidden = jnp.concatenate([first_grad, second_grad]).reshape(-1, channels).astype(LOW)
    share = partial_hidden.shape[0] // plan.devices
    received = exchange(partial_hidden, BOTH, plan.devices)
    summed = jnp.sum(received.reshape(plan.devices, share, channels).astype(WIDE), axis=0)
    hidden_grad = exchange(
        jnp.tile(summed.astype(LOW), (plan.devices, 1)), BOTH, plan.devices
    )
    hidden_grad = hidden_grad.reshape(hidden_weight.shape).astype(WIDE)

    mixed_grad = analysis(
        plan,
        residual_grads[0].astype(LOW),
        residual_grads[1].astype(LOW),
        tables,
        inverse_scales,
        doubled,
    )
    riding = jnp.arange(8)[None, :, None] == RIDER
    mixed_grad = jnp.where(
        riding, gain_second.astype(LOW)[None, None, :], mixed_grad.reshape(plan.devices, 8, channels)
    ).reshape(-1, channels)
    mixed_grad = exchange(mixed_grad, BOTH, plan.devices)
    gain_second = jnp.sum(mixed_grad.reshape(plan.devices, 8, channels)[:, RIDER].astype(WIDE), axis=0)
    coef_grad = mixing(mixed_grad, weights, -1.0, ((1,), (0,)))
    coef_low = coef_grad.astype(LOW)
    used = (slot % 4 < 3)[:, None]
    gain_first = jnp.sum(
        jnp.where(used, coef_low.astype(WIDE) * held.astype(WIDE), 0.0), axis=0
    ) / norm_gains[0]
    coef_low = jnp.where(
        riding, gain_first.astype(LOW)[None, None, :], coef_low.reshape(plan.devices, 8, channels)
    ).reshape(-1, channels)

    swapped = jnp.concatenate([mixed_grad[split:], -mixed_grad[:split]])
    own_grads = []
    for owned in range(OWNED):
        zero = jnp.zeros_like(held)
        picked = jnp.where(masks[owned], held, zero)
        own_grads.append(
            jnp.stack(
                [
                    wide_dot(mixed_grad, picked, ((0,), (0,))),
                    wide_dot(swapped, picked, ((0,), (0,))),
                ]
            )
        )
    own_grad = jnp.stack(own_grads)

    coef_low = exchange(coef_low, BOTH, plan.devices)
    gain_first = jnp.sum(coef_low.reshape(plan.devices, 8, channels)[:, RIDER].astype(WIDE), axis=0)
    back_scales = (forward_scales[0], forward_scales[1])
    normed_back = synthesis(plan, coef_low, tables, back_scales, weighted)
    gradients = []
    for pull, back, residual_grad in (
        (pull_fine, normed_back[0], residual_grads[0]),
        (pull_coarse, normed_back[1], residual_grads[1]),
    ):
        gradients.append((residual_grad + pull(back.astype(WIDE))[0]).astype(LOW))

    spectral_grad = from_owners(plan, own_grad.astype(LOW)).astype(WIDE)
    spectral_moment = MOMENTUM_DECAY * spectral_momentum + spectral_grad
    iterate = orthogonal_complex(MOMENTUM_DECAY * momentum + own_grad)
    step = from_owners(plan, iterate.astype(LOW)).astype(WIDE)
    spectral_updated = spectral_weight - STEP_RATE * step

    hidden_moment = MOMENTUM_DECAY * hidden_momentum + hidden_grad
    hidden_updated = hidden_weight - STEP_RATE * jnp.stack(
        [orthogonal_real(hidden_moment[0]), orthogonal_real(hidden_moment[1])]
    )
    gains_total = jnp.stack([gain_first, gain_second])
    gain_moment = MOMENTUM_DECAY * gain_momentum + gains_total
    gain_scale = jnp.sqrt(jnp.mean(gain_moment * gain_moment, axis=-1, keepdims=True))
    gain_updated = norm_gains - GAIN_RATE * gain_moment / (gain_scale + 1e-06)
    return (
        outputs[0],
        outputs[1],
        gradients[0],
        gradients[1],
        spectral_grad,
        spectral_moment,
        spectral_updated,
        spectral_updated.astype(LOW),
        hidden_grad,
        hidden_moment,
        hidden_updated,
        hidden_updated.astype(LOW),
        gains_total,
        gain_moment,
        gain_updated,
    )


def solution(mesh):
    grid = P("lat", "lon", None)
    degree = P("lat", None, "lon", None)
    return jax.shard_map(
        body,
        mesh=mesh,
        in_specs=(grid,) * 4 + (degree,) * 2 + (P(),) * 4,
        out_specs=(grid,) * 4 + (degree,) * 4 + (P(),) * 7,
        check_vma=False,
    )
```

```python
import functools
import math

import jax
import jax.numpy as jnp
import ml_dtypes
import numpy as np
from jax import lax
from jax.experimental import pallas as pl
from jax.experimental.pallas import tpu as pltpu
from jax.sharding import PartitionSpec as P

OWNED = 2
RIDER = 3
LANES = 128
MUON_PASSES = (1, 1, 1, 3, 3)
NORM_EPSILON = 1e-05
MOMENTUM_DECAY = 0.5
STEP_RATE = 0.6
GAIN_RATE = 0.2
POLY_FIRST = 3.4445
POLY_SECOND = -4.775
POLY_THIRD = 2.0315
VMEM_BYTES = 56 << 20
BOTH = ("lat", "lon")
LOW = jnp.bfloat16
WIDE = jnp.float32


class Plan:
    def __init__(self, lat_count, lon_count, fine, coarse, weight):
        self.lat, self.lon = lat_count, lon_count
        self.devices = lat_count * lon_count
        self.tf, self.nf, self.channels = fine.shape
        self.tc, self.nc = coarse.shape[:2]
        self.deg_dev = weight.shape[0]
        self.degrees = self.deg_dev * lat_count
        self.half = self.degrees // 2
        self.fine_lat, self.coarse_lat = self.tf * lat_count, self.tc * lat_count
        self.fine_lon, self.coarse_lon = self.nf * lon_count, self.nc * lon_count
        self.rows = 3 * self.tf + 2 * self.tc
        self.fine_ka = math.sqrt(self.fine_lat * self.fine_lon / (4.0 * math.pi))
        self.coarse_ka = math.sqrt(self.coarse_lat * self.coarse_lon / (4.0 * math.pi))
        self.parts_lat = lat_count // 2

    def orders(self, lat_index, lon_index):
        part = lat_index // self.parts_lat
        trio = (lat_index % self.parts_lat) * self.lon + lon_index
        even = 1 - trio % 2
        pair = trio // 2
        low, high = 3 * pair, self.half + 3 * pair
        first = high + 2 * (1 - even)
        second = even * (high + 1) + (1 - even) * (low + 1)
        third = even * low + (1 - even) * (low + 2)
        return (first, second, third), part, even

    def fourier(self):
        fine = np.zeros((self.lon, 3, self.devices, self.nf))
        coarse = np.zeros((self.lon, 2, self.devices, self.nc))

        def fill(out, order, part, total):
            position = np.arange(total)
            angle = 2.0 * np.pi / total * (position * order % total)
            line = -np.sin(angle) if part else np.cos(angle)
            out[...] = line.reshape(self.lon, -1)

        for lat_index in range(self.lat):
            for lon_index in range(self.lon):
                device = lat_index * self.lon + lon_index
                orders, part, even = self.orders(lat_index, lon_index)
                for row in range(3):
                    fill(fine[:, row, device], orders[row], part, self.fine_lon)
                for row in range(1 + even):
                    fill(coarse[:, row, device], orders[row] - self.half, part, self.coarse_lon)
        results = []
        for table in (fine, coarse):
            flat = table.reshape(self.lon, -1, table.shape[-1]).astype(ml_dtypes.bfloat16)
            results += [flat, np.swapaxes(flat, 1, 2)]
        return results


def legendre_kernel(columns, weighted_out, doubled_out, slope, back, start, *, degrees, half):
    order, cosine, quadrature, doubling = (columns[row : row + 1, :] for row in range(4))
    used, diagonal = columns[4:5, :], columns[5:6, :]
    degree = lax.broadcasted_iota(jnp.int32, slope.shape, 0).astype(WIDE)

    def factor(at):
        square = at * at
        return jnp.sqrt(
            jnp.maximum(4.0 * square - 1.0, 1.0) / jnp.maximum(square - order * order, 1.0)
        )

    now = factor(degree)
    running = (degree > order) & (degree < used)
    slope[...] = jnp.where(running, now * cosine, 0.0)
    back[...] = jnp.where(running, now / factor(degree - 1.0), 0.0)
    start[...] = jnp.where((degree == order) & (degree < used), diagonal, 0.0)

    def step(block, carried):
        latest, earlier = carried
        base = pl.multiple_of(block * 8, 8)
        slopes, backs, starts = (ref[pl.ds(base, 8), :] for ref in (slope, back, start))
        found = []
        for row in range(8):
            at = slice(row, row + 1)
            latest, earlier = slopes[at] * latest - backs[at] * earlier + starts[at], latest
            found.append(latest)
        start[pl.ds(base, 8), :] = jnp.concatenate(found, axis=0)
        return latest, earlier

    zero = jnp.zeros_like(order)
    lax.fori_loop(0, degrees // 8, step, (zero, zero))
    plain = start[...]
    weighted_out[...] = (quadrature * plain).astype(LOW)
    doubled_out[...] = (doubling * plain.astype(LOW).astype(WIDE)).astype(LOW)


def legendre_tables(plan, lat_index, lon_index):
    orders, part, even = plan.orders(lat_index, lon_index)
    fine_kind = np.repeat(np.arange(3), plan.tf)
    coarse_kind = np.repeat(np.arange(2), plan.tc)
    kind = np.tile(np.concatenate([fine_kind, coarse_kind]), plan.devices)
    is_fine = np.tile(np.arange(plan.rows) < 3 * plan.tf, plan.devices)
    lat_of = np.repeat(np.arange(plan.devices) // plan.lon, plan.rows)
    fine_lat = lat_of * plan.tf + np.tile(np.arange(plan.rows) % plan.tf, plan.devices)
    coarse_lat = lat_of * plan.tc + np.tile(np.arange(plan.rows) % plan.tc, plan.devices)
    position = np.where(is_fine, fine_lat, coarse_lat)
    count = np.where(is_fine, plan.fine_lat, plan.coarse_lat)
    colatitude = np.pi * (position + 0.5) / count
    own = jnp.where(kind == 0, orders[0], jnp.where(kind == 1, orders[1], orders[2]))
    own = jnp.where(is_fine, own, own - plan.half)
    held = own >= 0
    own = jnp.maximum(own, 0)
    span = np.arange(plan.degrees)
    norms = np.array(
        [
            0.5
            * (
                math.log((2.0 * m + 1.0) / (4.0 * math.pi))
                + math.lgamma(m + 0.5)
                - math.lgamma(m + 1.0)
                - 0.5 * math.log(math.pi)
            )
            for m in span
        ],
        np.float32,
    )
    norm = jnp.sum(jnp.where(own[None, :] == span[:, None], norms[:, None], 0.0), axis=0)
    log_sine = np.log(np.sin(colatitude)).astype(np.float32)
    diagonal = jnp.where(held, jnp.exp(norm + own.astype(WIDE) * log_sine), 0.0)
    columns = jnp.stack(
        [
            own.astype(WIDE),
            jnp.asarray(np.cos(colatitude).astype(np.float32)),
            jnp.asarray((np.pi / count * np.sin(colatitude)).astype(np.float32)),
            jnp.where(own == 0, 1.0, 2.0),
            jnp.asarray(np.where(is_fine, plan.degrees, plan.half).astype(np.float32)),
            diagonal,
        ]
    )
    shape = (plan.degrees, plan.devices * plan.rows)
    compact = pl.pallas_call(
        functools.partial(legendre_kernel, degrees=plan.degrees, half=plan.half),
        out_shape=(jax.ShapeDtypeStruct(shape, LOW),) * 2,
        scratch_shapes=[pltpu.VMEM(shape, WIDE)] * 3,
        compiler_params=pltpu.CompilerParams(vmem_limit_bytes=VMEM_BYTES),
        name="legendre",
    )(columns)
    chosen = kind[None, :] == np.arange(4)[:, None]
    pairs = plan.deg_dev // OWNED
    results = []
    for table in compact:
        spread = table.reshape(plan.lat, pairs, OWNED, 1, shape[1])
        spread = jnp.where(chosen, spread, jnp.zeros_like(spread))
        spread = jnp.pad(spread, ((0, 0), (0, plan.lon - pairs), (0, 0), (0, 0), (0, 0)))
        results.append(spread.reshape(plan.devices * 8, shape[1]))
    return results


def wide_dot(left, right, contract=((1,), (0,))):
    return lax.dot_general(left, right, (contract, ((), ())), preferred_element_type=WIDE)


def normalize(values):
    shifted = values - jnp.mean(values, axis=-1, keepdims=True)
    inverse = lax.rsqrt(jnp.mean(shifted * shifted, axis=-1, keepdims=True) + NORM_EPSILON)
    return shifted * inverse, inverse


def norm_back(grad, unit, inverse):
    return (
        grad
        - jnp.mean(grad, axis=-1, keepdims=True)
        - unit * jnp.mean(grad * unit, axis=-1, keepdims=True)
    ) * inverse


def kernel_call(kernel, name, out_shape, scratch=()):
    return pl.pallas_call(
        kernel,
        out_shape=out_shape,
        scratch_shapes=[pltpu.VMEM(*each) for each in scratch],
        compiler_params=pltpu.CompilerParams(vmem_limit_bytes=VMEM_BYTES),
        name=name,
    )


class Blocks:
    def __init__(self, plan):
        self.plan = plan
        self.items = [(0, t) for t in range(plan.tf)] + [(1, t) for t in range(plan.tc)]

    def strides(self, grid, t):
        plan = self.plan
        starts = (
            [row * plan.tf + t for row in range(3)]
            if grid == 0
            else [3 * plan.tf + row * plan.tc + t for row in range(2)]
        )
        return [pl.ds(start, plan.devices, stride=plan.rows) for start in starts]

    def load(self, scratch, received):
        for lane in range(scratch.shape[0]):
            scratch[lane] = received[:, lane * LANES : (lane + 1) * LANES].astype(WIDE)

    def store(self, scratch, sent):
        for lane in range(scratch.shape[0]):
            sent[:, lane * LANES : (lane + 1) * LANES] = scratch[lane].astype(LOW)

    def put(self, scratch, grid, t, table, values, scale):
        summed = wide_dot(table, values) * scale
        for row, where in enumerate(self.strides(grid, t)):
            part = summed[row * self.plan.devices : (row + 1) * self.plan.devices]
            for lane in range(scratch.shape[0]):
                scratch[lane, where, :] = part[:, lane * LANES : (lane + 1) * LANES]

    def take(self, scratch, grid, t, table, scale):
        found = [
            jnp.concatenate([scratch[lane, where, :] for lane in range(scratch.shape[0])], axis=1)
            for where in self.strides(grid, t)
        ]
        values = jnp.concatenate(found, axis=0).astype(LOW)
        return (wide_dot(table, values) * scale).astype(LOW).astype(WIDE)


def front_kernel(fine, coarse, gains, table_fine, table_coarse, sent, scratch, *, plan, scales):
    blocks = Blocks(plan)
    grids, tables = (fine, coarse), (table_fine, table_coarse)
    for grid, t in blocks.items:
        unit, inverse = normalize(grids[grid][t].astype(WIDE))
        normed = (unit * gains[0:1, :]).astype(LOW)
        blocks.put(scratch, grid, t, tables[grid][...], normed, scales[grid])
    blocks.store(scratch, sent)


def middle_kernel(
    fine, coarse, fine_up, coarse_up, received, gains, first, second,
    table_fine, table_coarse, back_fine, back_coarse,
    fine_out, coarse_out, fine_left, coarse_left, sent, hidden, gain, scratch, *, plan, scales,
):
    blocks = Blocks(plan)
    grids, ups, outs, lefts = (
        (fine, coarse), (fine_up, coarse_up), (fine_out, coarse_out), (fine_left, coarse_left)
    )
    tables, backs = (table_fine, table_coarse), (back_fine, back_coarse)
    root = math.sqrt(2.0 / math.pi)
    scaling = gains[1:2, :]
    first_low, second_low = first[...], second[...]
    first_sum = second_sum = gain_sum = None
    blocks.load(scratch, received)
    branches = [blocks.take(scratch, grid, t, backs[grid][...], scales[grid]) for grid, t in blocks.items]
    for (grid, t), branch in zip(blocks.items, branches):
        residual = grids[grid][t].astype(WIDE) + branch
        unit, inverse = normalize(residual)
        normed = (unit * scaling).astype(LOW)
        pre = wide_dot(normed, first_low)
        square = pre * pre
        bent = jnp.tanh(root * pre * (1.0 + 0.044715 * square))
        active = (0.5 * pre * (1.0 + bent)).astype(LOW)
        outs[grid][t] = (residual + wide_dot(active, second_low, ((1,), (1,)))).astype(LOW)
        upstream = ups[grid][t]
        slope = 0.5 * (1.0 + bent) + 0.5 * pre * (1.0 - bent * bent) * root * (1.0 + 3.0 * 0.044715 * square)
        pre_grad = (wide_dot(upstream, second_low) * slope).astype(LOW)
        normed_grad = wide_dot(pre_grad, first_low, ((1,), (1,)))
        left = upstream.astype(WIDE) + norm_back(normed_grad * scaling, unit, inverse)
        left_low = left.astype(LOW)
        lefts[grid][t] = left_low
        blocks.put(scratch, grid, t, tables[grid][...], left_low, scales[grid])
        first_part = wide_dot(normed, pre_grad, ((0,), (0,)))
        second_part = wide_dot(upstream, active, ((0,), (0,)))
        gain_part = jnp.sum(normed_grad * unit, axis=0, keepdims=True)
        if first_sum is None:
            first_sum, second_sum, gain_sum = first_part, second_part, gain_part
        else:
            first_sum, second_sum, gain_sum = (
                first_sum + first_part, second_sum + second_part, gain_sum + gain_part
            )
    blocks.store(scratch, sent)
    hidden[0] = first_sum.astype(LOW)
    hidden[1] = second_sum.astype(LOW)
    gain[...] = gain_sum


def last_kernel(
    fine, coarse, fine_left, coarse_left, received, gains, back_fine, back_coarse,
    fine_out, coarse_out, scratch, *, plan, scales,
):
    blocks = Blocks(plan)
    grids, lefts, outs = (fine, coarse), (fine_left, coarse_left), (fine_out, coarse_out)
    backs = (back_fine, back_coarse)
    blocks.load(scratch, received)
    for grid, t in blocks.items:
        normed_grad = blocks.take(scratch, grid, t, backs[grid][...], scales[grid])
        unit, inverse = normalize(grids[grid][t].astype(WIDE))
        outs[grid][t] = (
            lefts[grid][t].astype(WIDE) + norm_back(normed_grad * gains[0:1, :], unit, inverse)
        ).astype(LOW)


def row_masks(count):
    slot = lax.broadcasted_iota(jnp.int32, (count, 1), 0) % 8
    return [(slot // 4 == owned) & (slot % 4 < RIDER) for owned in range(OWNED)], slot == RIDER


def mixing(rows, weights, masks, sign, contract):
    split = rows.shape[0] // 2
    top, bottom = None, None
    for owned in range(OWNED):
        chosen = jnp.where(masks[owned], rows, 0.0).astype(LOW)
        by_real = wide_dot(chosen, weights[owned, 0], contract)
        by_imag = wide_dot(chosen, weights[owned, 1], contract) * sign
        up = by_real[:split] - by_imag[split:]
        down = by_real[split:] + by_imag[:split]
        top, bottom = (up, down) if top is None else (top + up, bottom + down)
    return top, bottom


def mix_kernel(held, weights, out):
    split = held.shape[0] // 2
    masks, rider = row_masks(held.shape[0])
    top, bottom = mixing(held[...].astype(WIDE), weights, masks, 1.0, ((1,), (1,)))
    out[:split] = top.astype(LOW)
    out[split:] = bottom.astype(LOW)


def mix_back_kernel(grads, held, weights, gains, out, own, own_low, gain):
    count = held.shape[0]
    split = count // 2
    masks, rider = row_masks(count)
    coeffs = held[...].astype(WIDE)
    rows = grads[...].astype(WIDE)
    gain[...] = jnp.sum(jnp.where(rider, rows, 0.0), axis=0, keepdims=True)
    top, bottom = mixing(rows, weights, masks, -1.0, ((1,), (0,)))
    back = jnp.concatenate([top, bottom], axis=0)
    gain_row = jnp.sum(back * coeffs, axis=0, keepdims=True) / gains[0:1, :]
    out[...] = jnp.where(rider, gain_row, back).astype(LOW)
    straight = grads[...]
    swapped = jnp.concatenate([rows[split:], -rows[:split]], axis=0).astype(LOW)
    for owned in range(OWNED):
        picked = jnp.where(masks[owned], coeffs, 0.0).astype(LOW)
        for part, side in enumerate((straight, swapped)):
            value = wide_dot(side, picked, ((0,), (0,)))
            own[owned, part] = value
            for block in range(own_low.shape[0]):
                size = own_low.shape[3]
                own_low[block, owned, part] = value[block * size : (block + 1) * size].astype(LOW)


def split_low(value, passes):
    high = value.astype(LOW)
    if passes == 1:
        return (high,)
    return (high, (value - high.astype(WIDE)).astype(LOW))


def multi_dot(left, right, contract=((1,), (0,))):
    total = wide_dot(left[0], right[0], contract)
    if len(left) > 1:
        total = total + (wide_dot(left[0], right[1], contract) + wide_dot(left[1], right[0], contract))
    return total


def complex_muon_kernel(grads, momentum, out):
    states = []
    for owned in range(OWNED):
        parts = [MOMENTUM_DECAY * momentum[owned, part] + grads[owned, part] for part in range(2)]
        total = jnp.sum(parts[0] * parts[0]) + jnp.sum(parts[1] * parts[1])
        scale = 1.0 / (jnp.sqrt(total) + 1e-07)
        states.append([part * scale for part in parts])
    rows_by_rows = ((1,), (1,))
    for passes in MUON_PASSES:
        for state in states:
            real, imag = state
            low_real, low_imag = split_low(real, passes), split_low(imag, passes)
            gram_real = multi_dot(low_real, low_real, rows_by_rows) + multi_dot(low_imag, low_imag, rows_by_rows)
            gram_imag = multi_dot(low_imag, low_real, rows_by_rows) - multi_dot(low_real, low_imag, rows_by_rows)
            low_gram_real, low_gram_imag = split_low(gram_real, passes), split_low(gram_imag, passes)
            square_real = multi_dot(low_gram_real, low_gram_real) - multi_dot(low_gram_imag, low_gram_imag)
            square_imag = multi_dot(low_gram_real, low_gram_imag) + multi_dot(low_gram_imag, low_gram_real)
            poly_real = split_low(POLY_SECOND * gram_real + POLY_THIRD * square_real, passes)
            poly_imag = split_low(POLY_SECOND * gram_imag + POLY_THIRD * square_imag, passes)
            state[0] = POLY_FIRST * real + (multi_dot(poly_real, low_real) - multi_dot(poly_imag, low_imag))
            state[1] = POLY_FIRST * imag + (multi_dot(poly_real, low_imag) + multi_dot(poly_imag, low_real))
    size = out.shape[3]
    for owned in range(OWNED):
        for part in range(2):
            for block in range(out.shape[0]):
                out[block, owned, part] = states[owned][part][block * size : (block + 1) * size].astype(LOW)


def real_muon_kernel(grads, momentum, weight, grad_out, moment_out, updated_out, low_out):
    currents = []
    for part in range(2):
        grad = grads[part].astype(WIDE)
        grad_out[part] = grad
        moment = MOMENTUM_DECAY * momentum[part] + grad
        moment_out[part] = moment
        currents.append(moment * (1.0 / (jnp.sqrt(jnp.sum(moment * moment)) + 1e-07)))
    for passes in MUON_PASSES:
        for part in range(2):
            current = currents[part]
            low = split_low(current, passes)
            gram = multi_dot(low, low, ((1,), (1,)))
            low_gram = split_low(gram, passes)
            poly = split_low(POLY_SECOND * gram + POLY_THIRD * multi_dot(low_gram, low_gram), passes)
            currents[part] = POLY_FIRST * current + multi_dot(poly, low)
    for part in range(2):
        updated = weight[part] - STEP_RATE * currents[part]
        updated_out[part] = updated
        low_out[part] = updated.astype(LOW)


def exchange(rows, axes, count):
    block = rows.reshape((count, -1) + rows.shape[1:])
    return lax.all_to_all(block, axes, 0, 0, tiled=True).reshape(rows.shape)


def to_owners(plan, rows):
    held, block = rows.shape[0], rows.shape[2]
    padded = jnp.pad(rows, ((0, plan.lon * OWNED - held), (0, 0), (0, 0), (0, 0)))
    padded = padded.reshape(plan.lon, OWNED, 2, block, plan.channels)
    got = lax.all_to_all(padded, "lon", 0, 0, tiled=True)
    return jnp.transpose(got, (1, 2, 0, 3, 4)).reshape(OWNED, 2, plan.lon * block, plan.channels)


def from_owners(plan, sent):
    got = lax.all_to_all(sent, "lon", 0, 0, tiled=True)
    return got.reshape((plan.lon * OWNED,) + sent.shape[2:])[: plan.deg_dev]


def body(
    fine_grid,
    coarse_grid,
    fine_cotangent,
    coarse_cotangent,
    spectral_weight,
    spectral_momentum,
    hidden_weight,
    hidden_momentum,
    norm_gains,
    gain_momentum,
):
    plan = Plan(lax.axis_size("lat"), lax.axis_size("lon"), fine_grid, coarse_grid, spectral_weight)
    lat_index, lon_index = lax.axis_index("lat"), lax.axis_index("lon")
    channels, devices = plan.channels, plan.devices
    block_rows = channels // plan.lon
    fine_table, fine_back, coarse_table, coarse_back = (
        lax.dynamic_index_in_dim(jnp.asarray(table), lon_index, 0, keepdims=False)
        for table in plan.fourier()
    )
    exchanged = jax.ShapeDtypeStruct((devices * plan.rows, channels), LOW)
    rows_scratch = [((channels // LANES, devices * plan.rows, LANES), WIDE)]
    owned_rows = jax.ShapeDtypeStruct((devices * 8, channels), LOW)
    grid_low = [jax.ShapeDtypeStruct(grid.shape, LOW) for grid in (fine_grid, coarse_grid)]
    forward_scales = (
        2.0 * math.pi / plan.fine_lon * plan.fine_ka,
        2.0 * math.pi / plan.coarse_lon * plan.coarse_ka,
    )
    inverse_scales = (1.0 / plan.fine_ka, 1.0 / plan.coarse_ka)

    sent = kernel_call(
        functools.partial(front_kernel, plan=plan, scales=forward_scales), "front", exchanged, rows_scratch
    )(fine_grid, coarse_grid, norm_gains, fine_table, coarse_table)
    spectrum = exchange(sent, BOTH, devices)
    weighted, doubled = legendre_tables(plan, lat_index, lon_index)
    weights = to_owners(plan, spectral_weight.astype(LOW))
    momentum = to_owners(plan, spectral_momentum)
    hidden_low = hidden_weight.astype(LOW)

    held = exchange(wide_dot(weighted, spectrum).astype(LOW), BOTH, devices)
    mixed = kernel_call(mix_kernel, "mix", owned_rows)(held, weights)
    mixed = exchange(mixed, BOTH, devices)
    values = wide_dot(doubled, mixed, ((0,), (0,))).astype(LOW)
    values = exchange(values, BOTH, devices)

    fine_out, coarse_out, fine_left, coarse_left, sent, partial_hidden, gain_second = kernel_call(
        functools.partial(middle_kernel, plan=plan, scales=inverse_scales),
        "middle",
        (
            *grid_low,
            *grid_low,
            exchanged,
            jax.ShapeDtypeStruct(hidden_weight.shape, LOW),
            jax.ShapeDtypeStruct((1, channels), WIDE),
        ),
        rows_scratch,
    )(
        fine_grid, coarse_grid, fine_cotangent, coarse_cotangent, values, norm_gains,
        hidden_low[0], hidden_low[1], fine_table, coarse_table, fine_back, coarse_back,
    )
    spectrum = exchange(sent, BOTH, devices)

    share = hidden_weight.size // devices // hidden_weight.shape[2]
    received = exchange(partial_hidden.reshape(-1, hidden_weight.shape[2]), BOTH, devices)
    summed = jnp.sum(received.reshape(devices, share, -1).astype(WIDE), axis=0).astype(LOW)
    hidden_grad = exchange(jnp.tile(summed, (devices, 1)), BOTH, devices).reshape(hidden_weight.shape)

    mixed_grad = wide_dot(doubled, spectrum)
    riding = jnp.arange(8)[None, :, None] == RIDER
    mixed_grad = jnp.where(riding, gain_second[None], mixed_grad.reshape(devices, 8, channels))
    mixed_grad = exchange(mixed_grad.reshape(-1, channels).astype(LOW), BOTH, devices)
    owner_shape = (plan.lon, OWNED, 2, block_rows, channels)
    coef_grad, own_grad, own_low, gain_second = kernel_call(
        mix_back_kernel,
        "mix_back",
        (
            owned_rows,
            jax.ShapeDtypeStruct((OWNED, 2, channels, channels), WIDE),
            jax.ShapeDtypeStruct(owner_shape, LOW),
            jax.ShapeDtypeStruct((1, channels), WIDE),
        ),
    )(mixed_grad, held, weights, norm_gains)
    coef_grad = exchange(coef_grad, BOTH, devices)
    gain_first = jnp.sum(
        coef_grad.reshape(devices, 8, channels)[:, RIDER].astype(WIDE), axis=0, keepdims=True
    )
    values = wide_dot(weighted, coef_grad, ((0,), (0,))).astype(LOW)
    values = exchange(values, BOTH, devices)
    fine_gradient, coarse_gradient = kernel_call(
        functools.partial(last_kernel, plan=plan, scales=forward_scales), "last", tuple(grid_low), rows_scratch
    )(fine_grid, coarse_grid, fine_left, coarse_left, values, norm_gains, fine_back, coarse_back)

    spectral_grad = from_owners(plan, own_low).astype(WIDE)
    spectral_moment = MOMENTUM_DECAY * spectral_momentum + spectral_grad
    iterate = kernel_call(complex_muon_kernel, "complex_muon", jax.ShapeDtypeStruct(owner_shape, LOW))(
        own_grad, momentum
    )
    step = from_owners(plan, iterate).astype(WIDE)
    spectral_updated = spectral_weight - STEP_RATE * step

    hidden_wide = jax.ShapeDtypeStruct(hidden_weight.shape, WIDE)
    hidden_grad, hidden_moment, hidden_updated, hidden_copy = kernel_call(
        real_muon_kernel,
        "real_muon",
        (hidden_wide, hidden_wide, hidden_wide, jax.ShapeDtypeStruct(hidden_weight.shape, LOW)),
    )(hidden_grad, hidden_momentum, hidden_weight)
    gains_total = jnp.concatenate([gain_first, gain_second])
    gain_moment = MOMENTUM_DECAY * gain_momentum + gains_total
    gain_scale = jnp.sqrt(jnp.mean(gain_moment * gain_moment, axis=-1, keepdims=True))
    gain_updated = norm_gains - GAIN_RATE * gain_moment / (gain_scale + 1e-06)
    return (
        fine_out,
        coarse_out,
        fine_gradient,
        coarse_gradient,
        spectral_grad,
        spectral_moment,
        spectral_updated,
        spectral_updated.astype(LOW),
        hidden_grad,
        hidden_moment,
        hidden_updated,
        hidden_copy,
        gains_total,
        gain_moment,
        gain_updated,
    )


def solution(mesh):
    grid = P("lat", "lon", None)
    degree = P("lat", None, "lon", None)
    return jax.shard_map(
        body,
        mesh=mesh,
        in_specs=(grid,) * 4 + (degree,) * 2 + (P(),) * 4,
        out_specs=(grid,) * 4 + (degree,) * 4 + (P(),) * 7,
        check_vma=False,
    )
```

```python
import functools
import math

import jax
import jax.numpy as jnp
import ml_dtypes
import numpy as np
from jax import lax
from jax.experimental import pallas as pl
from jax.experimental.pallas import tpu as pltpu
from jax.sharding import PartitionSpec as P

OWNED = 2
RIDER = 3
LANES = 128
NORM_EPSILON = 1e-05
MOMENTUM_DECAY = 0.5
STEP_RATE = 0.6
GAIN_RATE = 0.2
POLY_FIRST = 3.4445
POLY_SECOND = -4.775
POLY_THIRD = 2.0315
BOTH = ("lat", "lon")
LOW = jnp.bfloat16
WIDE = jnp.float32


class Plan:
    def __init__(self, lat_count, lon_count, fine, coarse, weight):
        self.lat, self.lon = lat_count, lon_count
        self.devices = lat_count * lon_count
        self.tf, self.nf, self.channels = fine.shape
        self.tc, self.nc = coarse.shape[:2]
        self.deg_dev = weight.shape[0]
        self.degrees = self.deg_dev * lat_count
        self.half = self.degrees // 2
        self.fine_lat, self.coarse_lat = self.tf * lat_count, self.tc * lat_count
        self.fine_lon, self.coarse_lon = self.nf * lon_count, self.nc * lon_count
        self.rows = 3 * self.tf + 2 * self.tc
        self.fine_ka = math.sqrt(self.fine_lat * self.fine_lon / (4.0 * math.pi))
        self.coarse_ka = math.sqrt(self.coarse_lat * self.coarse_lon / (4.0 * math.pi))
        self.parts_lat = lat_count // 2

    def orders(self, lat_index, lon_index):
        part = lat_index // self.parts_lat
        trio = (lat_index % self.parts_lat) * self.lon + lon_index
        even = 1 - trio % 2
        pair = trio // 2
        low, high = 3 * pair, self.half + 3 * pair
        first = high + 2 * (1 - even)
        second = even * (high + 1) + (1 - even) * (low + 1)
        third = even * low + (1 - even) * (low + 2)
        return (first, second, third), part, even

    def fourier(self):
        fine = np.zeros((self.lon, 3, self.devices, self.nf))
        coarse = np.zeros((self.lon, 2, self.devices, self.nc))

        def fill(out, order, part, total):
            position = np.arange(total)
            angle = 2.0 * np.pi / total * (position * order % total)
            line = -np.sin(angle) if part else np.cos(angle)
            out[...] = line.reshape(self.lon, -1)

        for lat_index in range(self.lat):
            for lon_index in range(self.lon):
                device = lat_index * self.lon + lon_index
                orders, part, even = self.orders(lat_index, lon_index)
                for row in range(3):
                    fill(fine[:, row, device], orders[row], part, self.fine_lon)
                for row in range(1 + even):
                    fill(coarse[:, row, device], orders[row] - self.half, part, self.coarse_lon)
        results = []
        for table in (fine, coarse):
            flat = table.reshape(self.lon, -1, table.shape[-1]).astype(ml_dtypes.bfloat16)
            results += [flat, np.swapaxes(flat, 1, 2)]
        return results


def legendre_kernel(columns, weighted_out, doubled_out, slope, back, start, *, degrees, half):
    order, cosine, quadrature, doubling = (columns[row : row + 1, :] for row in range(4))
    used, diagonal = columns[4:5, :], columns[5:6, :]
    degree = lax.broadcasted_iota(jnp.int32, slope.shape, 0).astype(WIDE)

    def factor(at):
        square = at * at
        return jnp.sqrt(
            jnp.maximum(4.0 * square - 1.0, 1.0) / jnp.maximum(square - order * order, 1.0)
        )

    now = factor(degree)
    running = (degree > order) & (degree < used)
    slope[...] = jnp.where(running, now * cosine, 0.0)
    back[...] = jnp.where(running, now / factor(degree - 1.0), 0.0)
    start[...] = jnp.where((degree == order) & (degree < used), diagonal, 0.0)

    def step(block, carried):
        latest, earlier = carried
        base = pl.multiple_of(block * 8, 8)
        slopes, backs, starts = (ref[pl.ds(base, 8), :] for ref in (slope, back, start))
        found = []
        for row in range(8):
            at = slice(row, row + 1)
            latest, earlier = slopes[at] * latest - backs[at] * earlier + starts[at], latest
            found.append(latest)
        start[pl.ds(base, 8), :] = jnp.concatenate(found, axis=0)
        return latest, earlier

    zero = jnp.zeros_like(order)
    lax.fori_loop(0, degrees // 8, step, (zero, zero))
    plain = start[...]
    weighted_out[...] = (quadrature * plain).astype(LOW)
    doubled_out[...] = (doubling * plain.astype(LOW).astype(WIDE)).astype(LOW)


def legendre_tables(plan, lat_index, lon_index):
    orders, part, even = plan.orders(lat_index, lon_index)
    fine_kind = np.repeat(np.arange(3), plan.tf)
    coarse_kind = np.repeat(np.arange(2), plan.tc)
    kind = np.tile(np.concatenate([fine_kind, coarse_kind]), plan.devices)
    is_fine = np.tile(np.arange(plan.rows) < 3 * plan.tf, plan.devices)
    lat_of = np.repeat(np.arange(plan.devices) // plan.lon, plan.rows)
    fine_lat = lat_of * plan.tf + np.tile(np.arange(plan.rows) % plan.tf, plan.devices)
    coarse_lat = lat_of * plan.tc + np.tile(np.arange(plan.rows) % plan.tc, plan.devices)
    position = np.where(is_fine, fine_lat, coarse_lat)
    count = np.where(is_fine, plan.fine_lat, plan.coarse_lat)
    colatitude = np.pi * (position + 0.5) / count
    own = jnp.where(kind == 0, orders[0], jnp.where(kind == 1, orders[1], orders[2]))
    own = jnp.where(is_fine, own, own - plan.half)
    held = own >= 0
    own = jnp.maximum(own, 0)
    span = np.arange(plan.degrees)
    norms = np.array(
        [
            0.5
            * (
                math.log((2.0 * m + 1.0) / (4.0 * math.pi))
                + math.lgamma(m + 0.5)
                - math.lgamma(m + 1.0)
                - 0.5 * math.log(math.pi)
            )
            for m in span
        ],
        np.float32,
    )
    norm = jnp.sum(jnp.where(own[None, :] == span[:, None], norms[:, None], 0.0), axis=0)
    log_sine = np.log(np.sin(colatitude)).astype(np.float32)
    diagonal = jnp.where(held, jnp.exp(norm + own.astype(WIDE) * log_sine), 0.0)
    columns = jnp.stack(
        [
            own.astype(WIDE),
            jnp.asarray(np.cos(colatitude).astype(np.float32)),
            jnp.asarray((np.pi / count * np.sin(colatitude)).astype(np.float32)),
            jnp.where(own == 0, 1.0, 2.0),
            jnp.asarray(np.where(is_fine, plan.degrees, plan.half).astype(np.float32)),
            diagonal,
        ]
    )
    shape = (plan.degrees, plan.devices * plan.rows)
    compact = pl.pallas_call(
        functools.partial(legendre_kernel, degrees=plan.degrees, half=plan.half),
        out_shape=(jax.ShapeDtypeStruct(shape, LOW),) * 2,
        scratch_shapes=[pltpu.VMEM(shape, WIDE)] * 3,
        compiler_params=pltpu.CompilerParams(vmem_limit_bytes=(16 if shape[1] <= 512 else 56) << 20),
        name="legendre",
    )(columns)
    chosen = kind[None, :] == np.arange(4)[:, None]
    pairs = plan.deg_dev // OWNED
    results = []
    for table in compact:
        spread = table.reshape(plan.lat, pairs, OWNED, 1, shape[1])
        spread = jnp.where(chosen, spread, jnp.zeros_like(spread))
        spread = jnp.pad(spread, ((0, 0), (0, plan.lon - pairs), (0, 0), (0, 0), (0, 0)))
        results.append(spread.reshape(plan.devices * 8, shape[1]))
    return results


def wide_dot(left, right, contract=((1,), (0,))):
    return lax.dot_general(left, right, (contract, ((), ())), preferred_element_type=WIDE)


def normalize(values):
    shifted = values - jnp.mean(values, axis=-1, keepdims=True)
    inverse = lax.rsqrt(jnp.mean(shifted * shifted, axis=-1, keepdims=True) + NORM_EPSILON)
    return shifted * inverse, inverse


def norm_back(grad, unit, inverse):
    return (
        grad
        - jnp.mean(grad, axis=-1, keepdims=True)
        - unit * jnp.mean(grad * unit, axis=-1, keepdims=True)
    ) * inverse


def kernel_call(kernel, name, out_shape, scratch=(), views=None, megabytes=16, cost=2):
    views = views or {}

    def run(place, *arrays):
        def spec(shape, at=None):
            if at in views:
                block, index = views[at]
                return pl.BlockSpec(block, lambda step, place: index(place))
            return pl.BlockSpec(tuple(shape), lambda step, place: (0,) * len(shape))

        outs = jax.tree.leaves(out_shape)
        found = pl.pallas_call(
            kernel,
            out_shape=outs,
            grid_spec=pltpu.PrefetchScalarGridSpec(
                num_scalar_prefetch=1,
                grid=(1,),
                in_specs=[spec(each.shape, at) for at, each in enumerate(arrays)],
                out_specs=[spec(each.shape) for each in outs],
                scratch_shapes=[pltpu.VMEM(*each) for each in scratch],
            ),
            compiler_params=pltpu.CompilerParams(vmem_limit_bytes=megabytes << 20),
            cost_estimate=estimate(cost),
            name=name,
        )(place, *arrays)
        return jax.tree.unflatten(jax.tree.structure(out_shape), found)

    return run


def estimate(microseconds):
    return pl.CostEstimate(
        flops=int(microseconds * 1.1e9), bytes_accessed=int(microseconds * 3e6), transcendentals=0
    )


def of_lon(table):
    return (None,) + table.shape[1:], lambda place: (place[1], 0, 0)


def cut(block, size):
    return pl.ds(pl.multiple_of(block * size, size), size)


class Blocks:
    def __init__(self, plan):
        self.plan = plan
        self.items = [(0, t) for t in range(plan.tf)] + [(1, t) for t in range(plan.tc)]

    def strides(self, grid, t):
        plan = self.plan
        starts = (
            [row * plan.tf + t for row in range(3)]
            if grid == 0
            else [3 * plan.tf + row * plan.tc + t for row in range(2)]
        )
        return [pl.ds(start, plan.devices, stride=plan.rows) for start in starts]

    def load(self, scratch, received):
        for lane in range(scratch.shape[0]):
            scratch[lane] = received[:, lane * LANES : (lane + 1) * LANES].astype(WIDE)

    def store(self, scratch, sent):
        for lane in range(scratch.shape[0]):
            sent[:, lane * LANES : (lane + 1) * LANES] = scratch[lane].astype(LOW)

    def put(self, scratch, grid, t, table, values, scale):
        summed = wide_dot(table, values) * scale
        for row, where in enumerate(self.strides(grid, t)):
            part = summed[row * self.plan.devices : (row + 1) * self.plan.devices]
            for lane in range(scratch.shape[0]):
                scratch[lane, where, :] = part[:, lane * LANES : (lane + 1) * LANES]

    def take(self, scratch, grid, t, table, scale):
        found = [
            jnp.concatenate([scratch[lane, where, :] for lane in range(scratch.shape[0])], axis=1)
            for where in self.strides(grid, t)
        ]
        values = jnp.concatenate(found, axis=0).astype(LOW)
        return (wide_dot(table, values) * scale).astype(LOW).astype(WIDE)


def front_kernel(place, fine, coarse, gains, table_fine, table_coarse, sent, scratch, *, plan, scales):
    blocks = Blocks(plan)
    grids, tables = (fine, coarse), (table_fine, table_coarse)
    for grid, t in blocks.items:
        unit, inverse = normalize(grids[grid][t].astype(WIDE))
        normed = (unit * gains[0:1, :]).astype(LOW)
        blocks.put(scratch, grid, t, tables[grid][...], normed, scales[grid])
    blocks.store(scratch, sent)


def middle_kernel(
    place, fine, coarse, fine_up, coarse_up, received, gains, first, second,
    table_fine, table_coarse, back_fine, back_coarse,
    fine_out, coarse_out, fine_left, coarse_left, sent, gain, *rest, plan, scales,
):
    *pieces, scratch, hidden = rest
    blocks = Blocks(plan)
    grids, ups, outs, lefts = (
        (fine, coarse), (fine_up, coarse_up), (fine_out, coarse_out), (fine_left, coarse_left)
    )
    tables, backs = (table_fine, table_coarse), (back_fine, back_coarse)
    root = math.sqrt(2.0 / math.pi)
    scaling = gains[1:2, :]
    first_low, second_low = first[...], second[...]
    first_sum = second_sum = gain_sum = None
    blocks.load(scratch, received)
    branches = [blocks.take(scratch, grid, t, backs[grid][...], scales[grid]) for grid, t in blocks.items]
    for (grid, t), branch in zip(blocks.items, branches):
        residual = grids[grid][t].astype(WIDE) + branch
        unit, inverse = normalize(residual)
        normed = (unit * scaling).astype(LOW)
        pre = wide_dot(normed, first_low)
        square = pre * pre
        bent = jnp.tanh(root * pre * (1.0 + 0.044715 * square))
        active = (0.5 * pre * (1.0 + bent)).astype(LOW)
        outs[grid][t] = (residual + wide_dot(active, second_low, ((1,), (1,)))).astype(LOW)
        upstream = ups[grid][t]
        slope = 0.5 * (1.0 + bent) + 0.5 * pre * (1.0 - bent * bent) * root * (1.0 + 3.0 * 0.044715 * square)
        pre_grad = (wide_dot(upstream, second_low) * slope).astype(LOW)
        normed_grad = wide_dot(pre_grad, first_low, ((1,), (1,)))
        left = upstream.astype(WIDE) + norm_back(normed_grad * scaling, unit, inverse)
        left_low = left.astype(LOW)
        lefts[grid][t] = left_low
        blocks.put(scratch, grid, t, tables[grid][...], left_low, scales[grid])
        first_part = wide_dot(normed, pre_grad, ((0,), (0,)))
        second_part = wide_dot(upstream, active, ((0,), (0,)))
        gain_part = jnp.sum(normed_grad * unit, axis=0, keepdims=True)
        if first_sum is None:
            first_sum, second_sum, gain_sum = first_part, second_part, gain_part
        else:
            first_sum, second_sum, gain_sum = (
                first_sum + first_part, second_sum + second_part, gain_sum + gain_part
            )
    blocks.store(scratch, sent)
    gain[...] = gain_sum
    hidden[: plan.channels] = first_sum
    hidden[plan.channels :] = second_sum
    size = pieces[0].shape[0]
    for shift, piece in enumerate(pieces):
        block = (place[0] + shift) % len(pieces)
        piece[...] = hidden[cut(block, size), :].astype(piece.dtype)


def last_kernel(
    place, fine, coarse, fine_left, coarse_left, received, gains, back_fine, back_coarse,
    fine_out, coarse_out, scratch, *, plan, scales,
):
    blocks = Blocks(plan)
    grids, lefts, outs = (fine, coarse), (fine_left, coarse_left), (fine_out, coarse_out)
    backs = (back_fine, back_coarse)
    blocks.load(scratch, received)
    for grid, t in blocks.items:
        normed_grad = blocks.take(scratch, grid, t, backs[grid][...], scales[grid])
        unit, inverse = normalize(grids[grid][t].astype(WIDE))
        outs[grid][t] = (
            lefts[grid][t].astype(WIDE) + norm_back(normed_grad * gains[0:1, :], unit, inverse)
        ).astype(LOW)


def row_masks(count):
    slot = lax.broadcasted_iota(jnp.int32, (count, 1), 0) % 8
    return [(slot // 4 == owned) & (slot % 4 < RIDER) for owned in range(OWNED)], slot == RIDER


def mixing(rows, weights, masks, sign, contract):
    split = rows.shape[0] // 2
    top, bottom = None, None
    for owned in range(OWNED):
        chosen = jnp.where(masks[owned], rows, 0.0).astype(LOW)
        by_real = wide_dot(chosen, weights[owned, 0], contract)
        by_imag = wide_dot(chosen, weights[owned, 1], contract) * sign
        up = by_real[:split] - by_imag[split:]
        down = by_real[split:] + by_imag[:split]
        top, bottom = (up, down) if top is None else (top + up, bottom + down)
    return top, bottom


class Joined:
    def __init__(self, ref):
        self.ref = ref

    def __getitem__(self, at):
        value = self.ref[at[0], at[1]]
        return value.reshape(-1, value.shape[-1])


def collect(own, pieces, target):
    for shift, piece in enumerate(pieces):
        source = (own + len(pieces) - shift) % len(pieces)
        for owned in range(OWNED):
            for part in range(2):
                target[owned, part, source] = piece[owned, part]


def mix_kernel(place, held, *refs):
    *pieces, out, weights = refs
    collect(place[1], pieces, weights)
    split = held.shape[0] // 2
    masks, rider = row_masks(held.shape[0])
    top, bottom = mixing(held[...].astype(WIDE), Joined(weights), masks, 1.0, ((1,), (1,)))
    out[:split] = top.astype(LOW)
    out[split:] = bottom.astype(LOW)


def sum_kernel(place, *refs, axis):
    *pieces, out, ordered = refs
    for shift, piece in enumerate(pieces):
        ordered[(place[axis] + len(pieces) - shift) % len(pieces)] = piece[...].astype(WIDE)
    total = ordered[0]
    for at in range(1, len(pieces)):
        total = total + ordered[at]
    out[...] = total.astype(out.dtype)


def join_kernel(place, table, spectrum, gain, out):
    masks, rider = row_masks(table.shape[0])
    out[...] = jnp.where(rider, gain[...], wide_dot(table[...], spectrum[...])).astype(LOW)


def mix_back_kernel(place, received, held, weights, gains, out, gain):
    masks, rider = row_masks(held.shape[0])
    rows = received[...].astype(WIDE)
    gain[...] = jnp.sum(jnp.where(rider, rows, 0.0), axis=0, keepdims=True)
    top, bottom = mixing(rows, Joined(weights), masks, -1.0, ((1,), (0,)))
    back = jnp.concatenate([top, bottom], axis=0)
    gain_row = jnp.sum(back * held[...].astype(WIDE), axis=0, keepdims=True) / gains[0:1, :]
    out[...] = jnp.where(rider, gain_row, back).astype(LOW)


def spread_kernel(place, table, received, second, momentum, gains, out, total_out, moment_out, updated_out):
    masks, rider = row_masks(table.shape[0])
    out[...] = wide_dot(table[...], received[...], ((0,), (0,))).astype(LOW)
    first = jnp.sum(jnp.where(rider, received[...].astype(WIDE), 0.0), axis=0, keepdims=True)
    for row, total in enumerate((first, second[...])):
        at = slice(row, row + 1)
        total_out[at, :] = total
        moment = MOMENTUM_DECAY * momentum[at, :] + total
        moment_out[at, :] = moment
        scale = jnp.sqrt(jnp.mean(moment * moment, axis=-1, keepdims=True)) + 1e-06
        updated_out[at, :] = gains[at, :] - GAIN_RATE * moment / scale


def scatter(own, source, pieces, kind):
    size = pieces[0].shape[3]
    for shift, piece in enumerate(pieces):
        block = (own + shift) % len(pieces)
        for owned in range(OWNED):
            for part in range(2):
                piece[kind, owned, part] = source[owned, part, cut(block, size), :].astype(LOW)


def shift_gram(gram):
    size = gram.shape[0]
    unit = lax.broadcasted_iota(jnp.int32, gram.shape, 0) == lax.broadcasted_iota(jnp.int32, gram.shape, 1)
    level = jnp.sum(jnp.sum(jnp.where(unit, gram, 0.0), axis=1, keepdims=True), axis=0, keepdims=True) / size
    keep = POLY_FIRST + level * (POLY_SECOND + POLY_THIRD * level)
    return jnp.where(unit, gram - level, gram), keep, POLY_SECOND + 2.0 * POLY_THIRD * level


def beside(left, right):
    return jnp.concatenate([left, right], axis=1)


def below(top, bottom):
    return jnp.concatenate([top, bottom], axis=0)


def complex_rows(real, imag):
    return below(beside(real, -imag), beside(imag, real))


def complex_muon_kernel(place, mixed_grads, held, *refs):
    count = (len(refs) - 3) // 2
    sources, pieces, (momentum, grads, result) = refs[:count], refs[count : 2 * count], refs[2 * count :]
    collect(place[1], sources, momentum)
    masks, rider = row_masks(held.shape[0])
    split = held.shape[0] // 2
    coeffs, rows = held[...].astype(WIDE), mixed_grads[...].astype(WIDE)
    swapped = jnp.concatenate([rows[split:], -rows[:split]], axis=0).astype(LOW)
    for owned in range(OWNED):
        picked = jnp.where(masks[owned], coeffs, 0.0).astype(LOW)
        for part, side in enumerate((mixed_grads[...], swapped)):
            grads[owned, part] = wide_dot(side, picked, ((0,), (0,)))
    momentum = Joined(momentum)
    states = []
    for owned in range(OWNED):
        parts = [
            MOMENTUM_DECAY * momentum[owned, part].astype(WIDE) + grads[owned, part] for part in range(2)
        ]
        total = jnp.sum(parts[0] * parts[0]) + jnp.sum(parts[1] * parts[1])
        scale = 1.0 / (jnp.sqrt(total) + 1e-07)
        states.append([part * scale for part in parts])
    for iteration in range(5):
        for state in states:
            size = state[0].shape[0]
            real, imag = state[0].astype(LOW), state[1].astype(LOW)
            side = beside(real, imag)
            gram = wide_dot(below(side, beside(imag, -real)), side, ((1,), (1,)))
            rest, keep, lead = shift_gram(gram[:size])
            gram = below(rest, gram[size:])
            low = gram.astype(LOW)
            square = wide_dot(complex_rows(low[:size], low[size:]), low)
            poly = (lead * gram + POLY_THIRD * square).astype(LOW)
            change = wide_dot(complex_rows(poly[:size], poly[size:]), below(real, imag))
            state[0] = keep * state[0] + change[:size]
            state[1] = keep * state[1] + change[size:]
    for owned in range(OWNED):
        for part in range(2):
            result[owned, part] = states[owned][part]
    scatter(place[1], grads, pieces, 0)
    scatter(place[1], result, pieces, 1)


def real_muon_kernel(place, momentum, weight, *refs):
    *pieces, grad_out, moment_out, updated_out, low_out, gathered = refs
    for shift, piece in enumerate(pieces):
        gathered[(place[0] + len(pieces) - shift) % len(pieces)] = piece[...].astype(WIDE)
    whole = gathered[...].reshape(momentum.shape)
    currents = []
    for part in range(2):
        grad = whole[part]
        grad_out[part] = grad
        moment = MOMENTUM_DECAY * momentum[part] + grad
        moment_out[part] = moment
        currents.append(moment * (1.0 / (jnp.sqrt(jnp.sum(moment * moment)) + 1e-07)))
    for iteration in range(5):
        for part in range(2):
            current = currents[part]
            low = current.astype(LOW)
            rest, keep, lead = shift_gram(wide_dot(low, low, ((1,), (1,))))
            low_rest = rest.astype(LOW)
            poly = lead * rest + POLY_THIRD * wide_dot(low_rest, low_rest)
            currents[part] = keep * current + wide_dot(poly.astype(LOW), low)
    for part in range(2):
        updated = weight[part] - STEP_RATE * currents[part]
        updated_out[part] = updated
        low_out[part] = updated.astype(LOW)


def finish_kernel(place, momentum, weight, *refs, count):
    pieces, (grad_out, moment_out, updated_out, low_out) = refs[:count], refs[count:]
    shift = (place[1] + count - pl.program_id(0)) % count
    for at in range(count):

        @pl.when(shift == at)
        def _():
            grad = pieces[at][0].astype(WIDE)
            grad_out[...] = grad
            moment_out[...] = MOMENTUM_DECAY * momentum[...] + grad
            updated = weight[...] - STEP_RATE * pieces[at][1].astype(WIDE)
            updated_out[...] = updated
            low_out[...] = updated.astype(LOW)


def finish(place, momentum, weight, pieces):
    shape, count = weight.shape, len(pieces)
    block = pl.BlockSpec((OWNED,) + shape[1:], lambda owner, at: (owner, 0, 0, 0))
    whole = pl.BlockSpec(pieces[0].shape, lambda owner, at: (0, 0, 0, 0, 0))
    return pl.pallas_call(
        functools.partial(finish_kernel, count=count),
        out_shape=[jax.ShapeDtypeStruct(shape, dtype) for dtype in (WIDE, WIDE, WIDE, LOW)],
        grid_spec=pltpu.PrefetchScalarGridSpec(
            num_scalar_prefetch=1,
            grid=(shape[0] // OWNED,),
            in_specs=[block] * 2 + [whole] * count,
            out_specs=[block] * 4,
        ),
        compiler_params=pltpu.CompilerParams(vmem_limit_bytes=60 << 20),
        cost_estimate=estimate(6),
        name="finish",
    )(place, momentum, weight, *pieces)


def exchange(rows, axes, count):
    block = rows.reshape((count, -1) + rows.shape[1:])
    return lax.all_to_all(block, axes, 0, 0, tiled=True).reshape(rows.shape)


def shifted(piece, shift, count, axis="lon"):
    return lax.ppermute(piece, axis, [(source, (source + shift) % count) for source in range(count)])


def for_owners(plan, rows, lon_index, owners):
    pieces = []
    for shift in range(plan.lon):
        owner = jnp.minimum((lon_index + shift) % plan.lon, owners - 1)
        pieces.append(lax.dynamic_slice_in_dim(rows, owner * OWNED, OWNED, 0).astype(LOW))
    return pieces


def together(*values):
    return lax.optimization_barrier(values)


def body(
    fine_grid,
    coarse_grid,
    fine_cotangent,
    coarse_cotangent,
    spectral_weight,
    spectral_momentum,
    hidden_weight,
    hidden_momentum,
    norm_gains,
    gain_momentum,
):
    plan = Plan(lax.axis_size("lat"), lax.axis_size("lon"), fine_grid, coarse_grid, spectral_weight)
    lat_index, lon_index = lax.axis_index("lat"), lax.axis_index("lon")
    place = jnp.stack([lat_index, lon_index]).astype(jnp.int32)
    channels, devices = plan.channels, plan.devices
    owners = plan.deg_dev // OWNED
    block_rows = channels // plan.lon
    fine_table, fine_back, coarse_table, coarse_back = map(jnp.asarray, plan.fourier())
    exchanged = jax.ShapeDtypeStruct((devices * plan.rows, channels), LOW)
    rows_scratch = ((channels // LANES, devices * plan.rows, LANES), WIDE)
    owned_rows = jax.ShapeDtypeStruct((devices * 8, channels), LOW)
    gain_shape = jax.ShapeDtypeStruct((1, channels), WIDE)
    grid_low = [jax.ShapeDtypeStruct(grid.shape, LOW) for grid in (fine_grid, coarse_grid)]
    piece_shape = jax.ShapeDtypeStruct((2, OWNED, 2, block_rows, channels), LOW)
    own_shape = (OWNED, 2, channels, channels)
    collected_shape = (OWNED, 2, plan.lon, block_rows, channels)
    forward_scales = (
        2.0 * math.pi / plan.fine_lon * plan.fine_ka,
        2.0 * math.pi / plan.coarse_lon * plan.coarse_ka,
    )
    inverse_scales = (1.0 / plan.fine_ka, 1.0 / plan.coarse_ka)
    large = 16 if devices <= 32 else 56

    sent = kernel_call(
        functools.partial(front_kernel, plan=plan, scales=forward_scales),
        "front",
        exchanged,
        [rows_scratch],
        {3: of_lon(fine_table), 4: of_lon(coarse_table)},
        megabytes=60,
        cost=3,
    )(place, fine_grid, coarse_grid, norm_gains, fine_table, coarse_table)
    weights = for_owners(plan, spectral_weight, lon_index, owners)
    momentum = for_owners(plan, spectral_momentum, lon_index, owners)
    first_shifts, middle_shift = [1, *range(3, plan.lon)], 2
    sent, weights = together(sent, weights)
    spectrum = exchange(sent, BOTH, devices)
    for shift in first_shifts:
        weights[shift] = shifted(weights[shift], shift, plan.lon)
    weighted, doubled = legendre_tables(plan, lat_index, lon_index)
    hidden_low = hidden_weight.astype(LOW)

    coeffs, weights, momentum = together(wide_dot(weighted, spectrum).astype(LOW), weights, momentum)
    held = exchange(coeffs, BOTH, devices)
    weights[middle_shift] = shifted(weights[middle_shift], middle_shift, plan.lon)
    mixed, weights = kernel_call(
        mix_kernel, "mix", (owned_rows, jax.ShapeDtypeStruct(collected_shape, LOW))
    )(place, held, *weights)
    mixed, momentum = together(mixed, momentum)
    mixed = exchange(mixed, BOTH, devices)
    for shift in first_shifts:
        momentum[shift] = shifted(momentum[shift], shift, plan.lon)
    values, momentum = together(wide_dot(doubled, mixed, ((0,), (0,))).astype(LOW), momentum)
    values, momentum = together(values, momentum)
    values = exchange(values, BOTH, devices)
    momentum[middle_shift] = shifted(momentum[middle_shift], middle_shift, plan.lon)

    parts = plan.lat if plan.lat <= 8 else 1
    hidden_piece = jax.ShapeDtypeStruct(
        (2 * channels // parts, hidden_weight.shape[2]), LOW if parts > 1 else WIDE
    )
    fine_out, coarse_out, fine_left, coarse_left, sent, gain_second, *pieces = kernel_call(
        functools.partial(middle_kernel, plan=plan, scales=inverse_scales),
        "middle",
        (*grid_low, *grid_low, exchanged, gain_shape, *[hidden_piece] * parts),
        [rows_scratch, ((2 * channels, hidden_weight.shape[2]), WIDE)],
        {
            8: of_lon(fine_table),
            9: of_lon(coarse_table),
            10: of_lon(fine_back),
            11: of_lon(coarse_back),
        },
        megabytes=60,
        cost=10,
    )(
        place, fine_grid, coarse_grid, fine_cotangent, coarse_cotangent, values, norm_gains,
        hidden_low[0], hidden_low[1], fine_table, coarse_table, fine_back, coarse_back,
    )
    sent, momentum = together(sent, momentum)
    spectrum = exchange(sent, BOTH, devices)
    if parts > 1:
        for shift in range(1, parts):
            pieces[shift] = shifted(pieces[shift], shift, parts, "lat")
    coeffs = kernel_call(join_kernel, "join", owned_rows, megabytes=large)(
        place, doubled, spectrum, gain_second
    )
    mixed_grad = exchange(coeffs, BOTH, devices)
    if parts > 1:
        total = kernel_call(
            functools.partial(sum_kernel, axis=0), "sum_lat", hidden_piece, [((parts, *hidden_piece.shape), WIDE)]
        )(place, *pieces)
        totals = [total] + [shifted(total, shift, plan.lon) for shift in range(1, plan.lon)]
        mixed_grad, totals = together(mixed_grad, totals)
        total = kernel_call(
            functools.partial(sum_kernel, axis=1), "sum_lon", hidden_piece, [((plan.lon, *hidden_piece.shape), WIDE)]
        )(place, *totals)
    else:
        pieces = [lax.psum(pieces[0], BOTH)]

    coeffs, gain_second = kernel_call(
        mix_back_kernel, "mix_back", (owned_rows, gain_shape), megabytes=large, cost=2
    )(place, mixed_grad, held, weights, norm_gains)
    if parts > 1:
        coeffs, total = together(coeffs, total)
        pieces = [total] + [shifted(total, shift, parts, "lat") for shift in range(1, parts)]
    coeffs = exchange(coeffs, BOTH, devices)
    steps = kernel_call(
        complex_muon_kernel,
        "complex_muon",
        (piece_shape,) * plan.lon,
        [(collected_shape, LOW), (own_shape, WIDE), (own_shape, WIDE)],
        megabytes=60,
        cost=10,
    )(place, mixed_grad, held, *momentum)
    steps = [steps[0]] + [shifted(steps[shift], shift, plan.lon) for shift in range(1, plan.lon)]
    gains_shape = jax.ShapeDtypeStruct(norm_gains.shape, WIDE)
    values, gains_total, gain_moment, gain_updated = kernel_call(
        spread_kernel, "spread", (exchanged, gains_shape, gains_shape, gains_shape), megabytes=large
    )(place, weighted, coeffs, gain_second, gain_momentum, norm_gains)
    pieces, _ = together(pieces, gains_total)
    values = exchange(values, BOTH, devices)
    hidden_wide = jax.ShapeDtypeStruct(hidden_weight.shape, WIDE)
    hidden_grad, hidden_moment, hidden_updated, hidden_copy = kernel_call(
        real_muon_kernel,
        "real_muon",
        (hidden_wide, hidden_wide, hidden_wide, jax.ShapeDtypeStruct(hidden_weight.shape, LOW)),
        [((parts, *hidden_piece.shape), WIDE)],
        megabytes=60,
        cost=9,
    )(place, hidden_momentum, hidden_weight, *pieces)
    fine_gradient, coarse_gradient = kernel_call(
        functools.partial(last_kernel, plan=plan, scales=forward_scales),
        "last",
        tuple(grid_low),
        [rows_scratch],
        {6: of_lon(fine_back), 7: of_lon(coarse_back)},
        megabytes=60,
        cost=4,
    )(place, fine_grid, coarse_grid, fine_left, coarse_left, values, norm_gains, fine_back, coarse_back)
    steps, _ = together(steps, fine_gradient)
    spectral_grad, spectral_moment, spectral_updated, spectral_copy = finish(
        place, spectral_momentum, spectral_weight, steps
    )

    return (
        fine_out,
        coarse_out,
        fine_gradient,
        coarse_gradient,
        spectral_grad,
        spectral_moment,
        spectral_updated,
        spectral_copy,
        hidden_grad,
        hidden_moment,
        hidden_updated,
        hidden_copy,
        gains_total,
        gain_moment,
        gain_updated,
    )


def solution(mesh):
    grid = P("lat", "lon", None)
    degree = P("lat", None, "lon", None)
    return jax.shard_map(
        body,
        mesh=mesh,
        in_specs=(grid,) * 4 + (degree,) * 2 + (P(),) * 4,
        out_specs=(grid,) * 4 + (degree,) * 4 + (P(),) * 7,
        check_vma=False,
    )
```

```python
import functools
import math

import jax
import jax.numpy as jnp
import ml_dtypes
import numpy as np
from jax import lax
from jax.experimental import pallas as pl
from jax.experimental.pallas import tpu as pltpu
from jax.sharding import PartitionSpec as P

OWNED = 2
RIDER = 3
LANES = 128
NORM_EPSILON = 1e-05
MOMENTUM_DECAY = 0.5
STEP_RATE = 0.6
GAIN_RATE = 0.2
POLY_FIRST = 3.4445
POLY_SECOND = -4.775
POLY_THIRD = 2.0315
BOTH = ("lat", "lon")
LOW = jnp.bfloat16
WIDE = jnp.float32


class Plan:
    def __init__(self, lat_count, lon_count, fine, coarse, weight):
        self.lat, self.lon = lat_count, lon_count
        self.devices = lat_count * lon_count
        self.tf, self.nf, self.channels = fine.shape
        self.tc, self.nc = coarse.shape[:2]
        self.deg_dev = weight.shape[0]
        self.degrees = self.deg_dev * lat_count
        self.half = self.degrees // 2
        self.fine_lat, self.coarse_lat = self.tf * lat_count, self.tc * lat_count
        self.fine_lon, self.coarse_lon = self.nf * lon_count, self.nc * lon_count
        self.rows = 3 * self.tf + 2 * self.tc
        self.fine_ka = math.sqrt(self.fine_lat * self.fine_lon / (4.0 * math.pi))
        self.coarse_ka = math.sqrt(self.coarse_lat * self.coarse_lon / (4.0 * math.pi))
        self.parts_lat = lat_count // 2

    def orders(self, lat_index, lon_index):
        part = lat_index // self.parts_lat
        trio = (lat_index % self.parts_lat) * self.lon + lon_index
        even = 1 - trio % 2
        pair = trio // 2
        low, high = 3 * pair, self.half + 3 * pair
        first = high + 2 * (1 - even)
        second = even * (high + 1) + (1 - even) * (low + 1)
        third = even * low + (1 - even) * (low + 2)
        return (first, second, third), part, even

    def fourier(self):
        fine = np.zeros((self.lon, 3, self.devices, self.nf))
        coarse = np.zeros((self.lon, 2, self.devices, self.nc))

        def fill(out, order, part, total):
            position = np.arange(total)
            angle = 2.0 * np.pi / total * (position * order % total)
            line = -np.sin(angle) if part else np.cos(angle)
            out[...] = line.reshape(self.lon, -1)

        for lat_index in range(self.lat):
            for lon_index in range(self.lon):
                device = lat_index * self.lon + lon_index
                orders, part, even = self.orders(lat_index, lon_index)
                for row in range(3):
                    fill(fine[:, row, device], orders[row], part, self.fine_lon)
                for row in range(1 + even):
                    fill(coarse[:, row, device], orders[row] - self.half, part, self.coarse_lon)
        results = []
        for table in (fine, coarse):
            flat = table.reshape(self.lon, -1, table.shape[-1]).astype(ml_dtypes.bfloat16)
            results += [flat, np.swapaxes(flat, 1, 2)]
        return results


def legendre_kernel(columns, weighted_out, doubled_out, slope, back, start, *, degrees, half):
    order, cosine, quadrature, doubling = (columns[row : row + 1, :] for row in range(4))
    used, diagonal = columns[4:5, :], columns[5:6, :]
    degree = lax.broadcasted_iota(jnp.int32, slope.shape, 0).astype(WIDE)

    def factor(at):
        square = at * at
        return jnp.sqrt(
            jnp.maximum(4.0 * square - 1.0, 1.0) / jnp.maximum(square - order * order, 1.0)
        )

    now = factor(degree)
    running = (degree > order) & (degree < used)
    slope[...] = jnp.where(running, now * cosine, 0.0)
    back[...] = jnp.where(running, now / factor(degree - 1.0), 0.0)
    start[...] = jnp.where((degree == order) & (degree < used), diagonal, 0.0)

    def step(block, carried):
        latest, earlier = carried
        base = pl.multiple_of(block * 8, 8)
        slopes, backs, starts = (ref[pl.ds(base, 8), :] for ref in (slope, back, start))
        found = []
        for row in range(8):
            at = slice(row, row + 1)
            latest, earlier = slopes[at] * latest - backs[at] * earlier + starts[at], latest
            found.append(latest)
        start[pl.ds(base, 8), :] = jnp.concatenate(found, axis=0)
        return latest, earlier

    zero = jnp.zeros_like(order)
    lax.fori_loop(0, degrees // 8, step, (zero, zero))
    plain = start[...]
    weighted_out[...] = (quadrature * plain).astype(LOW)
    doubled_out[...] = (doubling * plain.astype(LOW).astype(WIDE)).astype(LOW)


def legendre_tables(plan, lat_index, lon_index):
    orders, part, even = plan.orders(lat_index, lon_index)
    fine_kind = np.repeat(np.arange(3), plan.tf)
    coarse_kind = np.repeat(np.arange(2), plan.tc)
    kind = np.tile(np.concatenate([fine_kind, coarse_kind]), plan.devices)
    is_fine = np.tile(np.arange(plan.rows) < 3 * plan.tf, plan.devices)
    lat_of = np.repeat(np.arange(plan.devices) // plan.lon, plan.rows)
    fine_lat = lat_of * plan.tf + np.tile(np.arange(plan.rows) % plan.tf, plan.devices)
    coarse_lat = lat_of * plan.tc + np.tile(np.arange(plan.rows) % plan.tc, plan.devices)
    position = np.where(is_fine, fine_lat, coarse_lat)
    count = np.where(is_fine, plan.fine_lat, plan.coarse_lat)
    colatitude = np.pi * (position + 0.5) / count
    own = jnp.where(kind == 0, orders[0], jnp.where(kind == 1, orders[1], orders[2]))
    own = jnp.where(is_fine, own, own - plan.half)
    held = own >= 0
    own = jnp.maximum(own, 0)
    span = np.arange(plan.degrees)
    norms = np.array(
        [
            0.5
            * (
                math.log((2.0 * m + 1.0) / (4.0 * math.pi))
                + math.lgamma(m + 0.5)
                - math.lgamma(m + 1.0)
                - 0.5 * math.log(math.pi)
            )
            for m in span
        ],
        np.float32,
    )
    norm = jnp.sum(jnp.where(own[None, :] == span[:, None], norms[:, None], 0.0), axis=0)
    log_sine = np.log(np.sin(colatitude)).astype(np.float32)
    diagonal = jnp.where(held, jnp.exp(norm + own.astype(WIDE) * log_sine), 0.0)
    columns = jnp.stack(
        [
            own.astype(WIDE),
            jnp.asarray(np.cos(colatitude).astype(np.float32)),
            jnp.asarray((np.pi / count * np.sin(colatitude)).astype(np.float32)),
            jnp.where(own == 0, 1.0, 2.0),
            jnp.asarray(np.where(is_fine, plan.degrees, plan.half).astype(np.float32)),
            diagonal,
        ]
    )
    shape = (plan.degrees, plan.devices * plan.rows)
    compact = pl.pallas_call(
        functools.partial(legendre_kernel, degrees=plan.degrees, half=plan.half),
        out_shape=(jax.ShapeDtypeStruct(shape, LOW),) * 2,
        scratch_shapes=[pltpu.VMEM(shape, WIDE)] * 3,
        compiler_params=pltpu.CompilerParams(vmem_limit_bytes=(16 if shape[1] <= 512 else 56) << 20),
        name="legendre",
    )(columns)
    chosen = kind[None, :] == np.arange(4)[:, None]
    pairs = plan.deg_dev // OWNED
    results = []
    for table in compact:
        spread = table.reshape(plan.lat, pairs, OWNED, 1, shape[1])
        spread = jnp.where(chosen, spread, jnp.zeros_like(spread))
        spread = jnp.pad(spread, ((0, 0), (0, plan.lon - pairs), (0, 0), (0, 0), (0, 0)))
        results.append(spread.reshape(plan.devices * 8, shape[1]))
    return results


def wide_dot(left, right, contract=((1,), (0,))):
    return lax.dot_general(left, right, (contract, ((), ())), preferred_element_type=WIDE)


def normalize(values):
    shifted = values - jnp.mean(values, axis=-1, keepdims=True)
    inverse = lax.rsqrt(jnp.mean(shifted * shifted, axis=-1, keepdims=True) + NORM_EPSILON)
    return shifted * inverse, inverse


def norm_back(grad, unit, inverse):
    return (
        grad
        - jnp.mean(grad, axis=-1, keepdims=True)
        - unit * jnp.mean(grad * unit, axis=-1, keepdims=True)
    ) * inverse


def kernel_call(kernel, name, out_shape, scratch=(), views=None, megabytes=16, cost=2):
    views = views or {}

    def run(place, *arrays):
        def spec(shape, at=None):
            if at in views:
                block, index = views[at]
                return pl.BlockSpec(block, lambda step, place: index(place))
            return pl.BlockSpec(tuple(shape), lambda step, place: (0,) * len(shape))

        outs = jax.tree.leaves(out_shape)
        found = pl.pallas_call(
            kernel,
            out_shape=outs,
            grid_spec=pltpu.PrefetchScalarGridSpec(
                num_scalar_prefetch=1,
                grid=(1,),
                in_specs=[spec(each.shape, at) for at, each in enumerate(arrays)],
                out_specs=[spec(each.shape) for each in outs],
                scratch_shapes=[pltpu.VMEM(*each) for each in scratch],
            ),
            compiler_params=pltpu.CompilerParams(vmem_limit_bytes=megabytes << 20),
            cost_estimate=estimate(cost),
            name=name,
        )(place, *arrays)
        return jax.tree.unflatten(jax.tree.structure(out_shape), found)

    return run


def estimate(microseconds):
    return pl.CostEstimate(
        flops=int(microseconds * 1.1e9), bytes_accessed=int(microseconds * 3e6), transcendentals=0
    )


def of_lon(table):
    return (None,) + table.shape[1:], lambda place: (place[1], 0, 0)


def cut(block, size):
    return pl.ds(pl.multiple_of(block * size, size), size)


class Blocks:
    def __init__(self, plan):
        self.plan = plan
        self.items = [(0, t) for t in range(plan.tf)] + [(1, t) for t in range(plan.tc)]

    def strides(self, grid, t):
        plan = self.plan
        starts = (
            [row * plan.tf + t for row in range(3)]
            if grid == 0
            else [3 * plan.tf + row * plan.tc + t for row in range(2)]
        )
        return [pl.ds(start, plan.devices, stride=plan.rows) for start in starts]

    def load(self, scratch, received):
        for lane in range(scratch.shape[0]):
            scratch[lane] = received[:, lane * LANES : (lane + 1) * LANES].astype(WIDE)

    def store(self, scratch, sent):
        for lane in range(scratch.shape[0]):
            sent[:, lane * LANES : (lane + 1) * LANES] = scratch[lane].astype(LOW)

    def put(self, scratch, grid, t, table, values, scale):
        summed = wide_dot(table, values) * scale
        for row, where in enumerate(self.strides(grid, t)):
            part = summed[row * self.plan.devices : (row + 1) * self.plan.devices]
            for lane in range(scratch.shape[0]):
                scratch[lane, where, :] = part[:, lane * LANES : (lane + 1) * LANES]

    def take(self, scratch, grid, t, table, scale):
        found = [
            jnp.concatenate([scratch[lane, where, :] for lane in range(scratch.shape[0])], axis=1)
            for where in self.strides(grid, t)
        ]
        values = jnp.concatenate(found, axis=0).astype(LOW)
        return (wide_dot(table, values) * scale).astype(LOW).astype(WIDE)


def front_kernel(place, fine, coarse, gains, table_fine, table_coarse, sent, scratch, *, plan, scales):
    blocks = Blocks(plan)
    grids, tables = (fine, coarse), (table_fine, table_coarse)
    for grid, t in blocks.items:
        unit, inverse = normalize(grids[grid][t].astype(WIDE))
        normed = (unit * gains[0:1, :]).astype(LOW)
        blocks.put(scratch, grid, t, tables[grid][...], normed, scales[grid])
    blocks.store(scratch, sent)


def middle_kernel(
    place, fine, coarse, fine_up, coarse_up, received, gains, first, second,
    table_fine, table_coarse, back_fine, back_coarse,
    fine_out, coarse_out, fine_left, coarse_left, sent, gain, *rest, plan, scales,
):
    *pieces, scratch, hidden = rest
    blocks = Blocks(plan)
    grids, ups, outs, lefts = (
        (fine, coarse), (fine_up, coarse_up), (fine_out, coarse_out), (fine_left, coarse_left)
    )
    tables, backs = (table_fine, table_coarse), (back_fine, back_coarse)
    root = math.sqrt(2.0 / math.pi)
    scaling = gains[1:2, :]
    first_low, second_low = first[...], second[...]
    first_sum = second_sum = gain_sum = None
    blocks.load(scratch, received)
    branches = [blocks.take(scratch, grid, t, backs[grid][...], scales[grid]) for grid, t in blocks.items]
    for (grid, t), branch in zip(blocks.items, branches):
        residual = grids[grid][t].astype(WIDE) + branch
        unit, inverse = normalize(residual)
        normed = (unit * scaling).astype(LOW)
        pre = wide_dot(normed, first_low)
        square = pre * pre
        inner = pre * (root + root * 0.044715 * square)
        gate = 0.5 + 0.5 * jnp.tanh(inner)
        active = (pre * gate).astype(LOW)
        outs[grid][t] = (residual + wide_dot(active, second_low, ((1,), (1,)))).astype(LOW)
        upstream = ups[grid][t]
        slope = gate + gate * (1.0 - gate) * (pre * (2.0 * root + 6.0 * root * 0.044715 * square))
        pre_grad = (wide_dot(upstream, second_low) * slope).astype(LOW)
        normed_grad = wide_dot(pre_grad, first_low, ((1,), (1,)))
        left = upstream.astype(WIDE) + norm_back(normed_grad * scaling, unit, inverse)
        left_low = left.astype(LOW)
        lefts[grid][t] = left_low
        blocks.put(scratch, grid, t, tables[grid][...], left_low, scales[grid])
        first_part = wide_dot(normed, pre_grad, ((0,), (0,)))
        second_part = wide_dot(upstream, active, ((0,), (0,)))
        gain_part = jnp.sum(normed_grad * unit, axis=0, keepdims=True)
        if first_sum is None:
            first_sum, second_sum, gain_sum = first_part, second_part, gain_part
        else:
            first_sum, second_sum, gain_sum = (
                first_sum + first_part, second_sum + second_part, gain_sum + gain_part
            )
    blocks.store(scratch, sent)
    gain[...] = gain_sum
    hidden[: plan.channels] = first_sum
    hidden[plan.channels :] = second_sum
    size = pieces[0].shape[0]
    for shift, piece in enumerate(pieces):
        block = (place[0] + shift) % len(pieces)
        piece[...] = hidden[cut(block, size), :].astype(piece.dtype)


def last_kernel(
    place, fine, coarse, fine_left, coarse_left, received, gains, back_fine, back_coarse,
    fine_out, coarse_out, scratch, *, plan, scales,
):
    blocks = Blocks(plan)
    grids, lefts, outs = (fine, coarse), (fine_left, coarse_left), (fine_out, coarse_out)
    backs = (back_fine, back_coarse)
    blocks.load(scratch, received)
    for grid, t in blocks.items:
        normed_grad = blocks.take(scratch, grid, t, backs[grid][...], scales[grid])
        unit, inverse = normalize(grids[grid][t].astype(WIDE))
        outs[grid][t] = (
            lefts[grid][t].astype(WIDE) + norm_back(normed_grad * gains[0:1, :], unit, inverse)
        ).astype(LOW)


def row_masks(count):
    slot = lax.broadcasted_iota(jnp.int32, (count, 1), 0) % 8
    return [(slot // 4 == owned) & (slot % 4 < RIDER) for owned in range(OWNED)], slot == RIDER


def mixing(rows, weights, masks, sign, contract):
    split = rows.shape[0] // 2
    top, bottom = None, None
    for owned in range(OWNED):
        chosen = jnp.where(masks[owned], rows, 0.0).astype(LOW)
        by_real = wide_dot(chosen, weights[owned, 0], contract)
        by_imag = wide_dot(chosen, weights[owned, 1], contract) * sign
        up = by_real[:split] - by_imag[split:]
        down = by_real[split:] + by_imag[:split]
        top, bottom = (up, down) if top is None else (top + up, bottom + down)
    return top, bottom


class Joined:
    def __init__(self, ref):
        self.ref = ref

    def __getitem__(self, at):
        value = self.ref[at[0], at[1]]
        return value.reshape(-1, value.shape[-1])


def collect(own, pieces, target):
    for shift, piece in enumerate(pieces):
        source = (own + len(pieces) - shift) % len(pieces)
        for owned in range(OWNED):
            for part in range(2):
                target[owned, part, source] = piece[owned, part]


def mix_kernel(place, held, *refs):
    *pieces, out, weights = refs
    collect(place[1], pieces, weights)
    split = held.shape[0] // 2
    masks, rider = row_masks(held.shape[0])
    top, bottom = mixing(held[...].astype(WIDE), Joined(weights), masks, 1.0, ((1,), (1,)))
    out[:split] = top.astype(LOW)
    out[split:] = bottom.astype(LOW)


def sum_kernel(place, *refs, axis):
    *pieces, out, ordered = refs
    for shift, piece in enumerate(pieces):
        ordered[(place[axis] + len(pieces) - shift) % len(pieces)] = piece[...].astype(WIDE)
    total = ordered[0]
    for at in range(1, len(pieces)):
        total = total + ordered[at]
    out[...] = total.astype(out.dtype)


def join_kernel(place, table, spectrum, gain, out):
    masks, rider = row_masks(table.shape[0])
    out[...] = jnp.where(rider, gain[...], wide_dot(table[...], spectrum[...])).astype(LOW)


def mix_back_kernel(place, received, held, weights, gains, out, gain):
    masks, rider = row_masks(held.shape[0])
    rows = received[...].astype(WIDE)
    gain[...] = jnp.sum(jnp.where(rider, rows, 0.0), axis=0, keepdims=True)
    top, bottom = mixing(rows, Joined(weights), masks, -1.0, ((1,), (0,)))
    back = jnp.concatenate([top, bottom], axis=0)
    gain_row = jnp.sum(back * held[...].astype(WIDE), axis=0, keepdims=True) / gains[0:1, :]
    out[...] = jnp.where(rider, gain_row, back).astype(LOW)


def spread_kernel(place, table, received, second, momentum, gains, out, total_out, moment_out, updated_out):
    masks, rider = row_masks(table.shape[0])
    out[...] = wide_dot(table[...], received[...], ((0,), (0,))).astype(LOW)
    first = jnp.sum(jnp.where(rider, received[...].astype(WIDE), 0.0), axis=0, keepdims=True)
    for row, total in enumerate((first, second[...])):
        at = slice(row, row + 1)
        total_out[at, :] = total
        moment = MOMENTUM_DECAY * momentum[at, :] + total
        moment_out[at, :] = moment
        scale = jnp.sqrt(jnp.mean(moment * moment, axis=-1, keepdims=True)) + 1e-06
        updated_out[at, :] = gains[at, :] - GAIN_RATE * moment / scale


def scatter(own, source, pieces, kind):
    size = pieces[0].shape[3]
    for shift, piece in enumerate(pieces):
        block = (own + shift) % len(pieces)
        for owned in range(OWNED):
            for part in range(2):
                piece[kind, owned, part] = source[owned, part, cut(block, size), :].astype(LOW)


def shift_gram(gram):
    size = gram.shape[0]
    unit = lax.broadcasted_iota(jnp.int32, gram.shape, 0) == lax.broadcasted_iota(jnp.int32, gram.shape, 1)
    level = jnp.sum(jnp.sum(jnp.where(unit, gram, 0.0), axis=1, keepdims=True), axis=0, keepdims=True) / size
    keep = POLY_FIRST + level * (POLY_SECOND + POLY_THIRD * level)
    return jnp.where(unit, gram - level, gram), keep, POLY_SECOND + 2.0 * POLY_THIRD * level


def beside(left, right):
    return jnp.concatenate([left, right], axis=1)


def below(top, bottom):
    return jnp.concatenate([top, bottom], axis=0)


def complex_rows(real, imag):
    return below(beside(real, -imag), beside(imag, real))


def complex_muon_kernel(place, mixed_grads, held, *refs):
    count = (len(refs) - 3) // 2
    sources, pieces, (momentum, grads, result) = refs[:count], refs[count : 2 * count], refs[2 * count :]
    collect(place[1], sources, momentum)
    masks, rider = row_masks(held.shape[0])
    split = held.shape[0] // 2
    coeffs, rows = held[...].astype(WIDE), mixed_grads[...].astype(WIDE)
    swapped = jnp.concatenate([rows[split:], -rows[:split]], axis=0).astype(LOW)
    for owned in range(OWNED):
        picked = jnp.where(masks[owned], coeffs, 0.0).astype(LOW)
        for part, side in enumerate((mixed_grads[...], swapped)):
            grads[owned, part] = wide_dot(side, picked, ((0,), (0,)))
    momentum = Joined(momentum)
    states = []
    for owned in range(OWNED):
        parts = [
            MOMENTUM_DECAY * momentum[owned, part].astype(WIDE) + grads[owned, part] for part in range(2)
        ]
        total = jnp.sum(parts[0] * parts[0]) + jnp.sum(parts[1] * parts[1])
        scale = 1.0 / (jnp.sqrt(total) + 1e-07)
        states.append([part * scale for part in parts])
    for iteration in range(5):
        for state in states:
            size = state[0].shape[0]
            real, imag = state[0].astype(LOW), state[1].astype(LOW)
            side = beside(real, imag)
            gram = wide_dot(below(side, beside(imag, -real)), side, ((1,), (1,)))
            rest, keep, lead = shift_gram(gram[:size])
            gram = below(rest, gram[size:])
            low = gram.astype(LOW)
            square = wide_dot(complex_rows(low[:size], low[size:]), low)
            poly = (lead * gram + POLY_THIRD * square).astype(LOW)
            change = wide_dot(complex_rows(poly[:size], poly[size:]), below(real, imag))
            state[0] = keep * state[0] + change[:size]
            state[1] = keep * state[1] + change[size:]
    for owned in range(OWNED):
        for part in range(2):
            result[owned, part] = states[owned][part]
    scatter(place[1], grads, pieces, 0)
    scatter(place[1], result, pieces, 1)


def real_muon_kernel(place, momentum, weight, *refs):
    *pieces, grad_out, moment_out, updated_out, low_out, gathered = refs
    for shift, piece in enumerate(pieces):
        gathered[(place[0] + len(pieces) - shift) % len(pieces)] = piece[...].astype(WIDE)
    whole = gathered[...].reshape(momentum.shape)
    currents = []
    for part in range(2):
        grad = whole[part]
        grad_out[part] = grad
        moment = MOMENTUM_DECAY * momentum[part] + grad
        moment_out[part] = moment
        currents.append(moment * (1.0 / (jnp.sqrt(jnp.sum(moment * moment)) + 1e-07)))
    for iteration in range(5):
        for part in range(2):
            current = currents[part]
            low = current.astype(LOW)
            rest, keep, lead = shift_gram(wide_dot(low, low, ((1,), (1,))))
            low_rest = rest.astype(LOW)
            poly = lead * rest + POLY_THIRD * wide_dot(low_rest, low_rest)
            currents[part] = keep * current + wide_dot(poly.astype(LOW), low)
    for part in range(2):
        updated = weight[part] - STEP_RATE * currents[part]
        updated_out[part] = updated
        low_out[part] = updated.astype(LOW)


def finish_kernel(place, momentum, weight, *refs, count):
    pieces, (grad_out, moment_out, updated_out, low_out) = refs[:count], refs[count:]
    shift = (place[1] + count - pl.program_id(0)) % count
    for at in range(count):

        @pl.when(shift == at)
        def _():
            grad = pieces[at][0].astype(WIDE)
            grad_out[...] = grad
            moment_out[...] = MOMENTUM_DECAY * momentum[...] + grad
            updated = weight[...] - STEP_RATE * pieces[at][1].astype(WIDE)
            updated_out[...] = updated
            low_out[...] = updated.astype(LOW)


def finish(place, momentum, weight, pieces):
    shape, count = weight.shape, len(pieces)
    block = pl.BlockSpec((OWNED,) + shape[1:], lambda owner, at: (owner, 0, 0, 0))
    whole = pl.BlockSpec(pieces[0].shape, lambda owner, at: (0, 0, 0, 0, 0))
    return pl.pallas_call(
        functools.partial(finish_kernel, count=count),
        out_shape=[jax.ShapeDtypeStruct(shape, dtype) for dtype in (WIDE, WIDE, WIDE, LOW)],
        grid_spec=pltpu.PrefetchScalarGridSpec(
            num_scalar_prefetch=1,
            grid=(shape[0] // OWNED,),
            in_specs=[block] * 2 + [whole] * count,
            out_specs=[block] * 4,
        ),
        compiler_params=pltpu.CompilerParams(vmem_limit_bytes=16 << 20),
        cost_estimate=estimate(6),
        name="finish",
    )(place, momentum, weight, *pieces)


def exchange(rows, axes, count):
    block = rows.reshape((count, -1) + rows.shape[1:])
    return lax.all_to_all(block, axes, 0, 0, tiled=True).reshape(rows.shape)


def shifted(piece, shift, count, axis="lon"):
    return lax.ppermute(piece, axis, [(source, (source + shift) % count) for source in range(count)])


def for_owners(plan, rows, lon_index, owners):
    pieces = []
    for shift in range(plan.lon):
        owner = jnp.minimum((lon_index + shift) % plan.lon, owners - 1)
        pieces.append(lax.dynamic_slice_in_dim(rows, owner * OWNED, OWNED, 0).astype(LOW))
    return pieces


def together(*values):
    return lax.optimization_barrier(values)


def body(
    fine_grid,
    coarse_grid,
    fine_cotangent,
    coarse_cotangent,
    spectral_weight,
    spectral_momentum,
    hidden_weight,
    hidden_momentum,
    norm_gains,
    gain_momentum,
):
    plan = Plan(lax.axis_size("lat"), lax.axis_size("lon"), fine_grid, coarse_grid, spectral_weight)
    lat_index, lon_index = lax.axis_index("lat"), lax.axis_index("lon")
    place = jnp.stack([lat_index, lon_index]).astype(jnp.int32)
    channels, devices = plan.channels, plan.devices
    owners = plan.deg_dev // OWNED
    block_rows = channels // plan.lon
    fine_table, fine_back, coarse_table, coarse_back = map(jnp.asarray, plan.fourier())
    exchanged = jax.ShapeDtypeStruct((devices * plan.rows, channels), LOW)
    rows_scratch = ((channels // LANES, devices * plan.rows, LANES), WIDE)
    owned_rows = jax.ShapeDtypeStruct((devices * 8, channels), LOW)
    gain_shape = jax.ShapeDtypeStruct((1, channels), WIDE)
    grid_low = [jax.ShapeDtypeStruct(grid.shape, LOW) for grid in (fine_grid, coarse_grid)]
    piece_shape = jax.ShapeDtypeStruct((2, OWNED, 2, block_rows, channels), LOW)
    own_shape = (OWNED, 2, channels, channels)
    collected_shape = (OWNED, 2, plan.lon, block_rows, channels)
    forward_scales = (
        2.0 * math.pi / plan.fine_lon * plan.fine_ka,
        2.0 * math.pi / plan.coarse_lon * plan.coarse_ka,
    )
    inverse_scales = (1.0 / plan.fine_ka, 1.0 / plan.coarse_ka)
    large = 16 if devices <= 32 else 56

    sent = kernel_call(
        functools.partial(front_kernel, plan=plan, scales=forward_scales),
        "front",
        exchanged,
        [rows_scratch],
        {3: of_lon(fine_table), 4: of_lon(coarse_table)},
        megabytes=24,
        cost=3,
    )(place, fine_grid, coarse_grid, norm_gains, fine_table, coarse_table)
    weights = for_owners(plan, spectral_weight, lon_index, owners)
    momentum = for_owners(plan, spectral_momentum, lon_index, owners)
    first_shifts, middle_shift = [1, *range(3, plan.lon)], 2
    sent, weights = together(sent, weights)
    spectrum = exchange(sent, BOTH, devices)
    for shift in first_shifts:
        weights[shift] = shifted(weights[shift], shift, plan.lon)
    weighted, doubled = legendre_tables(plan, lat_index, lon_index)
    hidden_low = hidden_weight.astype(LOW)

    coeffs, weights, momentum = together(wide_dot(weighted, spectrum).astype(LOW), weights, momentum)
    held = exchange(coeffs, BOTH, devices)
    weights[middle_shift] = shifted(weights[middle_shift], middle_shift, plan.lon)
    mixed, weights = kernel_call(
        mix_kernel, "mix", (owned_rows, jax.ShapeDtypeStruct(collected_shape, LOW))
    )(place, held, *weights)
    mixed, momentum = together(mixed, momentum)
    mixed = exchange(mixed, BOTH, devices)
    for shift in first_shifts:
        momentum[shift] = shifted(momentum[shift], shift, plan.lon)
    values, momentum = together(wide_dot(doubled, mixed, ((0,), (0,))).astype(LOW), momentum)
    values = exchange(values, BOTH, devices)
    values, momentum = together(values, momentum)
    momentum[middle_shift] = shifted(momentum[middle_shift], middle_shift, plan.lon)

    parts = plan.lat if plan.lat <= 8 else 1
    hidden_piece = jax.ShapeDtypeStruct(
        (2 * channels // parts, hidden_weight.shape[2]), LOW if parts > 1 else WIDE
    )
    fine_out, coarse_out, fine_left, coarse_left, sent, gain_second, *pieces = kernel_call(
        functools.partial(middle_kernel, plan=plan, scales=inverse_scales),
        "middle",
        (*grid_low, *grid_low, exchanged, gain_shape, *[hidden_piece] * parts),
        [rows_scratch, ((2 * channels, hidden_weight.shape[2]), WIDE)],
        {
            8: of_lon(fine_table),
            9: of_lon(coarse_table),
            10: of_lon(fine_back),
            11: of_lon(coarse_back),
        },
        megabytes=60,
        cost=10,
    )(
        place, fine_grid, coarse_grid, fine_cotangent, coarse_cotangent, values, norm_gains,
        hidden_low[0], hidden_low[1], fine_table, coarse_table, fine_back, coarse_back,
    )
    sent, momentum = together(sent, momentum)
    spectrum = exchange(sent, BOTH, devices)
    if parts > 1:
        for shift in range(1, parts):
            pieces[shift] = shifted(pieces[shift], shift, parts, "lat")
    coeffs = kernel_call(join_kernel, "join", owned_rows, megabytes=large)(
        place, doubled, spectrum, gain_second
    )
    mixed_grad = exchange(coeffs, BOTH, devices)
    if parts > 1:
        total = kernel_call(
            functools.partial(sum_kernel, axis=0), "sum_lat", hidden_piece, [((parts, *hidden_piece.shape), WIDE)]
        )(place, *pieces)
        totals = [total] + [shifted(total, shift, plan.lon) for shift in range(1, plan.lon)]
    else:
        pieces = [lax.psum(pieces[0], BOTH)]

    coeffs, gain_second = kernel_call(
        mix_back_kernel, "mix_back", (owned_rows, gain_shape), megabytes=large, cost=2
    )(place, mixed_grad, held, weights, norm_gains)
    coeffs = exchange(coeffs, BOTH, devices)
    steps = kernel_call(
        complex_muon_kernel,
        "complex_muon",
        (piece_shape,) * plan.lon,
        [(collected_shape, LOW), (own_shape, WIDE), (own_shape, WIDE)],
        megabytes=32,
        cost=10,
    )(place, mixed_grad, held, *momentum)
    coeffs, steps = together(coeffs, steps)
    steps = [steps[0]] + [shifted(steps[shift], shift, plan.lon) for shift in range(1, plan.lon)]
    gains_shape = jax.ShapeDtypeStruct(norm_gains.shape, WIDE)
    values, gains_total, gain_moment, gain_updated = kernel_call(
        spread_kernel, "spread", (exchanged, gains_shape, gains_shape, gains_shape), megabytes=large
    )(place, weighted, coeffs, gain_second, gain_momentum, norm_gains)
    if parts > 1:
        totals, _ = together(totals, gain_second)
        total = kernel_call(
            functools.partial(sum_kernel, axis=1), "sum_lon", hidden_piece, [((plan.lon, *hidden_piece.shape), WIDE)]
        )(place, *totals)
        total, _ = together(total, gains_total)
        pieces = [total] + [shifted(total, shift, parts, "lat") for shift in range(1, parts)]
    else:
        pieces, _ = together(pieces, gains_total)
    values = exchange(values, BOTH, devices)
    hidden_wide = jax.ShapeDtypeStruct(hidden_weight.shape, WIDE)
    hidden_grad, hidden_moment, hidden_updated, hidden_copy = kernel_call(
        real_muon_kernel,
        "real_muon",
        (hidden_wide, hidden_wide, hidden_wide, jax.ShapeDtypeStruct(hidden_weight.shape, LOW)),
        [((parts, *hidden_piece.shape), WIDE)],
        megabytes=60,
        cost=3,
    )(place, hidden_momentum, hidden_weight, *pieces)
    fine_gradient, coarse_gradient = kernel_call(
        functools.partial(last_kernel, plan=plan, scales=forward_scales),
        "last",
        tuple(grid_low),
        [rows_scratch],
        {6: of_lon(fine_back), 7: of_lon(coarse_back)},
        megabytes=60,
        cost=4,
    )(place, fine_grid, coarse_grid, fine_left, coarse_left, values, norm_gains, fine_back, coarse_back)
    steps, _ = together(steps, fine_gradient)
    spectral_grad, spectral_moment, spectral_updated, spectral_copy = finish(
        place, spectral_momentum, spectral_weight, steps
    )

    return (
        fine_out,
        coarse_out,
        fine_gradient,
        coarse_gradient,
        spectral_grad,
        spectral_moment,
        spectral_updated,
        spectral_copy,
        hidden_grad,
        hidden_moment,
        hidden_updated,
        hidden_copy,
        gains_total,
        gain_moment,
        gain_updated,
    )


def solution(mesh):
    grid = P("lat", "lon", None)
    degree = P("lat", None, "lon", None)
    return jax.shard_map(
        body,
        mesh=mesh,
        in_specs=(grid,) * 4 + (degree,) * 2 + (P(),) * 4,
        out_specs=(grid,) * 4 + (degree,) * 4 + (P(),) * 7,
        check_vma=False,
    )
```

```python
import functools
import math

import jax
import jax.numpy as jnp
import ml_dtypes
import numpy as np
from jax import lax
from jax.experimental import pallas as pl
from jax.experimental.pallas import tpu as pltpu
from jax.sharding import PartitionSpec as P

OWNED = 2
RIDER = 3
LANES = 128
NORM_EPSILON = 1e-05
MOMENTUM_DECAY = 0.5
STEP_RATE = 0.6
GAIN_RATE = 0.2
POLY_FIRST = 3.4445
POLY_SECOND = -4.775
POLY_THIRD = 2.0315
BOTH = ("lat", "lon")
LOW = jnp.bfloat16
WIDE = jnp.float32


class Plan:
    def __init__(self, lat_count, lon_count, fine, coarse, weight):
        self.lat, self.lon = lat_count, lon_count
        self.devices = lat_count * lon_count
        self.tf, self.nf, self.channels = fine.shape
        self.tc, self.nc = coarse.shape[:2]
        self.deg_dev = weight.shape[0]
        self.degrees = self.deg_dev * lat_count
        self.half = self.degrees // 2
        self.fine_lat, self.coarse_lat = self.tf * lat_count, self.tc * lat_count
        self.fine_lon, self.coarse_lon = self.nf * lon_count, self.nc * lon_count
        self.rows = 3 * self.tf + 2 * self.tc
        self.fine_ka = math.sqrt(self.fine_lat * self.fine_lon / (4.0 * math.pi))
        self.coarse_ka = math.sqrt(self.coarse_lat * self.coarse_lon / (4.0 * math.pi))
        self.parts_lat = lat_count // 2

    def orders(self, lat_index, lon_index):
        part = lat_index // self.parts_lat
        trio = (lat_index % self.parts_lat) * self.lon + lon_index
        even = 1 - trio % 2
        pair = trio // 2
        low, high = 3 * pair, self.half + 3 * pair
        first = high + 2 * (1 - even)
        second = even * (high + 1) + (1 - even) * (low + 1)
        third = even * low + (1 - even) * (low + 2)
        return (first, second, third), part, even

    def fourier(self):
        fine = np.zeros((self.lon, 3, self.devices, self.nf))
        coarse = np.zeros((self.lon, 2, self.devices, self.nc))

        def fill(out, order, part, total):
            position = np.arange(total)
            angle = 2.0 * np.pi / total * (position * order % total)
            line = -np.sin(angle) if part else np.cos(angle)
            out[...] = line.reshape(self.lon, -1)

        for lat_index in range(self.lat):
            for lon_index in range(self.lon):
                device = lat_index * self.lon + lon_index
                orders, part, even = self.orders(lat_index, lon_index)
                for row in range(3):
                    fill(fine[:, row, device], orders[row], part, self.fine_lon)
                for row in range(1 + even):
                    fill(coarse[:, row, device], orders[row] - self.half, part, self.coarse_lon)
        results = []
        for table in (fine, coarse):
            flat = table.reshape(self.lon, -1, table.shape[-1]).astype(ml_dtypes.bfloat16)
            results += [flat, np.swapaxes(flat, 1, 2)]
        return results


def legendre_kernel(columns, weighted_out, doubled_out, slope, back, start, *, degrees, half):
    order, cosine, quadrature, doubling = (columns[row : row + 1, :] for row in range(4))
    used, diagonal = columns[4:5, :], columns[5:6, :]
    degree = lax.broadcasted_iota(jnp.int32, slope.shape, 0).astype(WIDE)

    def factor(at):
        square = at * at
        return jnp.sqrt(
            jnp.maximum(4.0 * square - 1.0, 1.0) / jnp.maximum(square - order * order, 1.0)
        )

    now = factor(degree)
    running = (degree > order) & (degree < used)
    slope[...] = jnp.where(running, now * cosine, 0.0)
    back[...] = jnp.where(running, now / factor(degree - 1.0), 0.0)
    start[...] = jnp.where((degree == order) & (degree < used), diagonal, 0.0)

    def step(block, carried):
        latest, earlier = carried
        base = pl.multiple_of(block * 8, 8)
        slopes, backs, starts = (ref[pl.ds(base, 8), :] for ref in (slope, back, start))
        found = []
        for row in range(8):
            at = slice(row, row + 1)
            latest, earlier = slopes[at] * latest - backs[at] * earlier + starts[at], latest
            found.append(latest)
        start[pl.ds(base, 8), :] = jnp.concatenate(found, axis=0)
        return latest, earlier

    zero = jnp.zeros_like(order)
    lax.fori_loop(0, degrees // 8, step, (zero, zero))
    plain = start[...]
    weighted_out[...] = (quadrature * plain).astype(LOW)
    doubled_out[...] = (doubling * plain.astype(LOW).astype(WIDE)).astype(LOW)


def legendre_tables(plan, lat_index, lon_index):
    orders, part, even = plan.orders(lat_index, lon_index)
    fine_kind = np.repeat(np.arange(3), plan.tf)
    coarse_kind = np.repeat(np.arange(2), plan.tc)
    kind = np.tile(np.concatenate([fine_kind, coarse_kind]), plan.devices)
    is_fine = np.tile(np.arange(plan.rows) < 3 * plan.tf, plan.devices)
    lat_of = np.repeat(np.arange(plan.devices) // plan.lon, plan.rows)
    fine_lat = lat_of * plan.tf + np.tile(np.arange(plan.rows) % plan.tf, plan.devices)
    coarse_lat = lat_of * plan.tc + np.tile(np.arange(plan.rows) % plan.tc, plan.devices)
    position = np.where(is_fine, fine_lat, coarse_lat)
    count = np.where(is_fine, plan.fine_lat, plan.coarse_lat)
    colatitude = np.pi * (position + 0.5) / count
    own = jnp.where(kind == 0, orders[0], jnp.where(kind == 1, orders[1], orders[2]))
    own = jnp.where(is_fine, own, own - plan.half)
    held = own >= 0
    own = jnp.maximum(own, 0)
    span = np.arange(plan.degrees)
    norms = np.array(
        [
            0.5
            * (
                math.log((2.0 * m + 1.0) / (4.0 * math.pi))
                + math.lgamma(m + 0.5)
                - math.lgamma(m + 1.0)
                - 0.5 * math.log(math.pi)
            )
            for m in span
        ],
        np.float32,
    )
    norm = jnp.sum(jnp.where(own[None, :] == span[:, None], norms[:, None], 0.0), axis=0)
    log_sine = np.log(np.sin(colatitude)).astype(np.float32)
    diagonal = jnp.where(held, jnp.exp(norm + own.astype(WIDE) * log_sine), 0.0)
    columns = jnp.stack(
        [
            own.astype(WIDE),
            jnp.asarray(np.cos(colatitude).astype(np.float32)),
            jnp.asarray((np.pi / count * np.sin(colatitude)).astype(np.float32)),
            jnp.where(own == 0, 1.0, 2.0),
            jnp.asarray(np.where(is_fine, plan.degrees, plan.half).astype(np.float32)),
            diagonal,
        ]
    )
    shape = (plan.degrees, plan.devices * plan.rows)
    compact = pl.pallas_call(
        functools.partial(legendre_kernel, degrees=plan.degrees, half=plan.half),
        out_shape=(jax.ShapeDtypeStruct(shape, LOW),) * 2,
        scratch_shapes=[pltpu.VMEM(shape, WIDE)] * 3,
        compiler_params=pltpu.CompilerParams(vmem_limit_bytes=(16 if shape[1] <= 512 else 56) << 20),
        name="legendre",
    )(columns)
    chosen = kind[None, :] == np.arange(4)[:, None]
    pairs = plan.deg_dev // OWNED
    results = []
    for table in compact:
        spread = table.reshape(plan.lat, pairs, OWNED, 1, shape[1])
        spread = jnp.where(chosen, spread, jnp.zeros_like(spread))
        spread = jnp.pad(spread, ((0, 0), (0, plan.lon - pairs), (0, 0), (0, 0), (0, 0)))
        results.append(spread.reshape(plan.devices * 8, shape[1]))
    return results


def wide_dot(left, right, contract=((1,), (0,))):
    return lax.dot_general(left, right, (contract, ((), ())), preferred_element_type=WIDE)


def normalize(values):
    shifted = values - jnp.mean(values, axis=-1, keepdims=True)
    inverse = lax.rsqrt(jnp.mean(shifted * shifted, axis=-1, keepdims=True) + NORM_EPSILON)
    return shifted * inverse, inverse


def norm_back(grad, unit, inverse):
    return (
        grad
        - jnp.mean(grad, axis=-1, keepdims=True)
        - unit * jnp.mean(grad * unit, axis=-1, keepdims=True)
    ) * inverse


def kernel_call(kernel, name, out_shape, scratch=(), views=None, megabytes=16, cost=2):
    views = views or {}

    def run(place, *arrays):
        def spec(shape, at=None):
            if at in views:
                block, index = views[at]
                return pl.BlockSpec(block, lambda step, place: index(place))
            return pl.BlockSpec(tuple(shape), lambda step, place: (0,) * len(shape))

        outs = jax.tree.leaves(out_shape)
        found = pl.pallas_call(
            kernel,
            out_shape=outs,
            grid_spec=pltpu.PrefetchScalarGridSpec(
                num_scalar_prefetch=1,
                grid=(1,),
                in_specs=[spec(each.shape, at) for at, each in enumerate(arrays)],
                out_specs=[spec(each.shape) for each in outs],
                scratch_shapes=[pltpu.VMEM(*each) for each in scratch],
            ),
            compiler_params=pltpu.CompilerParams(vmem_limit_bytes=megabytes << 20),
            cost_estimate=estimate(cost),
            name=name,
        )(place, *arrays)
        return jax.tree.unflatten(jax.tree.structure(out_shape), found)

    return run


def estimate(microseconds):
    return pl.CostEstimate(
        flops=int(microseconds * 1.1e9), bytes_accessed=int(microseconds * 3e6), transcendentals=0
    )


def of_lon(table):
    return (None,) + table.shape[1:], lambda place: (place[1], 0, 0)


def cut(block, size):
    return pl.ds(pl.multiple_of(block * size, size), size)


class Blocks:
    def __init__(self, plan):
        self.plan = plan
        self.items = [(0, t) for t in range(plan.tf)] + [(1, t) for t in range(plan.tc)]

    def strides(self, grid, t):
        plan = self.plan
        starts = (
            [row * plan.tf + t for row in range(3)]
            if grid == 0
            else [3 * plan.tf + row * plan.tc + t for row in range(2)]
        )
        return [pl.ds(start, plan.devices, stride=plan.rows) for start in starts]

    def read(self, ref, grid, t):
        return ref[t] if grid == 0 else ref[:, t, :]

    def write(self, ref, grid, t, value):
        if grid == 0:
            ref[t] = value
        else:
            ref[:, t, :] = value

    def load(self, scratch, received):
        for lane in range(scratch.shape[0]):
            scratch[lane] = received[:, lane * LANES : (lane + 1) * LANES].astype(WIDE)

    def store(self, scratch, sent):
        for lane in range(scratch.shape[0]):
            sent[:, lane * LANES : (lane + 1) * LANES] = scratch[lane].astype(LOW)

    def put(self, scratch, grid, t, table, values, scale):
        summed = wide_dot(table, values) * scale
        for row, where in enumerate(self.strides(grid, t)):
            part = summed[row * self.plan.devices : (row + 1) * self.plan.devices]
            for lane in range(scratch.shape[0]):
                scratch[lane, where, :] = part[:, lane * LANES : (lane + 1) * LANES]

    def take(self, scratch, grid, t, table, scale):
        found = [
            jnp.concatenate([scratch[lane, where, :] for lane in range(scratch.shape[0])], axis=1)
            for where in self.strides(grid, t)
        ]
        values = jnp.concatenate(found, axis=0).astype(LOW)
        return (wide_dot(table, values) * scale).astype(LOW).astype(WIDE)


def front_kernel(place, fine, coarse, gains, table_fine, table_coarse, sent, scratch, *, plan, scales):
    blocks = Blocks(plan)
    grids, tables = (fine, coarse), (table_fine, table_coarse)
    for grid, t in blocks.items:
        unit, inverse = normalize(blocks.read(grids[grid], grid, t).astype(WIDE))
        normed = (unit * gains[0:1, :]).astype(LOW)
        blocks.put(scratch, grid, t, tables[grid][...], normed, scales[grid])
    blocks.store(scratch, sent)


def middle_kernel(
    place, fine, coarse, fine_up, coarse_up, received, gains, first, second,
    table_fine, table_coarse, back_fine, back_coarse,
    fine_out, coarse_out, fine_left, coarse_left, sent, gain, *rest, plan, scales,
):
    *pieces, scratch, hidden = rest
    blocks = Blocks(plan)
    grids, ups, outs, lefts = (
        (fine, coarse), (fine_up, coarse_up), (fine_out, coarse_out), (fine_left, coarse_left)
    )
    tables, backs = (table_fine, table_coarse), (back_fine, back_coarse)
    root = math.sqrt(2.0 / math.pi)
    scaling = gains[1:2, :]
    first_low, second_low = first[...], second[...]
    first_sum = second_sum = gain_sum = None
    blocks.load(scratch, received)
    branches = [blocks.take(scratch, grid, t, backs[grid][...], scales[grid]) for grid, t in blocks.items]
    for (grid, t), branch in zip(blocks.items, branches):
        residual = blocks.read(grids[grid], grid, t).astype(WIDE) + branch
        unit, inverse = normalize(residual)
        normed = (unit * scaling).astype(LOW)
        pre = wide_dot(normed, first_low)
        square = pre * pre
        inner = pre * (root + root * 0.044715 * square)
        gate = 0.5 + 0.5 * jnp.tanh(inner)
        active = (pre * gate).astype(LOW)
        output = residual + wide_dot(active, second_low, ((1,), (1,)))
        blocks.write(outs[grid], grid, t, output.astype(LOW))
        upstream = blocks.read(ups[grid], grid, t)
        slope = gate + gate * (1.0 - gate) * (pre * (2.0 * root + 6.0 * root * 0.044715 * square))
        pre_grad = (wide_dot(upstream, second_low) * slope).astype(LOW)
        normed_grad = wide_dot(pre_grad, first_low, ((1,), (1,)))
        left = upstream.astype(WIDE) + norm_back(normed_grad * scaling, unit, inverse)
        left_low = left.astype(LOW)
        lefts[grid][t] = left_low
        blocks.put(scratch, grid, t, tables[grid][...], left_low, scales[grid])
        first_part = wide_dot(normed, pre_grad, ((0,), (0,)))
        second_part = wide_dot(upstream, active, ((0,), (0,)))
        gain_part = jnp.sum(normed_grad * unit, axis=0, keepdims=True)
        if first_sum is None:
            first_sum, second_sum, gain_sum = first_part, second_part, gain_part
        else:
            first_sum, second_sum, gain_sum = (
                first_sum + first_part, second_sum + second_part, gain_sum + gain_part
            )
    blocks.store(scratch, sent)
    gain[...] = gain_sum
    hidden[: plan.channels] = first_sum
    hidden[plan.channels :] = second_sum
    size = pieces[0].shape[0]
    for shift, piece in enumerate(pieces):
        block = (place[0] + shift) % len(pieces)
        piece[...] = hidden[cut(block, size), :].astype(piece.dtype)


def last_kernel(
    place, fine, coarse, fine_left, coarse_left, received, gains, back_fine, back_coarse,
    fine_out, coarse_out, scratch, *, plan, scales,
):
    blocks = Blocks(plan)
    grids, lefts, outs = (fine, coarse), (fine_left, coarse_left), (fine_out, coarse_out)
    backs = (back_fine, back_coarse)
    blocks.load(scratch, received)
    for grid, t in blocks.items:
        normed_grad = blocks.take(scratch, grid, t, backs[grid][...], scales[grid])
        unit, inverse = normalize(blocks.read(grids[grid], grid, t).astype(WIDE))
        gradient = lefts[grid][t].astype(WIDE) + norm_back(normed_grad * gains[0:1, :], unit, inverse)
        blocks.write(outs[grid], grid, t, gradient.astype(LOW))


def row_masks(count):
    slot = lax.broadcasted_iota(jnp.int32, (count, 1), 0) % 8
    return [(slot // 4 == owned) & (slot % 4 < RIDER) for owned in range(OWNED)], slot == RIDER


def mixing(rows, weights, masks, sign, contract):
    split = rows.shape[0] // 2
    top, bottom = None, None
    for owned in range(OWNED):
        chosen = jnp.where(masks[owned], rows, 0.0).astype(LOW)
        by_real = wide_dot(chosen, weights[owned, 0], contract)
        by_imag = wide_dot(chosen, weights[owned, 1], contract) * sign
        up = by_real[:split] - by_imag[split:]
        down = by_real[split:] + by_imag[:split]
        top, bottom = (up, down) if top is None else (top + up, bottom + down)
    return top, bottom


class Joined:
    def __init__(self, ref):
        self.ref = ref

    def __getitem__(self, at):
        value = self.ref[at[0], at[1]]
        return value.reshape(-1, value.shape[-1])


def collect(own, pieces, target):
    for shift, piece in enumerate(pieces):
        source = (own + len(pieces) - shift) % len(pieces)
        for owned in range(OWNED):
            for part in range(2):
                target[owned, part, source] = piece[owned, part]


def mix_kernel(place, held, *refs):
    *pieces, out, weights = refs
    collect(place[1], pieces, weights)
    split = held.shape[0] // 2
    masks, rider = row_masks(held.shape[0])
    top, bottom = mixing(held[...].astype(WIDE), Joined(weights), masks, 1.0, ((1,), (1,)))
    out[:split] = top.astype(LOW)
    out[split:] = bottom.astype(LOW)


def sum_kernel(place, *refs, axis):
    *pieces, out, ordered = refs
    for shift, piece in enumerate(pieces):
        ordered[(place[axis] + len(pieces) - shift) % len(pieces)] = piece[...].astype(WIDE)
    total = ordered[0]
    for at in range(1, len(pieces)):
        total = total + ordered[at]
    out[...] = total.astype(out.dtype)


def join_kernel(place, table, spectrum, gain, out):
    masks, rider = row_masks(table.shape[0])
    out[...] = jnp.where(rider, gain[...], wide_dot(table[...], spectrum[...])).astype(LOW)


def mix_back_kernel(place, received, held, weights, gains, out, gain):
    masks, rider = row_masks(held.shape[0])
    rows = received[...].astype(WIDE)
    gain[...] = jnp.sum(jnp.where(rider, rows, 0.0), axis=0, keepdims=True)
    top, bottom = mixing(rows, Joined(weights), masks, -1.0, ((1,), (0,)))
    back = jnp.concatenate([top, bottom], axis=0)
    gain_row = jnp.sum(back * held[...].astype(WIDE), axis=0, keepdims=True) / gains[0:1, :]
    out[...] = jnp.where(rider, gain_row, back).astype(LOW)


def spread_kernel(place, table, received, second, momentum, gains, out, total_out, moment_out, updated_out):
    masks, rider = row_masks(table.shape[0])
    out[...] = wide_dot(table[...], received[...], ((0,), (0,))).astype(LOW)
    first = jnp.sum(jnp.where(rider, received[...].astype(WIDE), 0.0), axis=0, keepdims=True)
    for row, total in enumerate((first, second[...])):
        at = slice(row, row + 1)
        total_out[at, :] = total
        moment = MOMENTUM_DECAY * momentum[at, :] + total
        moment_out[at, :] = moment
        scale = jnp.sqrt(jnp.mean(moment * moment, axis=-1, keepdims=True)) + 1e-06
        updated_out[at, :] = gains[at, :] - GAIN_RATE * moment / scale


def scatter(own, source, pieces, kind):
    size = pieces[0].shape[3]
    for shift, piece in enumerate(pieces):
        block = (own + shift) % len(pieces)
        for owned in range(OWNED):
            for part in range(2):
                piece[kind, owned, part] = source[owned, part, cut(block, size), :].astype(LOW)


def shift_gram(gram):
    size = gram.shape[0]
    unit = lax.broadcasted_iota(jnp.int32, gram.shape, 0) == lax.broadcasted_iota(jnp.int32, gram.shape, 1)
    level = jnp.sum(jnp.sum(jnp.where(unit, gram, 0.0), axis=1, keepdims=True), axis=0, keepdims=True) / size
    keep = POLY_FIRST + level * (POLY_SECOND + POLY_THIRD * level)
    return jnp.where(unit, gram - level, gram), keep, POLY_SECOND + 2.0 * POLY_THIRD * level


def beside(left, right):
    return jnp.concatenate([left, right], axis=1)


def below(top, bottom):
    return jnp.concatenate([top, bottom], axis=0)


def complex_rows(real, imag):
    return below(beside(real, -imag), beside(imag, real))


def complex_muon_kernel(place, mixed_grads, held, *refs):
    count = (len(refs) - 3) // 2
    sources, pieces, (momentum, grads, result) = refs[:count], refs[count : 2 * count], refs[2 * count :]
    collect(place[1], sources, momentum)
    masks, rider = row_masks(held.shape[0])
    split = held.shape[0] // 2
    coeffs, rows = held[...].astype(WIDE), mixed_grads[...].astype(WIDE)
    swapped = jnp.concatenate([rows[split:], -rows[:split]], axis=0).astype(LOW)
    for owned in range(OWNED):
        picked = jnp.where(masks[owned], coeffs, 0.0).astype(LOW)
        for part, side in enumerate((mixed_grads[...], swapped)):
            grads[owned, part] = wide_dot(side, picked, ((0,), (0,)))
    momentum = Joined(momentum)
    states = []
    for owned in range(OWNED):
        parts = [
            MOMENTUM_DECAY * momentum[owned, part].astype(WIDE) + grads[owned, part] for part in range(2)
        ]
        total = jnp.sum(parts[0] * parts[0]) + jnp.sum(parts[1] * parts[1])
        scale = 1.0 / (jnp.sqrt(total) + 1e-07)
        states.append([part * scale for part in parts])
    for iteration in range(5):
        for state in states:
            size = state[0].shape[0]
            real, imag = state[0].astype(LOW), state[1].astype(LOW)
            side = beside(real, imag)
            gram = wide_dot(below(side, beside(imag, -real)), side, ((1,), (1,)))
            rest, keep, lead = shift_gram(gram[:size])
            gram = below(rest, gram[size:])
            low = gram.astype(LOW)
            square = wide_dot(complex_rows(low[:size], low[size:]), low)
            poly = (lead * gram + POLY_THIRD * square).astype(LOW)
            change = wide_dot(complex_rows(poly[:size], poly[size:]), below(real, imag))
            state[0] = keep * state[0] + change[:size]
            state[1] = keep * state[1] + change[size:]
    for owned in range(OWNED):
        for part in range(2):
            result[owned, part] = states[owned][part]
    scatter(place[1], grads, pieces, 0)
    scatter(place[1], result, pieces, 1)


def real_muon_kernel(place, momentum, weight, *refs):
    *pieces, grad_out, moment_out, updated_out, low_out, gathered = refs
    if len(pieces) == 1:
        gathered[0] = pieces[0][...]
    else:
        side = place[0] % 2
        for shift, piece in enumerate(pieces):
            pair = (place[0] // 2 + len(pieces) - shift) % len(pieces)
            gathered[2 * pair + side] = piece[0].astype(WIDE)
            gathered[2 * pair + 1 - side] = piece[1].astype(WIDE)
    whole = gathered[...].reshape(momentum.shape)
    currents = []
    for part in range(2):
        grad = whole[part]
        grad_out[part] = grad
        moment = MOMENTUM_DECAY * momentum[part] + grad
        moment_out[part] = moment
        currents.append(moment * (1.0 / (jnp.sqrt(jnp.sum(moment * moment)) + 1e-07)))
    for iteration in range(5):
        for part in range(2):
            current = currents[part]
            low = current.astype(LOW)
            rest, keep, lead = shift_gram(wide_dot(low, low, ((1,), (1,))))
            low_rest = rest.astype(LOW)
            poly = lead * rest + POLY_THIRD * wide_dot(low_rest, low_rest)
            currents[part] = keep * current + wide_dot(poly.astype(LOW), low)
    for part in range(2):
        updated = weight[part] - STEP_RATE * currents[part]
        updated_out[part] = updated
        low_out[part] = updated.astype(LOW)


def finish_kernel(place, momentum, weight, *refs, count):
    pieces, (grad_out, moment_out, updated_out, low_out) = refs[:count], refs[count:]
    shift = (place[1] + count - pl.program_id(0)) % count
    for at in range(count):

        @pl.when(shift == at)
        def _():
            grad = pieces[at][0].astype(WIDE)
            grad_out[...] = grad
            moment_out[...] = MOMENTUM_DECAY * momentum[...] + grad
            updated = weight[...] - STEP_RATE * pieces[at][1].astype(WIDE)
            updated_out[...] = updated
            low_out[...] = updated.astype(LOW)


def finish(place, momentum, weight, pieces):
    shape, count = weight.shape, len(pieces)
    block = pl.BlockSpec((OWNED,) + shape[1:], lambda owner, at: (owner, 0, 0, 0))
    whole = pl.BlockSpec(pieces[0].shape, lambda owner, at: (0, 0, 0, 0, 0))
    return pl.pallas_call(
        functools.partial(finish_kernel, count=count),
        out_shape=[jax.ShapeDtypeStruct(shape, dtype) for dtype in (WIDE, WIDE, WIDE, LOW)],
        grid_spec=pltpu.PrefetchScalarGridSpec(
            num_scalar_prefetch=1,
            grid=(shape[0] // OWNED,),
            in_specs=[block] * 2 + [whole] * count,
            out_specs=[block] * 4,
        ),
        compiler_params=pltpu.CompilerParams(vmem_limit_bytes=16 << 20),
        cost_estimate=estimate(6),
        name="finish",
    )(place, momentum, weight, *pieces)


def exchange(rows, axes, count):
    block = rows.reshape((count, -1) + rows.shape[1:])
    return lax.all_to_all(block, axes, 0, 0, tiled=True).reshape(rows.shape)


def shifted(piece, shift, count, axis="lon"):
    return lax.ppermute(piece, axis, [(source, (source + shift) % count) for source in range(count)])


def for_owners(plan, rows, lon_index, owners):
    pieces = []
    for shift in range(plan.lon):
        owner = jnp.minimum((lon_index + shift) % plan.lon, owners - 1)
        pieces.append(lax.dynamic_slice_in_dim(rows, owner * OWNED, OWNED, 0).astype(LOW))
    return pieces


def together(*values):
    return lax.optimization_barrier(values)


def body(
    fine_grid,
    coarse_grid,
    fine_cotangent,
    coarse_cotangent,
    spectral_weight,
    spectral_momentum,
    hidden_weight,
    hidden_momentum,
    norm_gains,
    gain_momentum,
):
    plan = Plan(lax.axis_size("lat"), lax.axis_size("lon"), fine_grid, coarse_grid, spectral_weight)
    lat_index, lon_index = lax.axis_index("lat"), lax.axis_index("lon")
    place = jnp.stack([lat_index, lon_index]).astype(jnp.int32)
    channels, devices = plan.channels, plan.devices
    owners = plan.deg_dev // OWNED
    block_rows = channels // plan.lon
    fine_table, fine_back, coarse_table, coarse_back = map(jnp.asarray, plan.fourier())
    exchanged = jax.ShapeDtypeStruct((devices * plan.rows, channels), LOW)
    rows_scratch = ((channels // LANES, devices * plan.rows, LANES), WIDE)
    owned_rows = jax.ShapeDtypeStruct((devices * 8, channels), LOW)
    gain_shape = jax.ShapeDtypeStruct((1, channels), WIDE)
    left_low = [jax.ShapeDtypeStruct(grid.shape, LOW) for grid in (fine_grid, coarse_grid)]
    coarse_grid, coarse_cotangent = (jnp.swapaxes(grid, 0, 1) for grid in (coarse_grid, coarse_cotangent))
    grid_low = [jax.ShapeDtypeStruct(grid.shape, LOW) for grid in (fine_grid, coarse_grid)]
    piece_shape = jax.ShapeDtypeStruct((2, OWNED, 2, block_rows, channels), LOW)
    own_shape = (OWNED, 2, channels, channels)
    collected_shape = (OWNED, 2, plan.lon, block_rows, channels)
    forward_scales = (
        2.0 * math.pi / plan.fine_lon * plan.fine_ka,
        2.0 * math.pi / plan.coarse_lon * plan.coarse_ka,
    )
    inverse_scales = (1.0 / plan.fine_ka, 1.0 / plan.coarse_ka)
    large = 16 if devices <= 32 else 56

    sent = kernel_call(
        functools.partial(front_kernel, plan=plan, scales=forward_scales),
        "front",
        exchanged,
        [rows_scratch],
        {3: of_lon(fine_table), 4: of_lon(coarse_table)},
        megabytes=24,
        cost=3,
    )(place, fine_grid, coarse_grid, norm_gains, fine_table, coarse_table)
    weights = for_owners(plan, spectral_weight, lon_index, owners)
    momentum = for_owners(plan, spectral_momentum, lon_index, owners)
    first_shifts, middle_shift = [1, *range(3, plan.lon)], 2
    sent, weights = together(sent, weights)
    spectrum = exchange(sent, BOTH, devices)
    for shift in first_shifts:
        weights[shift] = shifted(weights[shift], shift, plan.lon)
    weighted, doubled = legendre_tables(plan, lat_index, lon_index)
    hidden_low = hidden_weight.astype(LOW)

    coeffs, weights, momentum = together(wide_dot(weighted, spectrum).astype(LOW), weights, momentum)
    held = exchange(coeffs, BOTH, devices)
    weights[middle_shift] = shifted(weights[middle_shift], middle_shift, plan.lon)
    mixed, weights = kernel_call(
        mix_kernel, "mix", (owned_rows, jax.ShapeDtypeStruct(collected_shape, LOW))
    )(place, held, *weights)
    mixed = exchange(mixed, BOTH, devices)
    values = wide_dot(doubled, mixed, ((0,), (0,))).astype(LOW)
    values = exchange(values, BOTH, devices)
    values, momentum = together(values, momentum)
    for shift in range(1, plan.lon):
        momentum[shift] = shifted(momentum[shift], shift, plan.lon)

    parts = plan.lat if plan.lat <= 8 else 1
    hidden_piece = jax.ShapeDtypeStruct(
        (2 * channels // parts, hidden_weight.shape[2]), LOW if parts > 1 else WIDE
    )
    fine_out, coarse_out, fine_left, coarse_left, sent, gain_second, *pieces = kernel_call(
        functools.partial(middle_kernel, plan=plan, scales=inverse_scales),
        "middle",
        (*grid_low, *left_low, exchanged, gain_shape, *[hidden_piece] * parts),
        [rows_scratch, ((2 * channels, hidden_weight.shape[2]), WIDE)],
        {
            8: of_lon(fine_table),
            9: of_lon(coarse_table),
            10: of_lon(fine_back),
            11: of_lon(coarse_back),
        },
        megabytes=60,
        cost=10,
    )(
        place, fine_grid, coarse_grid, fine_cotangent, coarse_cotangent, values, norm_gains,
        hidden_low[0], hidden_low[1], fine_table, coarse_table, fine_back, coarse_back,
    )
    sent, momentum = together(sent, momentum)
    spectrum = exchange(sent, BOTH, devices)
    if parts > 1:
        for shift in range(1, parts):
            pieces[shift] = shifted(pieces[shift], shift, parts, "lat")
    coeffs = kernel_call(join_kernel, "join", owned_rows, megabytes=large)(
        place, doubled, spectrum, gain_second
    )
    mixed_grad = exchange(coeffs, BOTH, devices)
    if parts > 1:
        total = kernel_call(
            functools.partial(sum_kernel, axis=0), "sum_lat", hidden_piece, [((parts, *hidden_piece.shape), WIDE)]
        )(place, *pieces)
        totals = [total] + [shifted(total, shift, plan.lon) for shift in range(1, plan.lon)]
    else:
        pieces = [lax.psum(pieces[0], BOTH)]

    coeffs, gain_second = kernel_call(
        mix_back_kernel, "mix_back", (owned_rows, gain_shape), megabytes=large, cost=2
    )(place, mixed_grad, held, weights, norm_gains)
    coeffs = exchange(coeffs, BOTH, devices)
    steps = kernel_call(
        complex_muon_kernel,
        "complex_muon",
        (piece_shape,) * plan.lon,
        [(collected_shape, LOW), (own_shape, WIDE), (own_shape, WIDE)],
        megabytes=32,
        cost=10,
    )(place, mixed_grad, held, *momentum)
    coeffs, steps = together(coeffs, steps)
    steps = [steps[0]] + [shifted(steps[shift], shift, plan.lon) for shift in range(1, plan.lon)]
    gains_shape = jax.ShapeDtypeStruct(norm_gains.shape, WIDE)
    values, gains_total, gain_moment, gain_updated = kernel_call(
        spread_kernel, "spread", (exchanged, gains_shape, gains_shape, gains_shape), megabytes=large
    )(place, weighted, coeffs, gain_second, gain_momentum, norm_gains)
    if parts > 1:
        totals, _ = together(totals, gain_second)
        total = kernel_call(
            functools.partial(sum_kernel, axis=1), "sum_lon", hidden_piece, [((plan.lon, *hidden_piece.shape), WIDE)]
        )(place, *totals)
        partner = lax.ppermute(total, "lat", [(source, source ^ 1) for source in range(parts)])
        both, _ = together(jnp.stack([total, partner]), gains_total)
        pieces = [both] + [shifted(both, shift, parts, "lat") for shift in range(2, parts, 2)]
    else:
        pieces, _ = together(pieces, gains_total)
    values = exchange(values, BOTH, devices)
    hidden_wide = jax.ShapeDtypeStruct(hidden_weight.shape, WIDE)
    hidden_grad, hidden_moment, hidden_updated, hidden_copy = kernel_call(
        real_muon_kernel,
        "real_muon",
        (hidden_wide, hidden_wide, hidden_wide, jax.ShapeDtypeStruct(hidden_weight.shape, LOW)),
        [((parts, *hidden_piece.shape), WIDE)],
        megabytes=60,
        cost=3,
    )(place, hidden_momentum, hidden_weight, *pieces)
    fine_gradient, coarse_gradient = kernel_call(
        functools.partial(last_kernel, plan=plan, scales=forward_scales),
        "last",
        tuple(grid_low),
        [rows_scratch],
        {6: of_lon(fine_back), 7: of_lon(coarse_back)},
        megabytes=60,
        cost=4,
    )(place, fine_grid, coarse_grid, fine_left, coarse_left, values, norm_gains, fine_back, coarse_back)
    steps, _ = together(steps, fine_gradient)
    spectral_grad, spectral_moment, spectral_updated, spectral_copy = finish(
        place, spectral_momentum, spectral_weight, steps
    )

    return (
        fine_out,
        jnp.swapaxes(coarse_out, 0, 1),
        fine_gradient,
        jnp.swapaxes(coarse_gradient, 0, 1),
        spectral_grad,
        spectral_moment,
        spectral_updated,
        spectral_copy,
        hidden_grad,
        hidden_moment,
        hidden_updated,
        hidden_copy,
        gains_total,
        gain_moment,
        gain_updated,
    )


def solution(mesh):
    grid = P("lat", "lon", None)
    degree = P("lat", None, "lon", None)
    return jax.shard_map(
        body,
        mesh=mesh,
        in_specs=(grid,) * 4 + (degree,) * 2 + (P(),) * 4,
        out_specs=(grid,) * 4 + (degree,) * 4 + (P(),) * 7,
        check_vma=False,
    )
```

```python
import functools
import math

import jax
import jax.numpy as jnp
import ml_dtypes
import numpy as np
from jax import lax
from jax.experimental import pallas as pl
from jax.experimental.pallas import tpu as pltpu
from jax.sharding import PartitionSpec as P

OWNED = 2
RIDER = 3
GROUP = 2
LANES = 128
NORM_EPSILON = 1e-05
MOMENTUM_DECAY = 0.5
STEP_RATE = 0.6
GAIN_RATE = 0.2
POLY_FIRST = 3.4445
POLY_SECOND = -4.775
POLY_THIRD = 2.0315
BOTH = ("lat", "lon")
LOW = jnp.bfloat16
WIDE = jnp.float32


class Plan:
    def __init__(self, lat_count, lon_count, fine, coarse, weight):
        self.lat, self.lon = lat_count, lon_count
        self.devices = lat_count * lon_count
        self.tf, self.nf, self.channels = fine.shape
        self.tc, self.nc = coarse.shape[:2]
        self.deg_dev = weight.shape[0]
        self.degrees = self.deg_dev * lat_count
        self.half = self.degrees // 2
        self.fine_lat, self.coarse_lat = self.tf * lat_count, self.tc * lat_count
        self.fine_lon, self.coarse_lon = self.nf * lon_count, self.nc * lon_count
        self.rows = 3 * self.tf + 2 * self.tc
        self.fine_ka = math.sqrt(self.fine_lat * self.fine_lon / (4.0 * math.pi))
        self.coarse_ka = math.sqrt(self.coarse_lat * self.coarse_lon / (4.0 * math.pi))
        self.parts_lat = lat_count // 2

    def orders(self, lat_index, lon_index):
        part = lat_index // self.parts_lat
        trio = (lat_index % self.parts_lat) * self.lon + lon_index
        even = 1 - trio % 2
        pair = trio // 2
        low, high = 3 * pair, self.half + 3 * pair
        first = high + 2 * (1 - even)
        second = even * (high + 1) + (1 - even) * (low + 1)
        third = even * low + (1 - even) * (low + 2)
        return (first, second, third), part, even

    def fourier(self):
        fine = np.zeros((self.lon, 3, self.devices, self.nf))
        coarse = np.zeros((self.lon, 2, self.devices, self.nc))

        def fill(out, order, part, total):
            position = np.arange(total)
            angle = 2.0 * np.pi / total * (position * order % total)
            line = -np.sin(angle) if part else np.cos(angle)
            out[...] = line.reshape(self.lon, -1)

        for lat_index in range(self.lat):
            for lon_index in range(self.lon):
                device = lat_index * self.lon + lon_index
                orders, part, even = self.orders(lat_index, lon_index)
                for row in range(3):
                    fill(fine[:, row, device], orders[row], part, self.fine_lon)
                for row in range(1 + even):
                    fill(coarse[:, row, device], orders[row] - self.half, part, self.coarse_lon)
        results = []
        for table in (fine, coarse):
            flat = table.reshape(self.lon, -1, table.shape[-1]).astype(ml_dtypes.bfloat16)
            results += [flat, np.swapaxes(flat, 1, 2)]
        return results


def legendre_kernel(columns, weighted_out, doubled_out, slope, back, start, *, degrees, half):
    order, cosine, quadrature, doubling = (columns[row : row + 1, :] for row in range(4))
    used, diagonal = columns[4:5, :], columns[5:6, :]
    degree = lax.broadcasted_iota(jnp.int32, slope.shape, 0).astype(WIDE)

    def factor(at):
        square = at * at
        return jnp.sqrt(
            jnp.maximum(4.0 * square - 1.0, 1.0) / jnp.maximum(square - order * order, 1.0)
        )

    now = factor(degree)
    running = (degree > order) & (degree < used)
    slope[...] = jnp.where(running, now * cosine, 0.0)
    back[...] = jnp.where(running, now / factor(degree - 1.0), 0.0)
    start[...] = jnp.where((degree == order) & (degree < used), diagonal, 0.0)

    def step(block, carried):
        latest, earlier = carried
        base = pl.multiple_of(block * 8, 8)
        slopes, backs, starts = (ref[pl.ds(base, 8), :] for ref in (slope, back, start))
        found = []
        for row in range(8):
            at = slice(row, row + 1)
            latest, earlier = slopes[at] * latest - backs[at] * earlier + starts[at], latest
            found.append(latest)
        start[pl.ds(base, 8), :] = jnp.concatenate(found, axis=0)
        return latest, earlier

    zero = jnp.zeros_like(order)
    lax.fori_loop(0, degrees // 8, step, (zero, zero))
    plain = start[...]
    weighted_out[...] = (quadrature * plain).astype(LOW)
    doubled_out[...] = (doubling * plain.astype(LOW).astype(WIDE)).astype(LOW)


def legendre_tables(plan, lat_index, lon_index):
    orders, part, even = plan.orders(lat_index, lon_index)
    fine_kind = np.repeat(np.arange(3), plan.tf)
    coarse_kind = np.repeat(np.arange(2), plan.tc)
    kind = np.tile(np.concatenate([fine_kind, coarse_kind]), plan.devices)
    is_fine = np.tile(np.arange(plan.rows) < 3 * plan.tf, plan.devices)
    lat_of = np.repeat(np.arange(plan.devices) // plan.lon, plan.rows)
    fine_lat = lat_of * plan.tf + np.tile(np.arange(plan.rows) % plan.tf, plan.devices)
    coarse_lat = lat_of * plan.tc + np.tile(np.arange(plan.rows) % plan.tc, plan.devices)
    position = np.where(is_fine, fine_lat, coarse_lat)
    count = np.where(is_fine, plan.fine_lat, plan.coarse_lat)
    colatitude = np.pi * (position + 0.5) / count
    own = jnp.where(kind == 0, orders[0], jnp.where(kind == 1, orders[1], orders[2]))
    own = jnp.where(is_fine, own, own - plan.half)
    held = own >= 0
    own = jnp.maximum(own, 0)
    span = np.arange(plan.degrees)
    norms = np.array(
        [
            0.5
            * (
                math.log((2.0 * m + 1.0) / (4.0 * math.pi))
                + math.lgamma(m + 0.5)
                - math.lgamma(m + 1.0)
                - 0.5 * math.log(math.pi)
            )
            for m in span
        ],
        np.float32,
    )
    norm = jnp.sum(jnp.where(own[None, :] == span[:, None], norms[:, None], 0.0), axis=0)
    log_sine = np.log(np.sin(colatitude)).astype(np.float32)
    diagonal = jnp.where(held, jnp.exp(norm + own.astype(WIDE) * log_sine), 0.0)
    columns = jnp.stack(
        [
            own.astype(WIDE),
            jnp.asarray(np.cos(colatitude).astype(np.float32)),
            jnp.asarray((np.pi / count * np.sin(colatitude)).astype(np.float32)),
            jnp.where(own == 0, 1.0, 2.0),
            jnp.asarray(np.where(is_fine, plan.degrees, plan.half).astype(np.float32)),
            diagonal,
        ]
    )
    shape = (plan.degrees, plan.devices * plan.rows)
    compact = pl.pallas_call(
        functools.partial(legendre_kernel, degrees=plan.degrees, half=plan.half),
        out_shape=(jax.ShapeDtypeStruct(shape, LOW),) * 2,
        scratch_shapes=[pltpu.VMEM(shape, WIDE)] * 3,
        compiler_params=pltpu.CompilerParams(vmem_limit_bytes=(16 if shape[1] <= 512 else 56) << 20),
        name="legendre",
    )(columns)
    chosen = kind[None, :] == np.arange(4)[:, None]
    pairs = plan.deg_dev // OWNED
    results = []
    for table in compact:
        spread = table.reshape(plan.lat, pairs, OWNED, 1, shape[1])
        spread = jnp.where(chosen, spread, jnp.zeros_like(spread))
        spread = jnp.pad(spread, ((0, 0), (0, plan.lon - pairs), (0, 0), (0, 0), (0, 0)))
        results.append(spread.reshape(plan.devices * 8, shape[1]))
    return results


def wide_dot(left, right, contract=((1,), (0,))):
    return lax.dot_general(left, right, (contract, ((), ())), preferred_element_type=WIDE)


def normalize(values):
    shifted = values - jnp.mean(values, axis=-1, keepdims=True)
    inverse = lax.rsqrt(jnp.mean(shifted * shifted, axis=-1, keepdims=True) + NORM_EPSILON)
    return shifted * inverse, inverse


def norm_back(grad, unit, inverse):
    return (
        grad
        - jnp.mean(grad, axis=-1, keepdims=True)
        - unit * jnp.mean(grad * unit, axis=-1, keepdims=True)
    ) * inverse


def kernel_call(kernel, name, out_shape, scratch=(), views=None, megabytes=16, cost=2):
    views = views or {}

    def run(place, *arrays):
        def spec(shape, at=None):
            if at in views:
                block, index = views[at]
                return pl.BlockSpec(block, lambda step, place: index(place))
            return pl.BlockSpec(tuple(shape), lambda step, place: (0,) * len(shape))

        outs = jax.tree.leaves(out_shape)
        found = pl.pallas_call(
            kernel,
            out_shape=outs,
            grid_spec=pltpu.PrefetchScalarGridSpec(
                num_scalar_prefetch=1,
                grid=(1,),
                in_specs=[spec(each.shape, at) for at, each in enumerate(arrays)],
                out_specs=[spec(each.shape) for each in outs],
                scratch_shapes=[pltpu.VMEM(*each) for each in scratch],
            ),
            compiler_params=pltpu.CompilerParams(vmem_limit_bytes=megabytes << 20),
            cost_estimate=estimate(cost),
            name=name,
        )(place, *arrays)
        return jax.tree.unflatten(jax.tree.structure(out_shape), found)

    return run


def estimate(microseconds):
    return pl.CostEstimate(
        flops=int(microseconds * 1.1e9), bytes_accessed=int(microseconds * 3e6), transcendentals=0
    )


def of_lon(table):
    return (None,) + table.shape[1:], lambda place: (place[1], 0, 0)


def cut(block, size):
    return pl.ds(pl.multiple_of(block * size, size), size)


class Blocks:
    def __init__(self, plan):
        self.plan = plan
        self.items = [(0, t) for t in range(plan.tf)] + [(1, t) for t in range(plan.tc)]

    def strides(self, grid, t):
        plan = self.plan
        starts = (
            [row * plan.tf + t for row in range(3)]
            if grid == 0
            else [3 * plan.tf + row * plan.tc + t for row in range(2)]
        )
        return [pl.ds(start, plan.devices, stride=plan.rows) for start in starts]

    def read(self, ref, grid, t):
        return ref[t] if grid == 0 else ref[:, t, :]

    def write(self, ref, grid, t, value):
        if grid == 0:
            ref[t] = value
        else:
            ref[:, t, :] = value

    def load(self, scratch, received):
        for lane in range(scratch.shape[0]):
            scratch[lane] = received[:, lane * LANES : (lane + 1) * LANES].astype(WIDE)

    def store(self, scratch, sent):
        for lane in range(scratch.shape[0]):
            sent[:, lane * LANES : (lane + 1) * LANES] = scratch[lane].astype(LOW)

    def put(self, scratch, grid, t, table, values, scale):
        summed = wide_dot(table, values) * scale
        for row, where in enumerate(self.strides(grid, t)):
            part = summed[row * self.plan.devices : (row + 1) * self.plan.devices]
            for lane in range(scratch.shape[0]):
                scratch[lane, where, :] = part[:, lane * LANES : (lane + 1) * LANES]

    def take(self, scratch, grid, t, table, scale):
        found = [
            jnp.concatenate([scratch[lane, where, :] for lane in range(scratch.shape[0])], axis=1)
            for where in self.strides(grid, t)
        ]
        values = jnp.concatenate(found, axis=0).astype(LOW)
        return (wide_dot(table, values) * scale).astype(LOW).astype(WIDE)


def front_kernel(place, fine, coarse, gains, table_fine, table_coarse, sent, scratch, *, plan, scales):
    blocks = Blocks(plan)
    grids, tables = (fine, coarse), (table_fine, table_coarse)
    for grid, t in blocks.items:
        unit, inverse = normalize(blocks.read(grids[grid], grid, t).astype(WIDE))
        normed = (unit * gains[0:1, :]).astype(LOW)
        blocks.put(scratch, grid, t, tables[grid][...], normed, scales[grid])
    blocks.store(scratch, sent)


def middle_kernel(
    place, fine, coarse, fine_up, coarse_up, received, gains, first, second,
    table_fine, table_coarse, back_fine, back_coarse,
    fine_out, coarse_out, fine_left, coarse_left, sent, gain, *rest, plan, scales,
):
    *pieces, scratch, hidden = rest
    blocks = Blocks(plan)
    grids, ups, outs, lefts = (
        (fine, coarse), (fine_up, coarse_up), (fine_out, coarse_out), (fine_left, coarse_left)
    )
    tables, backs = (table_fine, table_coarse), (back_fine, back_coarse)
    root = math.sqrt(2.0 / math.pi)
    scaling = gains[1:2, :]
    first_low, second_low = first[...], second[...]
    first_sum = second_sum = gain_sum = None
    blocks.load(scratch, received)
    branches = {
        (grid, t): blocks.take(scratch, grid, t, backs[grid][...], scales[grid]) for grid, t in blocks.items
    }
    groups = [(0, tuple(range(t, t + GROUP))) for t in range(0, plan.tf, GROUP)]
    groups += [(1, (t,)) for t in range(plan.tc)]
    for grid, group in groups:
        joined = lambda parts: parts[0] if len(parts) == 1 else jnp.concatenate(parts, axis=0)
        values = joined([blocks.read(grids[grid], grid, t) for t in group])
        upstream = joined([blocks.read(ups[grid], grid, t) for t in group])
        residual = values.astype(WIDE) + joined([branches[grid, t] for t in group])
        unit, inverse = normalize(residual)
        normed = (unit * scaling).astype(LOW)
        pre = wide_dot(normed, first_low)
        square = pre * pre
        inner = pre * (root + root * 0.044715 * square)
        gate = 0.5 + 0.5 * jnp.tanh(inner)
        active = (pre * gate).astype(LOW)
        output = (residual + wide_dot(active, second_low, ((1,), (1,)))).astype(LOW)
        slope = gate + gate * (1.0 - gate) * (pre * (2.0 * root + 6.0 * root * 0.044715 * square))
        pre_grad = (wide_dot(upstream, second_low) * slope).astype(LOW)
        normed_grad = wide_dot(pre_grad, first_low, ((1,), (1,)))
        left = upstream.astype(WIDE) + norm_back(normed_grad * scaling, unit, inverse)
        left_low = left.astype(LOW)
        size = left_low.shape[0] // len(group)
        for at, t in enumerate(group):
            rows = slice(at * size, (at + 1) * size)
            blocks.write(outs[grid], grid, t, output[rows])
            lefts[grid][t] = left_low[rows]
            blocks.put(scratch, grid, t, tables[grid][...], left_low[rows], scales[grid])
        first_part = wide_dot(normed, pre_grad, ((0,), (0,)))
        second_part = wide_dot(upstream, active, ((0,), (0,)))
        gain_part = jnp.sum(normed_grad * unit, axis=0, keepdims=True)
        if first_sum is None:
            first_sum, second_sum, gain_sum = first_part, second_part, gain_part
        else:
            first_sum, second_sum, gain_sum = (
                first_sum + first_part, second_sum + second_part, gain_sum + gain_part
            )
    blocks.store(scratch, sent)
    gain[...] = gain_sum
    hidden[: plan.channels] = first_sum
    hidden[plan.channels :] = second_sum
    size = pieces[0].shape[0]
    for shift, piece in enumerate(pieces):
        block = (place[0] + shift) % len(pieces)
        piece[...] = hidden[cut(block, size), :].astype(piece.dtype)


def last_kernel(
    place, fine, coarse, fine_left, coarse_left, received, gains, back_fine, back_coarse,
    fine_out, coarse_out, scratch, *, plan, scales,
):
    blocks = Blocks(plan)
    grids, lefts, outs = (fine, coarse), (fine_left, coarse_left), (fine_out, coarse_out)
    backs = (back_fine, back_coarse)
    blocks.load(scratch, received)
    for grid, t in blocks.items:
        normed_grad = blocks.take(scratch, grid, t, backs[grid][...], scales[grid])
        unit, inverse = normalize(blocks.read(grids[grid], grid, t).astype(WIDE))
        gradient = lefts[grid][t].astype(WIDE) + norm_back(normed_grad * gains[0:1, :], unit, inverse)
        blocks.write(outs[grid], grid, t, gradient.astype(LOW))


def row_masks(count):
    slot = lax.broadcasted_iota(jnp.int32, (count, 1), 0) % 8
    return [(slot // 4 == owned) & (slot % 4 < RIDER) for owned in range(OWNED)], slot == RIDER


def mixing(rows, weights, masks, sign, contract):
    split = rows.shape[0] // 2
    top, bottom = None, None
    for owned in range(OWNED):
        chosen = jnp.where(masks[owned], rows, 0.0).astype(LOW)
        by_real = wide_dot(chosen, weights[owned, 0], contract)
        by_imag = wide_dot(chosen, weights[owned, 1], contract) * sign
        up = by_real[:split] - by_imag[split:]
        down = by_real[split:] + by_imag[:split]
        top, bottom = (up, down) if top is None else (top + up, bottom + down)
    return top, bottom


class Joined:
    def __init__(self, ref):
        self.ref = ref

    def __getitem__(self, at):
        value = self.ref[at[0], at[1]]
        return value.reshape(-1, value.shape[-1])


def collect(own, pieces, target):
    for shift, piece in enumerate(pieces):
        source = (own + len(pieces) - shift) % len(pieces)
        for owned in range(OWNED):
            for part in range(2):
                target[owned, part, source] = piece[owned, part]


def mix_kernel(place, held, *refs):
    *pieces, out, weights = refs
    collect(place[1], pieces, weights)
    split = held.shape[0] // 2
    masks, rider = row_masks(held.shape[0])
    top, bottom = mixing(held[...].astype(WIDE), Joined(weights), masks, 1.0, ((1,), (1,)))
    out[:split] = top.astype(LOW)
    out[split:] = bottom.astype(LOW)


def sum_kernel(place, *refs, axis):
    *pieces, out, ordered = refs
    for shift, piece in enumerate(pieces):
        ordered[(place[axis] + len(pieces) - shift) % len(pieces)] = piece[...].astype(WIDE)
    total = ordered[0]
    for at in range(1, len(pieces)):
        total = total + ordered[at]
    out[...] = total.astype(out.dtype)


def join_kernel(place, table, spectrum, gain, out):
    masks, rider = row_masks(table.shape[0])
    out[...] = jnp.where(rider, gain[...], wide_dot(table[...], spectrum[...])).astype(LOW)


def mix_back_kernel(place, received, held, weights, gains, out, gain):
    masks, rider = row_masks(held.shape[0])
    rows = received[...].astype(WIDE)
    gain[...] = jnp.sum(jnp.where(rider, rows, 0.0), axis=0, keepdims=True)
    top, bottom = mixing(rows, Joined(weights), masks, -1.0, ((1,), (0,)))
    back = jnp.concatenate([top, bottom], axis=0)
    gain_row = jnp.sum(back * held[...].astype(WIDE), axis=0, keepdims=True) / gains[0:1, :]
    out[...] = jnp.where(rider, gain_row, back).astype(LOW)


def spread_kernel(place, table, received, second, momentum, gains, out, total_out, moment_out, updated_out):
    masks, rider = row_masks(table.shape[0])
    out[...] = wide_dot(table[...], received[...], ((0,), (0,))).astype(LOW)
    first = jnp.sum(jnp.where(rider, received[...].astype(WIDE), 0.0), axis=0, keepdims=True)
    for row, total in enumerate((first, second[...])):
        at = slice(row, row + 1)
        total_out[at, :] = total
        moment = MOMENTUM_DECAY * momentum[at, :] + total
        moment_out[at, :] = moment
        scale = jnp.sqrt(jnp.mean(moment * moment, axis=-1, keepdims=True)) + 1e-06
        updated_out[at, :] = gains[at, :] - GAIN_RATE * moment / scale


def scatter(own, source, pieces, kind):
    size = pieces[0].shape[3]
    for shift, piece in enumerate(pieces):
        block = (own + shift) % len(pieces)
        for owned in range(OWNED):
            for part in range(2):
                piece[kind, owned, part] = source[owned, part, cut(block, size), :].astype(LOW)


def shift_gram(gram):
    size = gram.shape[0]
    unit = lax.broadcasted_iota(jnp.int32, gram.shape, 0) == lax.broadcasted_iota(jnp.int32, gram.shape, 1)
    level = jnp.sum(jnp.sum(jnp.where(unit, gram, 0.0), axis=1, keepdims=True), axis=0, keepdims=True) / size
    keep = POLY_FIRST + level * (POLY_SECOND + POLY_THIRD * level)
    return jnp.where(unit, gram - level, gram), keep, POLY_SECOND + 2.0 * POLY_THIRD * level


def beside(left, right):
    return jnp.concatenate([left, right], axis=1)


def below(top, bottom):
    return jnp.concatenate([top, bottom], axis=0)


def complex_rows(real, imag):
    return below(beside(real, -imag), beside(imag, real))


def complex_muon_kernel(place, mixed_grads, held, *refs):
    count = (len(refs) - 3) // 2
    sources, pieces, (momentum, grads, result) = refs[:count], refs[count : 2 * count], refs[2 * count :]
    collect(place[1], sources, momentum)
    masks, rider = row_masks(held.shape[0])
    split = held.shape[0] // 2
    coeffs, rows = held[...].astype(WIDE), mixed_grads[...].astype(WIDE)
    swapped = jnp.concatenate([rows[split:], -rows[:split]], axis=0).astype(LOW)
    for owned in range(OWNED):
        picked = jnp.where(masks[owned], coeffs, 0.0).astype(LOW)
        for part, side in enumerate((mixed_grads[...], swapped)):
            grads[owned, part] = wide_dot(side, picked, ((0,), (0,)))
    momentum = Joined(momentum)
    states = []
    for owned in range(OWNED):
        parts = [
            MOMENTUM_DECAY * momentum[owned, part].astype(WIDE) + grads[owned, part] for part in range(2)
        ]
        total = jnp.sum(parts[0] * parts[0]) + jnp.sum(parts[1] * parts[1])
        scale = 1.0 / (jnp.sqrt(total) + 1e-07)
        states.append([part * scale for part in parts])
    for iteration in range(5):
        size = states[0][0].shape[0]
        lows = [[part.astype(LOW) for part in state] for state in states]
        sides = [beside(real, imag) for real, imag in lows]
        grams = [
            wide_dot(below(side, beside(imag, -real)), side, ((1,), (1,)))
            for side, (real, imag) in zip(sides, lows)
        ]
        shifts = [shift_gram(gram[:size]) for gram in grams]
        grams = [below(rest, gram[size:]) for gram, (rest, keep, lead) in zip(grams, shifts)]
        low_grams = [gram.astype(LOW) for gram in grams]
        squares = [wide_dot(complex_rows(low[:size], low[size:]), low) for low in low_grams]
        polys = [
            (lead * gram + POLY_THIRD * square).astype(LOW)
            for gram, square, (rest, keep, lead) in zip(grams, squares, shifts)
        ]
        changes = [
            wide_dot(complex_rows(poly[:size], poly[size:]), below(*low)) for poly, low in zip(polys, lows)
        ]
        states = [
            [keep * state[0] + change[:size], keep * state[1] + change[size:]]
            for state, change, (rest, keep, lead) in zip(states, changes, shifts)
        ]
    for owned in range(OWNED):
        for part in range(2):
            result[owned, part] = states[owned][part]
    scatter(place[1], grads, pieces, 0)
    scatter(place[1], result, pieces, 1)


def real_muon_kernel(place, momentum, weight, *refs):
    *pieces, grad_out, moment_out, updated_out, low_out, gathered = refs
    if len(pieces) == 1:
        gathered[0] = pieces[0][...]
    else:
        side = place[0] % 2
        for shift, piece in enumerate(pieces):
            pair = (place[0] // 2 + len(pieces) - shift) % len(pieces)
            gathered[2 * pair + side] = piece[0].astype(WIDE)
            gathered[2 * pair + 1 - side] = piece[1].astype(WIDE)
    whole = gathered[...].reshape(momentum.shape)
    currents = []
    for part in range(2):
        grad = whole[part]
        grad_out[part] = grad
        moment = MOMENTUM_DECAY * momentum[part] + grad
        moment_out[part] = moment
        currents.append(moment * (1.0 / (jnp.sqrt(jnp.sum(moment * moment)) + 1e-07)))
    for iteration in range(5):
        lows = [current.astype(LOW) for current in currents]
        shifts = [shift_gram(wide_dot(low, low, ((1,), (1,)))) for low in lows]
        rests = [rest.astype(LOW) for rest, keep, lead in shifts]
        squares = [wide_dot(rest, rest) for rest in rests]
        polys = [
            (lead * rest + POLY_THIRD * square).astype(LOW)
            for square, (rest, keep, lead) in zip(squares, shifts)
        ]
        changes = [wide_dot(poly, low) for poly, low in zip(polys, lows)]
        currents = [
            keep * current + change
            for current, change, (rest, keep, lead) in zip(currents, changes, shifts)
        ]
    for part in range(2):
        updated = weight[part] - STEP_RATE * currents[part]
        updated_out[part] = updated
        low_out[part] = updated.astype(LOW)


def finish_kernel(place, momentum, weight, *refs, count):
    pieces, (grad_out, moment_out, updated_out, low_out) = refs[:count], refs[count:]
    shift = (place[1] + count - pl.program_id(0)) % count
    for at in range(count):

        @pl.when(shift == at)
        def _():
            grad = pieces[at][0].astype(WIDE)
            grad_out[...] = grad
            moment_out[...] = MOMENTUM_DECAY * momentum[...] + grad
            updated = weight[...] - STEP_RATE * pieces[at][1].astype(WIDE)
            updated_out[...] = updated
            low_out[...] = updated.astype(LOW)


def finish(place, momentum, weight, pieces):
    shape, count = weight.shape, len(pieces)
    block = pl.BlockSpec((OWNED,) + shape[1:], lambda owner, at: (owner, 0, 0, 0))
    whole = pl.BlockSpec(pieces[0].shape, lambda owner, at: (0, 0, 0, 0, 0))
    return pl.pallas_call(
        functools.partial(finish_kernel, count=count),
        out_shape=[jax.ShapeDtypeStruct(shape, dtype) for dtype in (WIDE, WIDE, WIDE, LOW)],
        grid_spec=pltpu.PrefetchScalarGridSpec(
            num_scalar_prefetch=1,
            grid=(shape[0] // OWNED,),
            in_specs=[block] * 2 + [whole] * count,
            out_specs=[block] * 4,
        ),
        compiler_params=pltpu.CompilerParams(vmem_limit_bytes=16 << 20),
        cost_estimate=estimate(6),
        name="finish",
    )(place, momentum, weight, *pieces)


def exchange(rows, axes, count):
    block = rows.reshape((count, -1) + rows.shape[1:])
    return lax.all_to_all(block, axes, 0, 0, tiled=True).reshape(rows.shape)


def shifted(piece, shift, count, axis="lon"):
    return lax.ppermute(piece, axis, [(source, (source + shift) % count) for source in range(count)])


def for_owners(plan, rows, lon_index, owners):
    pieces = []
    for shift in range(plan.lon):
        owner = jnp.minimum((lon_index + shift) % plan.lon, owners - 1)
        pieces.append(lax.dynamic_slice_in_dim(rows, owner * OWNED, OWNED, 0).astype(LOW))
    return pieces


def together(*values):
    return lax.optimization_barrier(values)


def body(
    fine_grid,
    coarse_grid,
    fine_cotangent,
    coarse_cotangent,
    spectral_weight,
    spectral_momentum,
    hidden_weight,
    hidden_momentum,
    norm_gains,
    gain_momentum,
):
    plan = Plan(lax.axis_size("lat"), lax.axis_size("lon"), fine_grid, coarse_grid, spectral_weight)
    lat_index, lon_index = lax.axis_index("lat"), lax.axis_index("lon")
    place = jnp.stack([lat_index, lon_index]).astype(jnp.int32)
    channels, devices = plan.channels, plan.devices
    owners = plan.deg_dev // OWNED
    block_rows = channels // plan.lon
    fine_table, fine_back, coarse_table, coarse_back = map(jnp.asarray, plan.fourier())
    exchanged = jax.ShapeDtypeStruct((devices * plan.rows, channels), LOW)
    rows_scratch = ((channels // LANES, devices * plan.rows, LANES), WIDE)
    owned_rows = jax.ShapeDtypeStruct((devices * 8, channels), LOW)
    gain_shape = jax.ShapeDtypeStruct((1, channels), WIDE)
    left_low = [jax.ShapeDtypeStruct(grid.shape, LOW) for grid in (fine_grid, coarse_grid)]
    coarse_grid, coarse_cotangent = (jnp.swapaxes(grid, 0, 1) for grid in (coarse_grid, coarse_cotangent))
    grid_low = [jax.ShapeDtypeStruct(grid.shape, LOW) for grid in (fine_grid, coarse_grid)]
    piece_shape = jax.ShapeDtypeStruct((2, OWNED, 2, block_rows, channels), LOW)
    own_shape = (OWNED, 2, channels, channels)
    collected_shape = (OWNED, 2, plan.lon, block_rows, channels)
    forward_scales = (
        2.0 * math.pi / plan.fine_lon * plan.fine_ka,
        2.0 * math.pi / plan.coarse_lon * plan.coarse_ka,
    )
    inverse_scales = (1.0 / plan.fine_ka, 1.0 / plan.coarse_ka)
    large = 16 if devices <= 32 else 56

    sent = kernel_call(
        functools.partial(front_kernel, plan=plan, scales=forward_scales),
        "front",
        exchanged,
        [rows_scratch],
        {3: of_lon(fine_table), 4: of_lon(coarse_table)},
        megabytes=24,
        cost=3,
    )(place, fine_grid, coarse_grid, norm_gains, fine_table, coarse_table)
    weights = for_owners(plan, spectral_weight, lon_index, owners)
    momentum = for_owners(plan, spectral_momentum, lon_index, owners)
    first_shifts, middle_shift = [1, *range(3, plan.lon)], 2
    sent, weights = together(sent, weights)
    spectrum = exchange(sent, BOTH, devices)
    for shift in first_shifts:
        weights[shift] = shifted(weights[shift], shift, plan.lon)
    weighted, doubled = legendre_tables(plan, lat_index, lon_index)
    hidden_low = hidden_weight.astype(LOW)

    coeffs, weights, momentum = together(wide_dot(weighted, spectrum).astype(LOW), weights, momentum)
    held = exchange(coeffs, BOTH, devices)
    weights[middle_shift] = shifted(weights[middle_shift], middle_shift, plan.lon)
    mixed, weights = kernel_call(
        mix_kernel, "mix", (owned_rows, jax.ShapeDtypeStruct(collected_shape, LOW))
    )(place, held, *weights)
    mixed = exchange(mixed, BOTH, devices)
    values = wide_dot(doubled, mixed, ((0,), (0,))).astype(LOW)
    values = exchange(values, BOTH, devices)
    values, momentum = together(values, momentum)
    for shift in range(1, plan.lon):
        momentum[shift] = shifted(momentum[shift], shift, plan.lon)

    parts = plan.lat if plan.lat <= 8 else 1
    hidden_piece = jax.ShapeDtypeStruct(
        (2 * channels // parts, hidden_weight.shape[2]), LOW if parts > 1 else WIDE
    )
    fine_out, coarse_out, fine_left, coarse_left, sent, gain_second, *pieces = kernel_call(
        functools.partial(middle_kernel, plan=plan, scales=inverse_scales),
        "middle",
        (*grid_low, *left_low, exchanged, gain_shape, *[hidden_piece] * parts),
        [rows_scratch, ((2 * channels, hidden_weight.shape[2]), WIDE)],
        {
            8: of_lon(fine_table),
            9: of_lon(coarse_table),
            10: of_lon(fine_back),
            11: of_lon(coarse_back),
        },
        megabytes=60,
        cost=10,
    )(
        place, fine_grid, coarse_grid, fine_cotangent, coarse_cotangent, values, norm_gains,
        hidden_low[0], hidden_low[1], fine_table, coarse_table, fine_back, coarse_back,
    )
    sent, momentum = together(sent, momentum)
    spectrum = exchange(sent, BOTH, devices)
    if parts > 1:
        for shift in range(1, parts):
            pieces[shift] = shifted(pieces[shift], shift, parts, "lat")
    coeffs = kernel_call(join_kernel, "join", owned_rows, megabytes=large)(
        place, doubled, spectrum, gain_second
    )
    mixed_grad = exchange(coeffs, BOTH, devices)
    if parts > 1:
        total = kernel_call(
            functools.partial(sum_kernel, axis=0), "sum_lat", hidden_piece, [((parts, *hidden_piece.shape), WIDE)]
        )(place, *pieces)
        totals = [total] + [shifted(total, shift, plan.lon) for shift in range(1, plan.lon)]
    else:
        pieces = [lax.psum(pieces[0], BOTH)]

    coeffs, gain_second = kernel_call(
        mix_back_kernel, "mix_back", (owned_rows, gain_shape), megabytes=large, cost=2
    )(place, mixed_grad, held, weights, norm_gains)
    coeffs = exchange(coeffs, BOTH, devices)
    steps = kernel_call(
        complex_muon_kernel,
        "complex_muon",
        (piece_shape,) * plan.lon,
        [(collected_shape, LOW), (own_shape, WIDE), (own_shape, WIDE)],
        megabytes=32,
        cost=10,
    )(place, mixed_grad, held, *momentum)
    coeffs, steps = together(coeffs, steps)
    steps = [steps[0]] + [shifted(steps[shift], shift, plan.lon) for shift in range(1, plan.lon)]
    gains_shape = jax.ShapeDtypeStruct(norm_gains.shape, WIDE)
    values, gains_total, gain_moment, gain_updated = kernel_call(
        spread_kernel, "spread", (exchanged, gains_shape, gains_shape, gains_shape), megabytes=large
    )(place, weighted, coeffs, gain_second, gain_momentum, norm_gains)
    if parts > 1:
        totals, _ = together(totals, gain_second)
        total = kernel_call(
            functools.partial(sum_kernel, axis=1), "sum_lon", hidden_piece, [((plan.lon, *hidden_piece.shape), WIDE)]
        )(place, *totals)
        partner = lax.ppermute(total, "lat", [(source, source ^ 1) for source in range(parts)])
        both, _ = together(jnp.stack([total, partner]), gains_total)
        pieces = [both] + [shifted(both, shift, parts, "lat") for shift in range(2, parts, 2)]
    else:
        pieces, _ = together(pieces, gains_total)
    values = exchange(values, BOTH, devices)
    hidden_wide = jax.ShapeDtypeStruct(hidden_weight.shape, WIDE)
    hidden_grad, hidden_moment, hidden_updated, hidden_copy = kernel_call(
        real_muon_kernel,
        "real_muon",
        (hidden_wide, hidden_wide, hidden_wide, jax.ShapeDtypeStruct(hidden_weight.shape, LOW)),
        [((parts, *hidden_piece.shape), WIDE)],
        megabytes=60,
        cost=3,
    )(place, hidden_momentum, hidden_weight, *pieces)
    fine_gradient, coarse_gradient = kernel_call(
        functools.partial(last_kernel, plan=plan, scales=forward_scales),
        "last",
        tuple(grid_low),
        [rows_scratch],
        {6: of_lon(fine_back), 7: of_lon(coarse_back)},
        megabytes=60,
        cost=4,
    )(place, fine_grid, coarse_grid, fine_left, coarse_left, values, norm_gains, fine_back, coarse_back)
    steps, _ = together(steps, fine_gradient)
    spectral_grad, spectral_moment, spectral_updated, spectral_copy = finish(
        place, spectral_momentum, spectral_weight, steps
    )

    return (
        fine_out,
        jnp.swapaxes(coarse_out, 0, 1),
        fine_gradient,
        jnp.swapaxes(coarse_gradient, 0, 1),
        spectral_grad,
        spectral_moment,
        spectral_updated,
        spectral_copy,
        hidden_grad,
        hidden_moment,
        hidden_updated,
        hidden_copy,
        gains_total,
        gain_moment,
        gain_updated,
    )


def solution(mesh):
    grid = P("lat", "lon", None)
    degree = P("lat", None, "lon", None)
    return jax.shard_map(
        body,
        mesh=mesh,
        in_specs=(grid,) * 4 + (degree,) * 2 + (P(),) * 4,
        out_specs=(grid,) * 4 + (degree,) * 4 + (P(),) * 7,
        check_vma=False,
    )
```

```python
import functools
import math

import jax
import jax.numpy as jnp
import ml_dtypes
import numpy as np
from jax import lax
from jax.experimental import pallas as pl
from jax.experimental.pallas import tpu as pltpu
from jax.sharding import PartitionSpec as P

OWNED = 2
RIDER = 3
GROUP = 2
LANES = 128
NORM_EPSILON = 1e-05
MOMENTUM_DECAY = 0.5
STEP_RATE = 0.6
GAIN_RATE = 0.2
POLY_FIRST = 3.4445
POLY_SECOND = -4.775
POLY_THIRD = 2.0315
BOTH = ("lat", "lon")
LOW = jnp.bfloat16
WIDE = jnp.float32


class Plan:
    def __init__(self, lat_count, lon_count, fine, coarse, weight):
        self.lat, self.lon = lat_count, lon_count
        self.devices = lat_count * lon_count
        self.tf, self.nf, self.channels = fine.shape
        self.tc, self.nc = coarse.shape[:2]
        self.deg_dev = weight.shape[0]
        self.degrees = self.deg_dev * lat_count
        self.half = self.degrees // 2
        self.fine_lat, self.coarse_lat = self.tf * lat_count, self.tc * lat_count
        self.fine_lon, self.coarse_lon = self.nf * lon_count, self.nc * lon_count
        self.rows = 3 * self.tf + 2 * self.tc
        self.fine_ka = math.sqrt(self.fine_lat * self.fine_lon / (4.0 * math.pi))
        self.coarse_ka = math.sqrt(self.coarse_lat * self.coarse_lon / (4.0 * math.pi))
        self.parts_lat = lat_count // 2

    def orders(self, lat_index, lon_index):
        part = lat_index // self.parts_lat
        trio = (lat_index % self.parts_lat) * self.lon + lon_index
        even = 1 - trio % 2
        pair = trio // 2
        low, high = 3 * pair, self.half + 3 * pair
        first = high + 2 * (1 - even)
        second = even * (high + 1) + (1 - even) * (low + 1)
        third = even * low + (1 - even) * (low + 2)
        return (first, second, third), part, even

    def fourier(self):
        fine = np.zeros((self.lon, 3, self.devices, self.nf))
        coarse = np.zeros((self.lon, 2, self.devices, self.nc))

        def fill(out, order, part, total):
            position = np.arange(total)
            angle = 2.0 * np.pi / total * (position * order % total)
            line = -np.sin(angle) if part else np.cos(angle)
            out[...] = line.reshape(self.lon, -1)

        for lat_index in range(self.lat):
            for lon_index in range(self.lon):
                device = lat_index * self.lon + lon_index
                orders, part, even = self.orders(lat_index, lon_index)
                for row in range(3):
                    fill(fine[:, row, device], orders[row], part, self.fine_lon)
                for row in range(1 + even):
                    fill(coarse[:, row, device], orders[row] - self.half, part, self.coarse_lon)
        results = []
        for table in (fine, coarse):
            flat = table.reshape(self.lon, -1, table.shape[-1]).astype(ml_dtypes.bfloat16)
            results += [flat, np.swapaxes(flat, 1, 2)]
        return results


def legendre_kernel(columns, weighted_out, doubled_out, slope, back, start, *, degrees, half):
    order, cosine, quadrature, doubling = (columns[row : row + 1, :] for row in range(4))
    used, diagonal = columns[4:5, :], columns[5:6, :]
    degree = lax.broadcasted_iota(jnp.int32, slope.shape, 0).astype(WIDE)

    def factor(at):
        square = at * at
        return jnp.sqrt(
            jnp.maximum(4.0 * square - 1.0, 1.0) / jnp.maximum(square - order * order, 1.0)
        )

    now = factor(degree)
    running = (degree > order) & (degree < used)
    slope[...] = jnp.where(running, now * cosine, 0.0)
    back[...] = jnp.where(running, now / factor(degree - 1.0), 0.0)
    start[...] = jnp.where((degree == order) & (degree < used), diagonal, 0.0)

    def step(block, carried):
        latest, earlier = carried
        base = pl.multiple_of(block * 8, 8)
        slopes, backs, starts = (ref[pl.ds(base, 8), :] for ref in (slope, back, start))
        found = []
        for row in range(8):
            at = slice(row, row + 1)
            latest, earlier = slopes[at] * latest - backs[at] * earlier + starts[at], latest
            found.append(latest)
        start[pl.ds(base, 8), :] = jnp.concatenate(found, axis=0)
        return latest, earlier

    zero = jnp.zeros_like(order)
    lax.fori_loop(0, degrees // 8, step, (zero, zero))
    plain = start[...]
    weighted_out[...] = (quadrature * plain).astype(LOW)
    doubled_out[...] = (doubling * plain.astype(LOW).astype(WIDE)).astype(LOW)


def legendre_tables(plan, lat_index, lon_index):
    orders, part, even = plan.orders(lat_index, lon_index)
    fine_kind = np.repeat(np.arange(3), plan.tf)
    coarse_kind = np.repeat(np.arange(2), plan.tc)
    kind = np.tile(np.concatenate([fine_kind, coarse_kind]), plan.devices)
    is_fine = np.tile(np.arange(plan.rows) < 3 * plan.tf, plan.devices)
    lat_of = np.repeat(np.arange(plan.devices) // plan.lon, plan.rows)
    fine_lat = lat_of * plan.tf + np.tile(np.arange(plan.rows) % plan.tf, plan.devices)
    coarse_lat = lat_of * plan.tc + np.tile(np.arange(plan.rows) % plan.tc, plan.devices)
    position = np.where(is_fine, fine_lat, coarse_lat)
    count = np.where(is_fine, plan.fine_lat, plan.coarse_lat)
    colatitude = np.pi * (position + 0.5) / count
    own = jnp.where(kind == 0, orders[0], jnp.where(kind == 1, orders[1], orders[2]))
    own = jnp.where(is_fine, own, own - plan.half)
    held = own >= 0
    own = jnp.maximum(own, 0)
    span = np.arange(plan.degrees)
    norms = np.array(
        [
            0.5
            * (
                math.log((2.0 * m + 1.0) / (4.0 * math.pi))
                + math.lgamma(m + 0.5)
                - math.lgamma(m + 1.0)
                - 0.5 * math.log(math.pi)
            )
            for m in span
        ],
        np.float32,
    )
    norm = jnp.sum(jnp.where(own[None, :] == span[:, None], norms[:, None], 0.0), axis=0)
    log_sine = np.log(np.sin(colatitude)).astype(np.float32)
    diagonal = jnp.where(held, jnp.exp(norm + own.astype(WIDE) * log_sine), 0.0)
    columns = jnp.stack(
        [
            own.astype(WIDE),
            jnp.asarray(np.cos(colatitude).astype(np.float32)),
            jnp.asarray((np.pi / count * np.sin(colatitude)).astype(np.float32)),
            jnp.where(own == 0, 1.0, 2.0),
            jnp.asarray(np.where(is_fine, plan.degrees, plan.half).astype(np.float32)),
            diagonal,
        ]
    )
    shape = (plan.degrees, plan.devices * plan.rows)
    compact = pl.pallas_call(
        functools.partial(legendre_kernel, degrees=plan.degrees, half=plan.half),
        out_shape=(jax.ShapeDtypeStruct(shape, LOW),) * 2,
        scratch_shapes=[pltpu.VMEM(shape, WIDE)] * 3,
        compiler_params=pltpu.CompilerParams(vmem_limit_bytes=(16 if shape[1] <= 512 else 56) << 20),
        name="legendre",
    )(columns)
    chosen = kind[None, :] == np.arange(4)[:, None]
    pairs = plan.deg_dev // OWNED
    results = []
    for table in compact:
        spread = table.reshape(plan.lat, pairs, OWNED, 1, shape[1])
        spread = jnp.where(chosen, spread, jnp.zeros_like(spread))
        spread = jnp.pad(spread, ((0, 0), (0, plan.lon - pairs), (0, 0), (0, 0), (0, 0)))
        results.append(spread.reshape(plan.devices * 8, shape[1]))
    return results


def wide_dot(left, right, contract=((1,), (0,))):
    return lax.dot_general(left, right, (contract, ((), ())), preferred_element_type=WIDE)


def normalize(values):
    shifted = values - jnp.mean(values, axis=-1, keepdims=True)
    inverse = lax.rsqrt(jnp.mean(shifted * shifted, axis=-1, keepdims=True) + NORM_EPSILON)
    return shifted * inverse, inverse


def norm_back(grad, unit, inverse):
    return (
        grad
        - jnp.mean(grad, axis=-1, keepdims=True)
        - unit * jnp.mean(grad * unit, axis=-1, keepdims=True)
    ) * inverse


def kernel_call(kernel, name, out_shape, scratch=(), views=None, megabytes=16, cost=2):
    views = views or {}

    def run(place, *arrays):
        def spec(shape, at=None):
            if at in views:
                block, index = views[at]
                return pl.BlockSpec(block, lambda step, place: index(place))
            return pl.BlockSpec(tuple(shape), lambda step, place: (0,) * len(shape))

        outs = jax.tree.leaves(out_shape)
        found = pl.pallas_call(
            kernel,
            out_shape=outs,
            grid_spec=pltpu.PrefetchScalarGridSpec(
                num_scalar_prefetch=1,
                grid=(1,),
                in_specs=[spec(each.shape, at) for at, each in enumerate(arrays)],
                out_specs=[spec(each.shape) for each in outs],
                scratch_shapes=[pltpu.VMEM(*each) for each in scratch],
            ),
            compiler_params=pltpu.CompilerParams(vmem_limit_bytes=megabytes << 20),
            cost_estimate=estimate(cost),
            name=name,
        )(place, *arrays)
        return jax.tree.unflatten(jax.tree.structure(out_shape), found)

    return run


def estimate(microseconds):
    return pl.CostEstimate(
        flops=int(microseconds * 1.1e9), bytes_accessed=int(microseconds * 3e6), transcendentals=0
    )


def of_lon(table):
    return (None,) + table.shape[1:], lambda place: (place[1], 0, 0)


def cut(block, size):
    return pl.ds(pl.multiple_of(block * size, size), size)


class Blocks:
    def __init__(self, plan):
        self.plan = plan
        self.items = [(0, t) for t in range(plan.tf)] + [(1, t) for t in range(plan.tc)]

    def strides(self, grid, t):
        plan = self.plan
        starts = (
            [row * plan.tf + t for row in range(3)]
            if grid == 0
            else [3 * plan.tf + row * plan.tc + t for row in range(2)]
        )
        return [pl.ds(start, plan.devices, stride=plan.rows) for start in starts]

    def read(self, ref, grid, t):
        return ref[t] if grid == 0 else ref[:, t, :]

    def write(self, ref, grid, t, value):
        if grid == 0:
            ref[t] = value
        else:
            ref[:, t, :] = value

    def load(self, scratch, received):
        for lane in range(scratch.shape[0]):
            scratch[lane] = received[:, lane * LANES : (lane + 1) * LANES].astype(WIDE)

    def store(self, scratch, sent):
        for lane in range(scratch.shape[0]):
            sent[:, lane * LANES : (lane + 1) * LANES] = scratch[lane].astype(LOW)

    def put(self, scratch, grid, t, table, values, scale):
        summed = wide_dot(table, values) * scale
        for row, where in enumerate(self.strides(grid, t)):
            part = summed[row * self.plan.devices : (row + 1) * self.plan.devices]
            for lane in range(scratch.shape[0]):
                scratch[lane, where, :] = part[:, lane * LANES : (lane + 1) * LANES]

    def take(self, scratch, grid, t, table, scale):
        found = [
            jnp.concatenate([scratch[lane, where, :] for lane in range(scratch.shape[0])], axis=1)
            for where in self.strides(grid, t)
        ]
        values = jnp.concatenate(found, axis=0).astype(LOW)
        return (wide_dot(table, values) * scale).astype(LOW).astype(WIDE)


def front_kernel(place, fine, coarse, gains, table_fine, table_coarse, sent, scratch, *, plan, scales):
    blocks = Blocks(plan)
    grids, tables = (fine, coarse), (table_fine, table_coarse)
    for grid, t in blocks.items:
        unit, inverse = normalize(blocks.read(grids[grid], grid, t).astype(WIDE))
        normed = (unit * gains[0:1, :]).astype(LOW)
        blocks.put(scratch, grid, t, tables[grid][...], normed, scales[grid])
    blocks.store(scratch, sent)


def middle_kernel(
    place, fine, coarse, fine_up, coarse_up, received, gains, first, second,
    table_fine, table_coarse, back_fine, back_coarse,
    fine_out, coarse_out, fine_left, coarse_left, sent, gain, *rest, plan, scales,
):
    *pieces, scratch, hidden = rest
    blocks = Blocks(plan)
    grids, ups, outs, lefts = (
        (fine, coarse), (fine_up, coarse_up), (fine_out, coarse_out), (fine_left, coarse_left)
    )
    tables, backs = (table_fine, table_coarse), (back_fine, back_coarse)
    root = math.sqrt(2.0 / math.pi)
    scaling = gains[1:2, :]
    first_low, second_low = first[...], second[...]
    first_sum = second_sum = gain_sum = None
    blocks.load(scratch, received)
    branches = {
        (grid, t): blocks.take(scratch, grid, t, backs[grid][...], scales[grid]) for grid, t in blocks.items
    }
    groups = [(0, tuple(range(t, t + GROUP))) for t in range(0, plan.tf, GROUP)]
    groups += [(1, (t,)) for t in range(plan.tc)]
    for grid, group in groups:
        joined = lambda parts: parts[0] if len(parts) == 1 else jnp.concatenate(parts, axis=0)
        values = joined([blocks.read(grids[grid], grid, t) for t in group])
        upstream = joined([blocks.read(ups[grid], grid, t) for t in group])
        residual = values.astype(WIDE) + joined([branches[grid, t] for t in group])
        unit, inverse = normalize(residual)
        normed = (unit * scaling).astype(LOW)
        pre = wide_dot(normed, first_low)
        square = pre * pre
        inner = pre * (root + root * 0.044715 * square)
        gate = 0.5 + 0.5 * jnp.tanh(inner)
        active = (pre * gate).astype(LOW)
        output = (residual + wide_dot(active, second_low, ((1,), (1,)))).astype(LOW)
        slope = gate + gate * (1.0 - gate) * (pre * (2.0 * root + 6.0 * root * 0.044715 * square))
        pre_grad = (wide_dot(upstream, second_low) * slope).astype(LOW)
        normed_grad = wide_dot(pre_grad, first_low, ((1,), (1,)))
        left = upstream.astype(WIDE) + norm_back(normed_grad * scaling, unit, inverse)
        left_low = left.astype(LOW)
        size = left_low.shape[0] // len(group)
        for at, t in enumerate(group):
            rows = slice(at * size, (at + 1) * size)
            blocks.write(outs[grid], grid, t, output[rows])
            lefts[grid][t] = left_low[rows]
            blocks.put(scratch, grid, t, tables[grid][...], left_low[rows], scales[grid])
        first_part = wide_dot(normed, pre_grad, ((0,), (0,)))
        second_part = wide_dot(upstream, active, ((0,), (0,)))
        gain_part = jnp.sum(normed_grad * unit, axis=0, keepdims=True)
        if first_sum is None:
            first_sum, second_sum, gain_sum = first_part, second_part, gain_part
        else:
            first_sum, second_sum, gain_sum = (
                first_sum + first_part, second_sum + second_part, gain_sum + gain_part
            )
    blocks.store(scratch, sent)
    gain[...] = gain_sum
    hidden[: plan.channels] = first_sum
    hidden[plan.channels :] = second_sum
    size = pieces[0].shape[0]
    for shift, piece in enumerate(pieces):
        block = (place[0] + shift) % len(pieces)
        piece[...] = hidden[cut(block, size), :].astype(piece.dtype)


def last_kernel(
    place, fine, coarse, fine_left, coarse_left, received, gains, back_fine, back_coarse,
    fine_out, coarse_out, scratch, *, plan, scales,
):
    blocks = Blocks(plan)
    grids, lefts, outs = (fine, coarse), (fine_left, coarse_left), (fine_out, coarse_out)
    backs = (back_fine, back_coarse)
    blocks.load(scratch, received)
    for grid, t in blocks.items:
        normed_grad = blocks.take(scratch, grid, t, backs[grid][...], scales[grid])
        unit, inverse = normalize(blocks.read(grids[grid], grid, t).astype(WIDE))
        gradient = lefts[grid][t].astype(WIDE) + norm_back(normed_grad * gains[0:1, :], unit, inverse)
        blocks.write(outs[grid], grid, t, gradient.astype(LOW))


def row_masks(count):
    slot = lax.broadcasted_iota(jnp.int32, (count, 1), 0) % 8
    return [(slot // 4 == owned) & (slot % 4 < RIDER) for owned in range(OWNED)], slot == RIDER


def mixing(rows, weights, masks, sign, contract):
    split = rows.shape[0] // 2
    top, bottom = None, None
    for owned in range(OWNED):
        chosen = jnp.where(masks[owned], rows, 0.0).astype(LOW)
        by_real = wide_dot(chosen, weights[owned, 0], contract)
        by_imag = wide_dot(chosen, weights[owned, 1], contract) * sign
        up = by_real[:split] - by_imag[split:]
        down = by_real[split:] + by_imag[:split]
        top, bottom = (up, down) if top is None else (top + up, bottom + down)
    return top, bottom


class Joined:
    def __init__(self, ref):
        self.ref = ref

    def __getitem__(self, at):
        value = self.ref[at[0], at[1]]
        return value.reshape(-1, value.shape[-1])


def collect(own, pieces, target):
    for shift, piece in enumerate(pieces):
        source = (own + len(pieces) - shift) % len(pieces)
        for owned in range(OWNED):
            for part in range(2):
                target[owned, part, source] = piece[owned, part]


def mix_kernel(place, held, *refs):
    *pieces, out, weights = refs
    collect(place[1], pieces, weights)
    split = held.shape[0] // 2
    masks, rider = row_masks(held.shape[0])
    top, bottom = mixing(held[...].astype(WIDE), Joined(weights), masks, 1.0, ((1,), (1,)))
    out[:split] = top.astype(LOW)
    out[split:] = bottom.astype(LOW)


def sum_kernel(place, *refs, axis):
    *pieces, out, ordered = refs
    for shift, piece in enumerate(pieces):
        ordered[(place[axis] + len(pieces) - shift) % len(pieces)] = piece[...].astype(WIDE)
    total = ordered[0]
    for at in range(1, len(pieces)):
        total = total + ordered[at]
    out[...] = total.astype(out.dtype)


def join_kernel(place, table, spectrum, gain, out):
    masks, rider = row_masks(table.shape[0])
    out[...] = jnp.where(rider, gain[...], wide_dot(table[...], spectrum[...])).astype(LOW)


def mix_back_kernel(place, received, held, weights, gains, out, gain):
    masks, rider = row_masks(held.shape[0])
    rows = received[...].astype(WIDE)
    gain[...] = jnp.sum(jnp.where(rider, rows, 0.0), axis=0, keepdims=True)
    top, bottom = mixing(rows, Joined(weights), masks, -1.0, ((1,), (0,)))
    back = jnp.concatenate([top, bottom], axis=0)
    gain_row = jnp.sum(back * held[...].astype(WIDE), axis=0, keepdims=True) / gains[0:1, :]
    out[...] = jnp.where(rider, gain_row, back).astype(LOW)


def spread_kernel(place, table, received, second, momentum, gains, out, total_out, moment_out, updated_out):
    masks, rider = row_masks(table.shape[0])
    out[...] = wide_dot(table[...], received[...], ((0,), (0,))).astype(LOW)
    first = jnp.sum(jnp.where(rider, received[...].astype(WIDE), 0.0), axis=0, keepdims=True)
    for row, total in enumerate((first, second[...])):
        at = slice(row, row + 1)
        total_out[at, :] = total
        moment = MOMENTUM_DECAY * momentum[at, :] + total
        moment_out[at, :] = moment
        scale = jnp.sqrt(jnp.mean(moment * moment, axis=-1, keepdims=True)) + 1e-06
        updated_out[at, :] = gains[at, :] - GAIN_RATE * moment / scale


def scatter(own, source, pieces, kind):
    size = pieces[0].shape[3]
    for shift, piece in enumerate(pieces):
        block = (own + shift) % len(pieces)
        for owned in range(OWNED):
            for part in range(2):
                piece[kind, owned, part] = source[owned, part, cut(block, size), :].astype(LOW)


def shift_gram(gram):
    size = gram.shape[0]
    unit = lax.broadcasted_iota(jnp.int32, gram.shape, 0) == lax.broadcasted_iota(jnp.int32, gram.shape, 1)
    level = jnp.sum(jnp.sum(jnp.where(unit, gram, 0.0), axis=1, keepdims=True), axis=0, keepdims=True) / size
    keep = POLY_FIRST + level * (POLY_SECOND + POLY_THIRD * level)
    return jnp.where(unit, gram - level, gram), keep, POLY_SECOND + 2.0 * POLY_THIRD * level


def beside(left, right):
    return jnp.concatenate([left, right], axis=1)


def below(top, bottom):
    return jnp.concatenate([top, bottom], axis=0)


def complex_rows(real, imag):
    return below(beside(real, -imag), beside(imag, real))


def complex_muon_kernel(place, mixed_grads, held, *refs):
    count = (len(refs) - 3) // 2
    sources, pieces, (momentum, grads, result) = refs[:count], refs[count : 2 * count], refs[2 * count :]
    collect(place[1], sources, momentum)
    masks, rider = row_masks(held.shape[0])
    split = held.shape[0] // 2
    coeffs, rows = held[...].astype(WIDE), mixed_grads[...].astype(WIDE)
    swapped = jnp.concatenate([rows[split:], -rows[:split]], axis=0).astype(LOW)
    for owned in range(OWNED):
        picked = jnp.where(masks[owned], coeffs, 0.0).astype(LOW)
        for part, side in enumerate((mixed_grads[...], swapped)):
            grads[owned, part] = wide_dot(side, picked, ((0,), (0,)))
    momentum = Joined(momentum)
    states = []
    for owned in range(OWNED):
        parts = [
            MOMENTUM_DECAY * momentum[owned, part].astype(WIDE) + grads[owned, part] for part in range(2)
        ]
        total = jnp.sum(parts[0] * parts[0]) + jnp.sum(parts[1] * parts[1])
        scale = 1.0 / (jnp.sqrt(total) + 1e-07)
        states.append([part * scale for part in parts])
    for iteration in range(5):
        size = states[0][0].shape[0]
        lows = [[part.astype(LOW) for part in state] for state in states]
        sides = [beside(real, imag) for real, imag in lows]
        grams = [
            wide_dot(below(side, beside(imag, -real)), side, ((1,), (1,)))
            for side, (real, imag) in zip(sides, lows)
        ]
        shifts = [shift_gram(gram[:size]) for gram in grams]
        grams = [below(rest, gram[size:]) for gram, (rest, keep, lead) in zip(grams, shifts)]
        low_grams = [gram.astype(LOW) for gram in grams]
        squares = [wide_dot(complex_rows(low[:size], low[size:]), low) for low in low_grams]
        polys = [
            (lead * gram + POLY_THIRD * square).astype(LOW)
            for gram, square, (rest, keep, lead) in zip(grams, squares, shifts)
        ]
        changes = [
            wide_dot(complex_rows(poly[:size], poly[size:]), below(*low)) for poly, low in zip(polys, lows)
        ]
        states = [
            [keep * state[0] + change[:size], keep * state[1] + change[size:]]
            for state, change, (rest, keep, lead) in zip(states, changes, shifts)
        ]
    for owned in range(OWNED):
        for part in range(2):
            result[owned, part] = states[owned][part]
    scatter(place[1], grads, pieces, 0)
    scatter(place[1], result, pieces, 1)


def real_muon_kernel(place, momentum, weight, *refs):
    *pieces, grad_out, moment_out, updated_out, low_out, gathered = refs
    if len(pieces) == 1:
        gathered[0] = pieces[0][...]
    else:
        side = place[0] % 2
        for shift, piece in enumerate(pieces):
            pair = (place[0] // 2 + len(pieces) - shift) % len(pieces)
            gathered[2 * pair + side] = piece[0].astype(WIDE)
            gathered[2 * pair + 1 - side] = piece[1].astype(WIDE)
    whole = gathered[...].reshape(momentum.shape)
    currents = []
    for part in range(2):
        grad = whole[part]
        grad_out[part] = grad
        moment = MOMENTUM_DECAY * momentum[part] + grad
        moment_out[part] = moment
        currents.append(moment * (1.0 / (jnp.sqrt(jnp.sum(moment * moment)) + 1e-07)))
    for iteration in range(5):
        lows = [current.astype(LOW) for current in currents]
        shifts = [shift_gram(wide_dot(low, low, ((1,), (1,)))) for low in lows]
        rests = [rest.astype(LOW) for rest, keep, lead in shifts]
        squares = [wide_dot(rest, rest) for rest in rests]
        polys = [
            (lead * rest + POLY_THIRD * square).astype(LOW)
            for square, (rest, keep, lead) in zip(squares, shifts)
        ]
        changes = [wide_dot(poly, low) for poly, low in zip(polys, lows)]
        currents = [
            keep * current + change
            for current, change, (rest, keep, lead) in zip(currents, changes, shifts)
        ]
    for part in range(2):
        updated = weight[part] - STEP_RATE * currents[part]
        updated_out[part] = updated
        low_out[part] = updated.astype(LOW)


def finish_kernel(place, momentum, weight, *refs, count):
    pieces, (grad_out, moment_out, updated_out, low_out) = refs[:count], refs[count:]
    shift = (place[1] + count - pl.program_id(0)) % count
    for at in range(count):

        @pl.when(shift == at)
        def _():
            grad = pieces[at][0].astype(WIDE)
            grad_out[...] = grad
            moment_out[...] = MOMENTUM_DECAY * momentum[...] + grad
            updated = weight[...] - STEP_RATE * pieces[at][1].astype(WIDE)
            updated_out[...] = updated
            low_out[...] = updated.astype(LOW)


def finish(place, momentum, weight, pieces):
    shape, count = weight.shape, len(pieces)
    block = pl.BlockSpec((OWNED,) + shape[1:], lambda owner, at: (owner, 0, 0, 0))
    whole = pl.BlockSpec(pieces[0].shape, lambda owner, at: (0, 0, 0, 0, 0))
    return pl.pallas_call(
        functools.partial(finish_kernel, count=count),
        out_shape=[jax.ShapeDtypeStruct(shape, dtype) for dtype in (WIDE, WIDE, WIDE, LOW)],
        grid_spec=pltpu.PrefetchScalarGridSpec(
            num_scalar_prefetch=1,
            grid=(shape[0] // OWNED,),
            in_specs=[block] * 2 + [whole] * count,
            out_specs=[block] * 4,
        ),
        compiler_params=pltpu.CompilerParams(vmem_limit_bytes=16 << 20),
        cost_estimate=estimate(6),
        name="finish",
    )(place, momentum, weight, *pieces)


def exchange(rows, axes, count):
    block = rows.reshape((count, -1) + rows.shape[1:])
    return lax.all_to_all(block, axes, 0, 0, tiled=True).reshape(rows.shape)


def shifted(piece, shift, count, axis="lon"):
    return lax.ppermute(piece, axis, [(source, (source + shift) % count) for source in range(count)])


def for_owners(plan, rows, lon_index, owners):
    pieces = []
    for shift in range(plan.lon):
        owner = jnp.minimum((lon_index + shift) % plan.lon, owners - 1)
        pieces.append(lax.dynamic_slice_in_dim(rows, owner * OWNED, OWNED, 0).astype(LOW))
    return pieces


def together(*values):
    return lax.optimization_barrier(values)


def body(
    fine_grid,
    coarse_grid,
    fine_cotangent,
    coarse_cotangent,
    spectral_weight,
    spectral_momentum,
    hidden_weight,
    hidden_momentum,
    norm_gains,
    gain_momentum,
):
    plan = Plan(lax.axis_size("lat"), lax.axis_size("lon"), fine_grid, coarse_grid, spectral_weight)
    lat_index, lon_index = lax.axis_index("lat"), lax.axis_index("lon")
    place = jnp.stack([lat_index, lon_index]).astype(jnp.int32)
    channels, devices = plan.channels, plan.devices
    owners = plan.deg_dev // OWNED
    block_rows = channels // plan.lon
    fine_table, fine_back, coarse_table, coarse_back = map(jnp.asarray, plan.fourier())
    exchanged = jax.ShapeDtypeStruct((devices * plan.rows, channels), LOW)
    rows_scratch = ((channels // LANES, devices * plan.rows, LANES), WIDE)
    owned_rows = jax.ShapeDtypeStruct((devices * 8, channels), LOW)
    gain_shape = jax.ShapeDtypeStruct((1, channels), WIDE)
    left_low = [jax.ShapeDtypeStruct(grid.shape, LOW) for grid in (fine_grid, coarse_grid)]
    coarse_grid, coarse_cotangent = (jnp.swapaxes(grid, 0, 1) for grid in (coarse_grid, coarse_cotangent))
    grid_low = [jax.ShapeDtypeStruct(grid.shape, LOW) for grid in (fine_grid, coarse_grid)]
    piece_shape = jax.ShapeDtypeStruct((2, OWNED, 2, block_rows, channels), LOW)
    own_shape = (OWNED, 2, channels, channels)
    collected_shape = (OWNED, 2, plan.lon, block_rows, channels)
    forward_scales = (
        2.0 * math.pi / plan.fine_lon * plan.fine_ka,
        2.0 * math.pi / plan.coarse_lon * plan.coarse_ka,
    )
    inverse_scales = (1.0 / plan.fine_ka, 1.0 / plan.coarse_ka)
    large = 16 if devices <= 32 else 56

    sent = kernel_call(
        functools.partial(front_kernel, plan=plan, scales=forward_scales),
        "front",
        exchanged,
        [rows_scratch],
        {3: of_lon(fine_table), 4: of_lon(coarse_table)},
        megabytes=24,
        cost=3,
    )(place, fine_grid, coarse_grid, norm_gains, fine_table, coarse_table)
    weights = for_owners(plan, spectral_weight, lon_index, owners)
    momentum = for_owners(plan, spectral_momentum, lon_index, owners)
    first_shifts, middle_shift = [1, *range(3, plan.lon)], 2
    sent, weights = together(sent, weights)
    spectrum = exchange(sent, BOTH, devices)
    for shift in first_shifts:
        weights[shift] = shifted(weights[shift], shift, plan.lon)
    weighted, doubled = legendre_tables(plan, lat_index, lon_index)
    hidden_low = hidden_weight.astype(LOW)

    coeffs, weights, momentum = together(wide_dot(weighted, spectrum).astype(LOW), weights, momentum)
    held = exchange(coeffs, BOTH, devices)
    weights[middle_shift] = shifted(weights[middle_shift], middle_shift, plan.lon)
    mixed, weights = kernel_call(
        mix_kernel, "mix", (owned_rows, jax.ShapeDtypeStruct(collected_shape, LOW))
    )(place, held, *weights)
    mixed = exchange(mixed, BOTH, devices)
    values = wide_dot(doubled, mixed, ((0,), (0,))).astype(LOW)
    values = exchange(values, BOTH, devices)
    values, momentum = together(values, momentum)
    for shift in range(1, plan.lon):
        momentum[shift] = shifted(momentum[shift], shift, plan.lon)

    parts = plan.lat if plan.lat <= 8 else 1
    hidden_piece = jax.ShapeDtypeStruct(
        (2 * channels // parts, hidden_weight.shape[2]), LOW if parts > 1 else WIDE
    )
    fine_out, coarse_out, fine_left, coarse_left, sent, gain_second, *pieces = kernel_call(
        functools.partial(middle_kernel, plan=plan, scales=inverse_scales),
        "middle",
        (*grid_low, *left_low, exchanged, gain_shape, *[hidden_piece] * parts),
        [rows_scratch, ((2 * channels, hidden_weight.shape[2]), WIDE)],
        {
            8: of_lon(fine_table),
            9: of_lon(coarse_table),
            10: of_lon(fine_back),
            11: of_lon(coarse_back),
        },
        megabytes=60,
        cost=10,
    )(
        place, fine_grid, coarse_grid, fine_cotangent, coarse_cotangent, values, norm_gains,
        hidden_low[0], hidden_low[1], fine_table, coarse_table, fine_back, coarse_back,
    )
    sent, momentum = together(sent, momentum)
    spectrum = exchange(sent, BOTH, devices)
    if parts > 1:
        for shift in range(1, parts):
            pieces[shift] = shifted(pieces[shift], shift, parts, "lat")
    riding = jnp.arange(devices * 8)[:, None] % 8 == RIDER
    coeffs = jnp.where(riding, gain_second, wide_dot(doubled, spectrum)).astype(LOW)
    mixed_grad = exchange(coeffs, BOTH, devices)
    if parts > 1:
        total = kernel_call(
            functools.partial(sum_kernel, axis=0), "sum_lat", hidden_piece, [((parts, *hidden_piece.shape), WIDE)]
        )(place, *pieces)
        totals = [total] + [shifted(total, shift, plan.lon) for shift in range(1, plan.lon)]
    else:
        pieces = [lax.psum(pieces[0], BOTH)]

    coeffs, gain_second = kernel_call(
        mix_back_kernel, "mix_back", (owned_rows, gain_shape), megabytes=large, cost=2
    )(place, mixed_grad, held, weights, norm_gains)
    coeffs = exchange(coeffs, BOTH, devices)
    steps = kernel_call(
        complex_muon_kernel,
        "complex_muon",
        (piece_shape,) * plan.lon,
        [(collected_shape, LOW), (own_shape, WIDE), (own_shape, WIDE)],
        megabytes=32,
        cost=10,
    )(place, mixed_grad, held, *momentum)
    coeffs, steps = together(coeffs, steps)
    steps = [steps[0]] + [shifted(steps[shift], shift, plan.lon) for shift in range(1, plan.lon)]
    gains_shape = jax.ShapeDtypeStruct(norm_gains.shape, WIDE)
    values, gains_total, gain_moment, gain_updated = kernel_call(
        spread_kernel, "spread", (exchanged, gains_shape, gains_shape, gains_shape), megabytes=large
    )(place, weighted, coeffs, gain_second, gain_momentum, norm_gains)
    if parts > 1:
        totals, _ = together(totals, gain_second)
        total = kernel_call(
            functools.partial(sum_kernel, axis=1), "sum_lon", hidden_piece, [((plan.lon, *hidden_piece.shape), WIDE)]
        )(place, *totals)
        partner = lax.ppermute(total, "lat", [(source, source ^ 1) for source in range(parts)])
        both, _ = together(jnp.stack([total, partner]), gains_total)
        pieces = [both] + [shifted(both, shift, parts, "lat") for shift in range(2, parts, 2)]
    else:
        pieces, _ = together(pieces, gains_total)
    values = exchange(values, BOTH, devices)
    hidden_wide = jax.ShapeDtypeStruct(hidden_weight.shape, WIDE)
    hidden_grad, hidden_moment, hidden_updated, hidden_copy = kernel_call(
        real_muon_kernel,
        "real_muon",
        (hidden_wide, hidden_wide, hidden_wide, jax.ShapeDtypeStruct(hidden_weight.shape, LOW)),
        [((parts, *hidden_piece.shape), WIDE)],
        megabytes=60,
        cost=3,
    )(place, hidden_momentum, hidden_weight, *pieces)
    fine_gradient, coarse_gradient = kernel_call(
        functools.partial(last_kernel, plan=plan, scales=forward_scales),
        "last",
        tuple(grid_low),
        [rows_scratch],
        {6: of_lon(fine_back), 7: of_lon(coarse_back)},
        megabytes=60,
        cost=4,
    )(place, fine_grid, coarse_grid, fine_left, coarse_left, values, norm_gains, fine_back, coarse_back)
    steps, _ = together(steps, fine_gradient)
    spectral_grad, spectral_moment, spectral_updated, spectral_copy = finish(
        place, spectral_momentum, spectral_weight, steps
    )

    return (
        fine_out,
        jnp.swapaxes(coarse_out, 0, 1),
        fine_gradient,
        jnp.swapaxes(coarse_gradient, 0, 1),
        spectral_grad,
        spectral_moment,
        spectral_updated,
        spectral_copy,
        hidden_grad,
        hidden_moment,
        hidden_updated,
        hidden_copy,
        gains_total,
        gain_moment,
        gain_updated,
    )


def solution(mesh):
    grid = P("lat", "lon", None)
    degree = P("lat", None, "lon", None)
    return jax.shard_map(
        body,
        mesh=mesh,
        in_specs=(grid,) * 4 + (degree,) * 2 + (P(),) * 4,
        out_specs=(grid,) * 4 + (degree,) * 4 + (P(),) * 7,
        check_vma=False,
    )
```

```python
import functools
import math

import jax
import jax.numpy as jnp
import ml_dtypes
import numpy as np
from jax import lax
from jax.experimental import pallas as pl
from jax.experimental.pallas import tpu as pltpu
from jax.sharding import PartitionSpec as P

OWNED = 2
RIDER = 3
GROUP = 2
LANES = 128
NORM_EPSILON = 1e-05
MOMENTUM_DECAY = 0.5
STEP_RATE = 0.6
GAIN_RATE = 0.2
POLY_FIRST = 3.4445
POLY_SECOND = -4.775
POLY_THIRD = 2.0315
BOTH = ("lat", "lon")
LOW = jnp.bfloat16
WIDE = jnp.float32


class Plan:
    def __init__(self, lat_count, lon_count, fine, coarse, weight):
        self.lat, self.lon = lat_count, lon_count
        self.devices = lat_count * lon_count
        self.tf, self.nf, self.channels = fine.shape
        self.tc, self.nc = coarse.shape[:2]
        self.deg_dev = weight.shape[0]
        self.degrees = self.deg_dev * lat_count
        self.half = self.degrees // 2
        self.fine_lat, self.coarse_lat = self.tf * lat_count, self.tc * lat_count
        self.fine_lon, self.coarse_lon = self.nf * lon_count, self.nc * lon_count
        self.rows = 3 * self.tf + 2 * self.tc
        self.fine_ka = math.sqrt(self.fine_lat * self.fine_lon / (4.0 * math.pi))
        self.coarse_ka = math.sqrt(self.coarse_lat * self.coarse_lon / (4.0 * math.pi))
        self.parts_lat = lat_count // 2

    def orders(self, lat_index, lon_index):
        part = lat_index // self.parts_lat
        trio = (lat_index % self.parts_lat) * self.lon + lon_index
        even = 1 - trio % 2
        pair = trio // 2
        low, high = 3 * pair, self.half + 3 * pair
        first = high + 2 * (1 - even)
        second = even * (high + 1) + (1 - even) * (low + 1)
        third = even * low + (1 - even) * (low + 2)
        return (first, second, third), part, even

    def fourier(self):
        fine = np.zeros((self.lon, 3, self.devices, self.nf))
        coarse = np.zeros((self.lon, 2, self.devices, self.nc))

        def fill(out, order, part, total):
            position = np.arange(total)
            angle = 2.0 * np.pi / total * (position * order % total)
            line = -np.sin(angle) if part else np.cos(angle)
            out[...] = line.reshape(self.lon, -1)

        for lat_index in range(self.lat):
            for lon_index in range(self.lon):
                device = lat_index * self.lon + lon_index
                orders, part, even = self.orders(lat_index, lon_index)
                for row in range(3):
                    fill(fine[:, row, device], orders[row], part, self.fine_lon)
                for row in range(1 + even):
                    fill(coarse[:, row, device], orders[row] - self.half, part, self.coarse_lon)
        results = []
        for table in (fine, coarse):
            flat = table.reshape(self.lon, -1, table.shape[-1]).astype(ml_dtypes.bfloat16)
            results += [flat, np.swapaxes(flat, 1, 2)]
        return results


def legendre_kernel(columns, weighted_out, doubled_out, slope, back, start, *, degrees, half):
    order, cosine, quadrature, doubling = (columns[row : row + 1, :] for row in range(4))
    used, diagonal = columns[4:5, :], columns[5:6, :]
    degree = lax.broadcasted_iota(jnp.int32, slope.shape, 0).astype(WIDE)

    def factor(at):
        square = at * at
        return jnp.sqrt(
            jnp.maximum(4.0 * square - 1.0, 1.0) / jnp.maximum(square - order * order, 1.0)
        )

    now = factor(degree)
    running = (degree > order) & (degree < used)
    slope[...] = jnp.where(running, now * cosine, 0.0)
    back[...] = jnp.where(running, now / factor(degree - 1.0), 0.0)
    start[...] = jnp.where((degree == order) & (degree < used), diagonal, 0.0)

    def step(block, carried):
        latest, earlier = carried
        base = pl.multiple_of(block * 8, 8)
        slopes, backs, starts = (ref[pl.ds(base, 8), :] for ref in (slope, back, start))
        found = []
        for row in range(8):
            at = slice(row, row + 1)
            latest, earlier = slopes[at] * latest - backs[at] * earlier + starts[at], latest
            found.append(latest)
        start[pl.ds(base, 8), :] = jnp.concatenate(found, axis=0)
        return latest, earlier

    zero = jnp.zeros_like(order)
    lax.fori_loop(0, degrees // 8, step, (zero, zero))
    plain = start[...]
    weighted_out[...] = (quadrature * plain).astype(LOW)
    doubled_out[...] = (doubling * plain.astype(LOW).astype(WIDE)).astype(LOW)


def legendre_tables(plan, lat_index, lon_index):
    orders, part, even = plan.orders(lat_index, lon_index)
    fine_kind = np.repeat(np.arange(3), plan.tf)
    coarse_kind = np.repeat(np.arange(2), plan.tc)
    kind = np.tile(np.concatenate([fine_kind, coarse_kind]), plan.devices)
    is_fine = np.tile(np.arange(plan.rows) < 3 * plan.tf, plan.devices)
    lat_of = np.repeat(np.arange(plan.devices) // plan.lon, plan.rows)
    fine_lat = lat_of * plan.tf + np.tile(np.arange(plan.rows) % plan.tf, plan.devices)
    coarse_lat = lat_of * plan.tc + np.tile(np.arange(plan.rows) % plan.tc, plan.devices)
    position = np.where(is_fine, fine_lat, coarse_lat)
    count = np.where(is_fine, plan.fine_lat, plan.coarse_lat)
    colatitude = np.pi * (position + 0.5) / count
    own = jnp.where(kind == 0, orders[0], jnp.where(kind == 1, orders[1], orders[2]))
    own = jnp.where(is_fine, own, own - plan.half)
    held = own >= 0
    own = jnp.maximum(own, 0)
    span = np.arange(plan.degrees)
    norms = np.array(
        [
            0.5
            * (
                math.log((2.0 * m + 1.0) / (4.0 * math.pi))
                + math.lgamma(m + 0.5)
                - math.lgamma(m + 1.0)
                - 0.5 * math.log(math.pi)
            )
            for m in span
        ],
        np.float32,
    )
    norm = jnp.sum(jnp.where(own[None, :] == span[:, None], norms[:, None], 0.0), axis=0)
    log_sine = np.log(np.sin(colatitude)).astype(np.float32)
    diagonal = jnp.where(held, jnp.exp(norm + own.astype(WIDE) * log_sine), 0.0)
    columns = jnp.stack(
        [
            own.astype(WIDE),
            jnp.asarray(np.cos(colatitude).astype(np.float32)),
            jnp.asarray((np.pi / count * np.sin(colatitude)).astype(np.float32)),
            jnp.where(own == 0, 1.0, 2.0),
            jnp.asarray(np.where(is_fine, plan.degrees, plan.half).astype(np.float32)),
            diagonal,
        ]
    )
    shape = (plan.degrees, plan.devices * plan.rows)
    compact = pl.pallas_call(
        functools.partial(legendre_kernel, degrees=plan.degrees, half=plan.half),
        out_shape=(jax.ShapeDtypeStruct(shape, LOW),) * 2,
        scratch_shapes=[pltpu.VMEM(shape, WIDE)] * 3,
        compiler_params=pltpu.CompilerParams(vmem_limit_bytes=(16 if shape[1] <= 512 else 56) << 20),
        name="legendre",
    )(columns)
    chosen = kind[None, :] == np.arange(4)[:, None]
    pairs = plan.deg_dev // OWNED
    results = []
    for table in compact:
        spread = table.reshape(plan.lat, pairs, OWNED, 1, shape[1])
        spread = jnp.where(chosen, spread, jnp.zeros_like(spread))
        spread = jnp.pad(spread, ((0, 0), (0, plan.lon - pairs), (0, 0), (0, 0), (0, 0)))
        results.append(spread.reshape(plan.devices * 8, shape[1]))
    return results


def wide_dot(left, right, contract=((1,), (0,))):
    return lax.dot_general(left, right, (contract, ((), ())), preferred_element_type=WIDE)


def normalize(values):
    shifted = values - jnp.mean(values, axis=-1, keepdims=True)
    inverse = lax.rsqrt(jnp.mean(shifted * shifted, axis=-1, keepdims=True) + NORM_EPSILON)
    return shifted * inverse, inverse


def norm_back(grad, unit, inverse):
    return (
        grad
        - jnp.mean(grad, axis=-1, keepdims=True)
        - unit * jnp.mean(grad * unit, axis=-1, keepdims=True)
    ) * inverse


def kernel_call(kernel, name, out_shape, scratch=(), views=None, megabytes=16, cost=2):
    views = views or {}

    def run(place, *arrays):
        def spec(shape, at=None):
            if at in views:
                block, index = views[at]
                return pl.BlockSpec(block, lambda step, place: index(place))
            return pl.BlockSpec(tuple(shape), lambda step, place: (0,) * len(shape))

        outs = jax.tree.leaves(out_shape)
        found = pl.pallas_call(
            kernel,
            out_shape=outs,
            grid_spec=pltpu.PrefetchScalarGridSpec(
                num_scalar_prefetch=1,
                grid=(1,),
                in_specs=[spec(each.shape, at) for at, each in enumerate(arrays)],
                out_specs=[spec(each.shape) for each in outs],
                scratch_shapes=[pltpu.VMEM(*each) for each in scratch],
            ),
            compiler_params=pltpu.CompilerParams(vmem_limit_bytes=megabytes << 20),
            cost_estimate=estimate(cost),
            name=name,
        )(place, *arrays)
        return jax.tree.unflatten(jax.tree.structure(out_shape), found)

    return run


def estimate(microseconds):
    return pl.CostEstimate(
        flops=int(microseconds * 1.1e9), bytes_accessed=int(microseconds * 3e6), transcendentals=0
    )


def of_lon(table):
    return (None,) + table.shape[1:], lambda place: (place[1], 0, 0)


def cut(block, size):
    return pl.ds(pl.multiple_of(block * size, size), size)


class Blocks:
    def __init__(self, plan):
        self.plan = plan
        self.items = [(0, t) for t in range(plan.tf)] + [(1, t) for t in range(plan.tc)]

    def strides(self, grid, t):
        plan = self.plan
        starts = (
            [row * plan.tf + t for row in range(3)]
            if grid == 0
            else [3 * plan.tf + row * plan.tc + t for row in range(2)]
        )
        return [pl.ds(start, plan.devices, stride=plan.rows) for start in starts]

    def read(self, ref, grid, t):
        return ref[t] if grid == 0 else ref[:, t, :]

    def write(self, ref, grid, t, value):
        if grid == 0:
            ref[t] = value
        else:
            ref[:, t, :] = value

    def load(self, scratch, received):
        for lane in range(scratch.shape[0]):
            scratch[lane] = received[:, lane * LANES : (lane + 1) * LANES].astype(WIDE)

    def store(self, scratch, sent):
        for lane in range(scratch.shape[0]):
            sent[:, lane * LANES : (lane + 1) * LANES] = scratch[lane].astype(LOW)

    def put(self, scratch, grid, t, table, values, scale):
        summed = wide_dot(table, values) * scale
        for row, where in enumerate(self.strides(grid, t)):
            part = summed[row * self.plan.devices : (row + 1) * self.plan.devices]
            for lane in range(scratch.shape[0]):
                scratch[lane, where, :] = part[:, lane * LANES : (lane + 1) * LANES]

    def take(self, scratch, grid, t, table, scale):
        found = [
            jnp.concatenate([scratch[lane, where, :] for lane in range(scratch.shape[0])], axis=1)
            for where in self.strides(grid, t)
        ]
        values = jnp.concatenate(found, axis=0).astype(LOW)
        return (wide_dot(table, values) * scale).astype(LOW).astype(WIDE)


def front_kernel(place, fine, coarse, gains, table_fine, table_coarse, sent, scratch, *, plan, scales):
    blocks = Blocks(plan)
    grids, tables = (fine, coarse), (table_fine, table_coarse)
    for grid, t in blocks.items:
        unit, inverse = normalize(blocks.read(grids[grid], grid, t).astype(WIDE))
        normed = (unit * gains[0:1, :]).astype(LOW)
        blocks.put(scratch, grid, t, tables[grid][...], normed, scales[grid])
    blocks.store(scratch, sent)


def middle_kernel(
    place, fine, coarse, fine_up, coarse_up, received, gains, first, second,
    table_fine, table_coarse, back_fine, back_coarse,
    fine_out, coarse_out, fine_left, coarse_left, sent, gain, *rest, plan, scales,
):
    *pieces, scratch, hidden = rest
    blocks = Blocks(plan)
    grids, ups, outs, lefts = (
        (fine, coarse), (fine_up, coarse_up), (fine_out, coarse_out), (fine_left, coarse_left)
    )
    tables, backs = (table_fine, table_coarse), (back_fine, back_coarse)
    root = math.sqrt(2.0 / math.pi)
    scaling = gains[1:2, :]
    first_low, second_low = first[...], second[...]
    first_sum = second_sum = gain_sum = None
    blocks.load(scratch, received)
    branches = {
        (grid, t): blocks.take(scratch, grid, t, backs[grid][...], scales[grid]) for grid, t in blocks.items
    }
    groups = [(0, tuple(range(t, t + GROUP))) for t in range(0, plan.tf, GROUP)]
    groups += [(1, (t,)) for t in range(plan.tc)]
    for grid, group in groups:
        joined = lambda parts: parts[0] if len(parts) == 1 else jnp.concatenate(parts, axis=0)
        values = joined([blocks.read(grids[grid], grid, t) for t in group])
        upstream = joined([blocks.read(ups[grid], grid, t) for t in group])
        residual = values.astype(WIDE) + joined([branches[grid, t] for t in group])
        unit, inverse = normalize(residual)
        normed = (unit * scaling).astype(LOW)
        pre = wide_dot(normed, first_low)
        square = pre * pre
        inner = pre * (root + root * 0.044715 * square)
        gate = 0.5 + 0.5 * jnp.tanh(inner)
        active = (pre * gate).astype(LOW)
        output = (residual + wide_dot(active, second_low, ((1,), (1,)))).astype(LOW)
        slope = gate + gate * (1.0 - gate) * (pre * (2.0 * root + 6.0 * root * 0.044715 * square))
        pre_grad = (wide_dot(upstream, second_low) * slope).astype(LOW)
        normed_grad = wide_dot(pre_grad, first_low, ((1,), (1,)))
        left = upstream.astype(WIDE) + norm_back(normed_grad * scaling, unit, inverse)
        left_low = left.astype(LOW)
        size = left_low.shape[0] // len(group)
        for at, t in enumerate(group):
            rows = slice(at * size, (at + 1) * size)
            blocks.write(outs[grid], grid, t, output[rows])
            lefts[grid][t] = left_low[rows]
            blocks.put(scratch, grid, t, tables[grid][...], left_low[rows], scales[grid])
        first_part = wide_dot(normed, pre_grad, ((0,), (0,)))
        second_part = wide_dot(upstream, active, ((0,), (0,)))
        gain_part = jnp.sum(normed_grad * unit, axis=0, keepdims=True)
        if first_sum is None:
            first_sum, second_sum, gain_sum = first_part, second_part, gain_part
        else:
            first_sum, second_sum, gain_sum = (
                first_sum + first_part, second_sum + second_part, gain_sum + gain_part
            )
    blocks.store(scratch, sent)
    gain[...] = gain_sum
    hidden[: plan.channels] = first_sum
    hidden[plan.channels :] = second_sum
    size = pieces[0].shape[0]
    for shift, piece in enumerate(pieces):
        block = (place[0] + shift) % len(pieces)
        piece[...] = hidden[cut(block, size), :].astype(piece.dtype)


def last_kernel(
    place, fine, coarse, fine_left, coarse_left, received, gains, back_fine, back_coarse,
    fine_out, coarse_out, scratch, *, plan, scales,
):
    blocks = Blocks(plan)
    grids, lefts, outs = (fine, coarse), (fine_left, coarse_left), (fine_out, coarse_out)
    backs = (back_fine, back_coarse)
    blocks.load(scratch, received)
    for grid, t in blocks.items:
        normed_grad = blocks.take(scratch, grid, t, backs[grid][...], scales[grid])
        unit, inverse = normalize(blocks.read(grids[grid], grid, t).astype(WIDE))
        gradient = lefts[grid][t].astype(WIDE) + norm_back(normed_grad * gains[0:1, :], unit, inverse)
        blocks.write(outs[grid], grid, t, gradient.astype(LOW))


def row_masks(count):
    slot = lax.broadcasted_iota(jnp.int32, (count, 1), 0) % 8
    return [(slot // 4 == owned) & (slot % 4 < RIDER) for owned in range(OWNED)], slot == RIDER


def mixing(rows, weights, masks, sign, contract):
    split = rows.shape[0] // 2
    products = []
    for owned in range(OWNED):
        chosen = jnp.where(masks[owned], rows, 0.0).astype(LOW)
        products.append([wide_dot(chosen, weights[owned, part], contract) for part in range(2)])
    by_real = sum(product[0] for product in products[1:]) + products[0][0]
    by_imag = (sum(product[1] for product in products[1:]) + products[0][1]) * sign
    top = by_real[:split] - by_imag[split:]
    bottom = by_real[split:] + by_imag[:split]
    return top, bottom


class Joined:
    def __init__(self, ref):
        self.ref = ref

    def __getitem__(self, at):
        value = self.ref[at[0], at[1]]
        return value.reshape(-1, value.shape[-1])


def collect(own, pieces, target):
    for shift, piece in enumerate(pieces):
        source = (own + len(pieces) - shift) % len(pieces)
        for owned in range(OWNED):
            for part in range(2):
                target[owned, part, source] = piece[owned, part]


def mix_kernel(place, held, *refs):
    *pieces, out, weights = refs
    collect(place[1], pieces, weights)
    split = held.shape[0] // 2
    masks, rider = row_masks(held.shape[0])
    top, bottom = mixing(held[...].astype(WIDE), Joined(weights), masks, 1.0, ((1,), (1,)))
    out[:split] = top.astype(LOW)
    out[split:] = bottom.astype(LOW)


def sum_kernel(place, *refs, axis):
    *pieces, out, ordered = refs
    for shift, piece in enumerate(pieces):
        ordered[(place[axis] + len(pieces) - shift) % len(pieces)] = piece[...].astype(WIDE)
    total = ordered[0]
    for at in range(1, len(pieces)):
        total = total + ordered[at]
    out[...] = total.astype(out.dtype)


def join_kernel(place, table, spectrum, gain, out):
    masks, rider = row_masks(table.shape[0])
    out[...] = jnp.where(rider, gain[...], wide_dot(table[...], spectrum[...])).astype(LOW)


def mix_back_kernel(place, received, held, weights, gains, out, gain):
    masks, rider = row_masks(held.shape[0])
    rows = received[...].astype(WIDE)
    gain[...] = jnp.sum(jnp.where(rider, rows, 0.0), axis=0, keepdims=True)
    top, bottom = mixing(rows, Joined(weights), masks, -1.0, ((1,), (0,)))
    back = jnp.concatenate([top, bottom], axis=0)
    gain_row = jnp.sum(back * held[...].astype(WIDE), axis=0, keepdims=True) / gains[0:1, :]
    out[...] = jnp.where(rider, gain_row, back).astype(LOW)


def spread_kernel(place, table, received, second, momentum, gains, out, total_out, moment_out, updated_out):
    masks, rider = row_masks(table.shape[0])
    out[...] = wide_dot(table[...], received[...], ((0,), (0,))).astype(LOW)
    first = jnp.sum(jnp.where(rider, received[...].astype(WIDE), 0.0), axis=0, keepdims=True)
    for row, total in enumerate((first, second[...])):
        at = slice(row, row + 1)
        total_out[at, :] = total
        moment = MOMENTUM_DECAY * momentum[at, :] + total
        moment_out[at, :] = moment
        scale = jnp.sqrt(jnp.mean(moment * moment, axis=-1, keepdims=True)) + 1e-06
        updated_out[at, :] = gains[at, :] - GAIN_RATE * moment / scale


def scatter(own, source, pieces, kind):
    size = pieces[0].shape[3]
    for shift, piece in enumerate(pieces):
        block = (own + shift) % len(pieces)
        for owned in range(OWNED):
            for part in range(2):
                piece[kind, owned, part] = source[owned, part, cut(block, size), :].astype(LOW)


def shift_gram(gram):
    size = gram.shape[0]
    unit = lax.broadcasted_iota(jnp.int32, gram.shape, 0) == lax.broadcasted_iota(jnp.int32, gram.shape, 1)
    level = jnp.sum(jnp.sum(jnp.where(unit, gram, 0.0), axis=1, keepdims=True), axis=0, keepdims=True) / size
    keep = POLY_FIRST + level * (POLY_SECOND + POLY_THIRD * level)
    return jnp.where(unit, gram - level, gram), keep, POLY_SECOND + 2.0 * POLY_THIRD * level


def beside(left, right):
    return jnp.concatenate([left, right], axis=1)


def below(top, bottom):
    return jnp.concatenate([top, bottom], axis=0)


def complex_rows(real, imag):
    return below(beside(real, -imag), beside(imag, real))


def complex_muon_kernel(place, mixed_grads, held, *refs):
    count = (len(refs) - 3) // 2
    sources, pieces, (momentum, grads, result) = refs[:count], refs[count : 2 * count], refs[2 * count :]
    collect(place[1], sources, momentum)
    masks, rider = row_masks(held.shape[0])
    split = held.shape[0] // 2
    coeffs, rows = held[...].astype(WIDE), mixed_grads[...].astype(WIDE)
    swapped = jnp.concatenate([rows[split:], -rows[:split]], axis=0).astype(LOW)
    for owned in range(OWNED):
        picked = jnp.where(masks[owned], coeffs, 0.0).astype(LOW)
        for part, side in enumerate((mixed_grads[...], swapped)):
            grads[owned, part] = wide_dot(side, picked, ((0,), (0,)))
    momentum = Joined(momentum)
    states = []
    for owned in range(OWNED):
        parts = [
            MOMENTUM_DECAY * momentum[owned, part].astype(WIDE) + grads[owned, part] for part in range(2)
        ]
        total = jnp.sum(parts[0] * parts[0]) + jnp.sum(parts[1] * parts[1])
        scale = 1.0 / (jnp.sqrt(total) + 1e-07)
        states.append([part * scale for part in parts])
    for iteration in range(5):
        size = states[0][0].shape[0]
        lows = [[part.astype(LOW) for part in state] for state in states]
        sides = [beside(real, imag) for real, imag in lows]
        grams = [
            wide_dot(below(side, beside(imag, -real)), side, ((1,), (1,)))
            for side, (real, imag) in zip(sides, lows)
        ]
        shifts = [shift_gram(gram[:size]) for gram in grams]
        grams = [below(rest, gram[size:]) for gram, (rest, keep, lead) in zip(grams, shifts)]
        low_grams = [gram.astype(LOW) for gram in grams]
        squares = [wide_dot(complex_rows(low[:size], low[size:]), low) for low in low_grams]
        polys = [
            (lead * gram + POLY_THIRD * square).astype(LOW)
            for gram, square, (rest, keep, lead) in zip(grams, squares, shifts)
        ]
        changes = [
            wide_dot(complex_rows(poly[:size], poly[size:]), below(*low)) for poly, low in zip(polys, lows)
        ]
        states = [
            [keep * state[0] + change[:size], keep * state[1] + change[size:]]
            for state, change, (rest, keep, lead) in zip(states, changes, shifts)
        ]
    for owned in range(OWNED):
        for part in range(2):
            result[owned, part] = states[owned][part]
    scatter(place[1], grads, pieces, 0)
    scatter(place[1], result, pieces, 1)


def real_muon_kernel(place, momentum, weight, *refs):
    *pieces, grad_out, moment_out, updated_out, low_out, gathered = refs
    if len(pieces) == 1:
        gathered[0] = pieces[0][...]
    else:
        side = place[0] % 2
        for shift, piece in enumerate(pieces):
            pair = (place[0] // 2 + len(pieces) - shift) % len(pieces)
            gathered[2 * pair + side] = piece[0].astype(WIDE)
            gathered[2 * pair + 1 - side] = piece[1].astype(WIDE)
    whole = gathered[...].reshape(momentum.shape)
    currents = []
    for part in range(2):
        grad = whole[part]
        grad_out[part] = grad
        moment = MOMENTUM_DECAY * momentum[part] + grad
        moment_out[part] = moment
        currents.append(moment * (1.0 / (jnp.sqrt(jnp.sum(moment * moment)) + 1e-07)))
    for iteration in range(5):
        lows = [current.astype(LOW) for current in currents]
        shifts = [shift_gram(wide_dot(low, low, ((1,), (1,)))) for low in lows]
        rests = [rest.astype(LOW) for rest, keep, lead in shifts]
        squares = [wide_dot(rest, rest) for rest in rests]
        polys = [
            (lead * rest + POLY_THIRD * square).astype(LOW)
            for square, (rest, keep, lead) in zip(squares, shifts)
        ]
        changes = [wide_dot(poly, low) for poly, low in zip(polys, lows)]
        currents = [
            keep * current + change
            for current, change, (rest, keep, lead) in zip(currents, changes, shifts)
        ]
    for part in range(2):
        updated = weight[part] - STEP_RATE * currents[part]
        updated_out[part] = updated
        low_out[part] = updated.astype(LOW)


def finish_kernel(place, momentum, weight, *refs, count):
    pieces, (grad_out, moment_out, updated_out, low_out) = refs[:count], refs[count:]
    shift = (place[1] + count - pl.program_id(0)) % count
    for at in range(count):

        @pl.when(shift == at)
        def _():
            grad = pieces[at][0].astype(WIDE)
            grad_out[...] = grad
            moment_out[...] = MOMENTUM_DECAY * momentum[...] + grad
            updated = weight[...] - STEP_RATE * pieces[at][1].astype(WIDE)
            updated_out[...] = updated
            low_out[...] = updated.astype(LOW)


def finish(place, momentum, weight, pieces):
    shape, count = weight.shape, len(pieces)
    block = pl.BlockSpec((OWNED,) + shape[1:], lambda owner, at: (owner, 0, 0, 0))
    whole = pl.BlockSpec(pieces[0].shape, lambda owner, at: (0, 0, 0, 0, 0))
    return pl.pallas_call(
        functools.partial(finish_kernel, count=count),
        out_shape=[jax.ShapeDtypeStruct(shape, dtype) for dtype in (WIDE, WIDE, WIDE, LOW)],
        grid_spec=pltpu.PrefetchScalarGridSpec(
            num_scalar_prefetch=1,
            grid=(shape[0] // OWNED,),
            in_specs=[block] * 2 + [whole] * count,
            out_specs=[block] * 4,
        ),
        compiler_params=pltpu.CompilerParams(vmem_limit_bytes=16 << 20),
        cost_estimate=estimate(6),
        name="finish",
    )(place, momentum, weight, *pieces)


def exchange(rows, axes, count):
    block = rows.reshape((count, -1) + rows.shape[1:])
    return lax.all_to_all(block, axes, 0, 0, tiled=True).reshape(rows.shape)


def shifted(piece, shift, count, axis="lon"):
    return lax.ppermute(piece, axis, [(source, (source + shift) % count) for source in range(count)])


def for_owners(plan, rows, lon_index, owners):
    pieces = []
    for shift in range(plan.lon):
        owner = jnp.minimum((lon_index + shift) % plan.lon, owners - 1)
        pieces.append(lax.dynamic_slice_in_dim(rows, owner * OWNED, OWNED, 0).astype(LOW))
    return pieces


def together(*values):
    return lax.optimization_barrier(values)


def body(
    fine_grid,
    coarse_grid,
    fine_cotangent,
    coarse_cotangent,
    spectral_weight,
    spectral_momentum,
    hidden_weight,
    hidden_momentum,
    norm_gains,
    gain_momentum,
):
    plan = Plan(lax.axis_size("lat"), lax.axis_size("lon"), fine_grid, coarse_grid, spectral_weight)
    lat_index, lon_index = lax.axis_index("lat"), lax.axis_index("lon")
    place = jnp.stack([lat_index, lon_index]).astype(jnp.int32)
    channels, devices = plan.channels, plan.devices
    owners = plan.deg_dev // OWNED
    block_rows = channels // plan.lon
    fine_table, fine_back, coarse_table, coarse_back = map(jnp.asarray, plan.fourier())
    exchanged = jax.ShapeDtypeStruct((devices * plan.rows, channels), LOW)
    rows_scratch = ((channels // LANES, devices * plan.rows, LANES), WIDE)
    owned_rows = jax.ShapeDtypeStruct((devices * 8, channels), LOW)
    gain_shape = jax.ShapeDtypeStruct((1, channels), WIDE)
    left_low = [jax.ShapeDtypeStruct(grid.shape, LOW) for grid in (fine_grid, coarse_grid)]
    coarse_grid, coarse_cotangent = (jnp.swapaxes(grid, 0, 1) for grid in (coarse_grid, coarse_cotangent))
    grid_low = [jax.ShapeDtypeStruct(grid.shape, LOW) for grid in (fine_grid, coarse_grid)]
    piece_shape = jax.ShapeDtypeStruct((2, OWNED, 2, block_rows, channels), LOW)
    own_shape = (OWNED, 2, channels, channels)
    collected_shape = (OWNED, 2, plan.lon, block_rows, channels)
    forward_scales = (
        2.0 * math.pi / plan.fine_lon * plan.fine_ka,
        2.0 * math.pi / plan.coarse_lon * plan.coarse_ka,
    )
    inverse_scales = (1.0 / plan.fine_ka, 1.0 / plan.coarse_ka)
    large = 16 if devices <= 32 else 56

    sent = kernel_call(
        functools.partial(front_kernel, plan=plan, scales=forward_scales),
        "front",
        exchanged,
        [rows_scratch],
        {3: of_lon(fine_table), 4: of_lon(coarse_table)},
        megabytes=24,
        cost=3,
    )(place, fine_grid, coarse_grid, norm_gains, fine_table, coarse_table)
    weights = for_owners(plan, spectral_weight, lon_index, owners)
    momentum = for_owners(plan, spectral_momentum, lon_index, owners)
    first_shifts, middle_shift = [1, *range(3, plan.lon)], 2
    sent, weights = together(sent, weights)
    spectrum = exchange(sent, BOTH, devices)
    for shift in first_shifts:
        weights[shift] = shifted(weights[shift], shift, plan.lon)
    weighted, doubled = legendre_tables(plan, lat_index, lon_index)
    hidden_low = hidden_weight.astype(LOW)

    coeffs, weights, momentum = together(wide_dot(weighted, spectrum).astype(LOW), weights, momentum)
    held = exchange(coeffs, BOTH, devices)
    weights[middle_shift] = shifted(weights[middle_shift], middle_shift, plan.lon)
    mixed, weights = kernel_call(
        mix_kernel, "mix", (owned_rows, jax.ShapeDtypeStruct(collected_shape, LOW))
    )(place, held, *weights)
    mixed = exchange(mixed, BOTH, devices)
    values = wide_dot(doubled, mixed, ((0,), (0,))).astype(LOW)
    values = exchange(values, BOTH, devices)
    values, momentum = together(values, momentum)
    for shift in range(1, plan.lon):
        momentum[shift] = shifted(momentum[shift], shift, plan.lon)

    parts = plan.lat if plan.lat <= 8 else 1
    hidden_piece = jax.ShapeDtypeStruct(
        (2 * channels // parts, hidden_weight.shape[2]), LOW if parts > 1 else WIDE
    )
    fine_out, coarse_out, fine_left, coarse_left, sent, gain_second, *pieces = kernel_call(
        functools.partial(middle_kernel, plan=plan, scales=inverse_scales),
        "middle",
        (*grid_low, *left_low, exchanged, gain_shape, *[hidden_piece] * parts),
        [rows_scratch, ((2 * channels, hidden_weight.shape[2]), WIDE)],
        {
            8: of_lon(fine_table),
            9: of_lon(coarse_table),
            10: of_lon(fine_back),
            11: of_lon(coarse_back),
        },
        megabytes=60,
        cost=10,
    )(
        place, fine_grid, coarse_grid, fine_cotangent, coarse_cotangent, values, norm_gains,
        hidden_low[0], hidden_low[1], fine_table, coarse_table, fine_back, coarse_back,
    )
    sent, momentum = together(sent, momentum)
    spectrum = exchange(sent, BOTH, devices)
    if parts > 1:
        for shift in range(1, parts):
            pieces[shift] = shifted(pieces[shift], shift, parts, "lat")
    riding = jnp.arange(devices * 8)[:, None] % 8 == RIDER
    coeffs = jnp.where(riding, gain_second, wide_dot(doubled, spectrum)).astype(LOW)
    mixed_grad = exchange(coeffs, BOTH, devices)
    if parts > 1:
        total = kernel_call(
            functools.partial(sum_kernel, axis=0), "sum_lat", hidden_piece, [((parts, *hidden_piece.shape), WIDE)]
        )(place, *pieces)
        totals = [total] + [shifted(total, shift, plan.lon) for shift in range(1, plan.lon)]
    else:
        pieces = [lax.psum(pieces[0], BOTH)]

    coeffs, gain_second = kernel_call(
        mix_back_kernel, "mix_back", (owned_rows, gain_shape), megabytes=large, cost=2
    )(place, mixed_grad, held, weights, norm_gains)
    coeffs = exchange(coeffs, BOTH, devices)
    steps = kernel_call(
        complex_muon_kernel,
        "complex_muon",
        (piece_shape,) * plan.lon,
        [(collected_shape, LOW), (own_shape, WIDE), (own_shape, WIDE)],
        megabytes=32,
        cost=10,
    )(place, mixed_grad, held, *momentum)
    coeffs, steps = together(coeffs, steps)
    steps = [steps[0]] + [shifted(steps[shift], shift, plan.lon) for shift in range(1, plan.lon)]
    gains_shape = jax.ShapeDtypeStruct(norm_gains.shape, WIDE)
    values, gains_total, gain_moment, gain_updated = kernel_call(
        spread_kernel, "spread", (exchanged, gains_shape, gains_shape, gains_shape), megabytes=large
    )(place, weighted, coeffs, gain_second, gain_momentum, norm_gains)
    if parts > 1:
        total = kernel_call(
            functools.partial(sum_kernel, axis=1), "sum_lon", hidden_piece, [((plan.lon, *hidden_piece.shape), WIDE)]
        )(place, *totals)
        partner = lax.ppermute(total, "lat", [(source, source ^ 1) for source in range(parts)])
        both, _ = together(jnp.stack([total, partner]), gains_total)
        pieces = [both] + [shifted(both, shift, parts, "lat") for shift in range(2, parts, 2)]
    else:
        pieces, _ = together(pieces, gains_total)
    values = exchange(values, BOTH, devices)
    hidden_wide = jax.ShapeDtypeStruct(hidden_weight.shape, WIDE)
    hidden_grad, hidden_moment, hidden_updated, hidden_copy = kernel_call(
        real_muon_kernel,
        "real_muon",
        (hidden_wide, hidden_wide, hidden_wide, jax.ShapeDtypeStruct(hidden_weight.shape, LOW)),
        [((parts, *hidden_piece.shape), WIDE)],
        megabytes=60,
        cost=2,
    )(place, hidden_momentum, hidden_weight, *pieces)
    fine_gradient, coarse_gradient = kernel_call(
        functools.partial(last_kernel, plan=plan, scales=forward_scales),
        "last",
        tuple(grid_low),
        [rows_scratch],
        {6: of_lon(fine_back), 7: of_lon(coarse_back)},
        megabytes=60,
        cost=4,
    )(place, fine_grid, coarse_grid, fine_left, coarse_left, values, norm_gains, fine_back, coarse_back)
    steps, _ = together(steps, fine_gradient)
    spectral_grad, spectral_moment, spectral_updated, spectral_copy = finish(
        place, spectral_momentum, spectral_weight, steps
    )

    return (
        fine_out,
        jnp.swapaxes(coarse_out, 0, 1),
        fine_gradient,
        jnp.swapaxes(coarse_gradient, 0, 1),
        spectral_grad,
        spectral_moment,
        spectral_updated,
        spectral_copy,
        hidden_grad,
        hidden_moment,
        hidden_updated,
        hidden_copy,
        gains_total,
        gain_moment,
        gain_updated,
    )


def solution(mesh):
    grid = P("lat", "lon", None)
    degree = P("lat", None, "lon", None)
    return jax.shard_map(
        body,
        mesh=mesh,
        in_specs=(grid,) * 4 + (degree,) * 2 + (P(),) * 4,
        out_specs=(grid,) * 4 + (degree,) * 4 + (P(),) * 7,
        check_vma=False,
    )
```
